32 devices in a mesh: rows: 4 (over z), tp: 8 (over y, x, core).
Axes of the slice: x: 2, y: 2, z: 4, core: 2. Of those that a mesh axis runs over, the one named last changes fastest.
Arguments:
- tokens: bfloat16 [8, 2048, 2048], P('rows', 'tp'), may hold values from -120 to 120, as said below
- segment_ids: int32 [8, 2048], P('rows'), may hold values from 0 to 3, as said below
- positions: int32 [8, 2048], P('rows'), may hold values from 0 to 1023, as said below
- norm_gain: bfloat16 [2048], replicated, may hold values from 0.5 to 1.5
- norm_shift: bfloat16 [2048], replicated, may hold values from -1.5 to 1.5
- query_key_value_weight: bfloat16 [2048, 3, 2048], P(None, None, 'tp'), may hold values from -1 to 1, as said below
- b_qkv: bfloat16 [3, 2048], P(None, 'tp'), may hold values from -1.5 to 1.5
- dense_weight: bfloat16 [2048, 2048], P('tp'), may hold values from -1 to 1
- b_dense: bfloat16 [2048], replicated, may hold values from -1.5 to 1.5
- inward_weight: bfloat16 [2048, 8192], P(None, 'tp'), may hold values from -1 to 1, as said below
- b_in: bfloat16 [8192], P('tp'), may hold values from -1.5 to 1.5
- outward_weight: bfloat16 [8192, 2048], P('tp'), may hold values from -0.0625 to 0.0625
- b_out: bfloat16 [2048], replicated, may hold values from -1.5 to 1.5
- cotangent: bfloat16 [8, 2048, 2048], P('rows', 'tp'), may hold values from -6 to 6
Outputs:
- layer_out: bfloat16 [8, 2048, 2048], P('rows', 'tp')
- input_grad: bfloat16 [8, 2048, 2048], P('rows', 'tp')
- gain_grad: float32 [2048], P('tp')
- shift_grad: float32 [2048], P('tp')
- qkv_weight_grad: float32 [2048, 3, 2048], P(None, None, 'tp')
- qkv_bias_grad: float32 [3, 2048], P(None, 'tp')
- dense_weight_grad: float32 [2048, 2048], P('tp')
- dense_bias_grad: float32 [2048], P('tp')
- in_weight_grad: float32 [2048, 8192], P(None, 'tp')
- in_bias_grad: float32 [8192], P('tp')
- out_weight_grad: float32 [8192, 2048], P('tp')
- out_bias_grad: float32 [2048], P('tp')
- rms_values: float32 [4], replicated
The draws below stay inside these ranges and needn't reach their ends.
Inputs may be any that keep to these rules, and one draw needn't show every extreme that they name: `segment_ids`: within each row the ids start at 0 and rise by one at each of 3 document starts; the first document of every row holds exactly 1024 tokens, the others fewer. `positions`: A token's position is the number of earlier tokens of its row with its segment id. `tokens`: Real-valued activations. `query_key_value_weight`: Real-valued weights. `inward_weight`: Real-valued weights.
All inputs are finite; a program needn't handle non-finite values.
Results may differ from the reference program's by a relative error of at most 0.0086.
Values may be sent and summed in bfloat16 or wider, within the bound.
No kernel may reach another device: no remote copies, remote signals or barrier semaphores. Data moves between devices by JAX's collectives and lax.ppermute only.
A program may use at most 384 MiB of HBM per device.

```python
from functools import partial
import jax
import jax.numpy as jnp
from jax import lax

D = 2048
H = 32
HD = 64
ROT = 32
FF = 8192
LEN = 2048
DOCS = 4
BATCH = 8


def draw_tokens(key, part):
    key_base, key_rough, key_cols = jax.random.split(key, 3)
    base = jnp.clip(jax.random.normal(key_base, (BATCH, LEN, D), jnp.float32), -4.0, 4.0)
    rough = 10.0 ** (jax.random.uniform(key_rough, (BATCH, LEN, 1), jnp.float32) - 0.5)
    column_scale = 10.0 ** (jax.random.uniform(key_cols, (1, 1, D), jnp.float32) - 0.5)
    row_ramp = 1.0 + 2.0 * jnp.arange(BATCH, dtype=jnp.float32) / max(BATCH - 1, 1)
    place_ramp = 1.0 + 2.0 * jnp.arange(LEN, dtype=jnp.float32) / max(LEN - 1, 1)
    ramp = jnp.sqrt(row_ramp[:, None, None] * place_ramp[None, :, None])
    return (base * rough * column_scale * ramp).astype(jnp.bfloat16)


def column_offset_weight(key, full_shape, column_shape, column_mask):
    key_main, key_column = jax.random.split(jax.random.fold_in(key, 11))
    main = jnp.clip(jax.random.normal(key_main, full_shape, jnp.float32), -4.0, 4.0)
    column = jnp.clip(jax.random.normal(key_column, column_shape, jnp.float32), -4.0, 4.0) * column_mask
    return ((main + column) * D ** (-0.5)).astype(jnp.bfloat16)


def draw_query_key_value_weight(key, part):
    column_mask = jnp.array([0.0, 0.0, 1.0], jnp.float32).reshape(1, 3, 1)
    return column_offset_weight(key, (D, 3, D), (1, 3, D), column_mask)


def draw_inward_weight(key, part):
    return column_offset_weight(key, (D, FF), (1, FF), 1.0)


def document_layout(key):
    half_len = LEN // 2
    row_keys = jax.random.split(jax.random.fold_in(key, 7), BATCH)
    orders = jax.vmap(lambda row_key: jax.random.permutation(row_key, half_len - 1))(row_keys)
    later = orders[:, :DOCS - 2].astype(jnp.int32) + half_len + 1
    first_start = jnp.full((BATCH, 1), half_len, jnp.int32)
    starts = jnp.concatenate([first_start, later], axis=1).astype(jnp.int32)
    places = jnp.arange(LEN, dtype=jnp.int32)
    passed = starts[:, None, :] <= places[None, :, None]
    segments = jnp.sum(passed.astype(jnp.int32), axis=-1).astype(jnp.int32)
    last_start = jnp.max(jnp.where(passed, starts[:, None, :], 0), axis=-1)
    return (segments, (places[None, :] - last_start).astype(jnp.int32))


def draw_segment_ids(key, part):
    return document_layout(key)[0]


def draw_positions(key, part):
    return document_layout(key)[1]


def shard_levels(rng, dims, cuts, low, largest):
    def one(position, shards_of):
        draws = jax.random.uniform(jax.random.fold_in(jax.random.fold_in(rng, 6), position), (shards_of,), jnp.float32, low / len(cuts), largest / len(cuts))
        return jnp.repeat(jnp.exp(draws), dims[position] // shards_of).reshape((-1,) + (1,) * (len(dims) - position - 1))

    gain = one(*cuts[0])
    for cut in cuts[1:]:
        gain = gain * one(*cut)
    return gain


def centred(stream_key, extent, scale, limit, pieces=(), kind=jnp.bfloat16):
    gain = shard_levels(stream_key, extent, pieces, -0.22, 0.18) if pieces else 1.0
    values = jax.random.normal(stream_key, extent, jnp.float32) * scale * gain
    return jnp.minimum(jnp.maximum(values, -limit), limit).astype(kind)


def setup_inputs(seed: int = 0) -> dict:
    key_of = jax.random.split(jax.random.key(seed), 15)
    tokens = draw_tokens(jax.random.fold_in(key_of[14], 71), 0)
    segment_ids = draw_segment_ids(jax.random.fold_in(key_of[14], 71), 0)
    positions = draw_positions(jax.random.fold_in(key_of[14], 71), 0)
    norm_gain = jnp.clip(1.0 + 0.1 * jax.random.normal(key_of[3], (D,), jnp.float32), 0.5, 1.5).astype(jnp.bfloat16)
    norm_shift = centred(key_of[4], (D,), 0.3, 1.5)
    query_key_value_weight = draw_query_key_value_weight(jax.random.fold_in(key_of[14], 71), 0)
    b_qkv = centred(key_of[6], (3, D), 0.3, 1.5, ((1, 8),))
    dense_weight = centred(key_of[7], (D, D), (D // 64) ** -0.5, 1.0, ((0, 8),))
    b_dense = centred(key_of[8], (D,), 0.3, 1.5)
    inward_weight = draw_inward_weight(jax.random.fold_in(key_of[14], 71), 0)
    b_in = centred(key_of[10], (FF,), 0.3, 1.5, ((0, 8),))
    outward_weight = centred(key_of[11], (FF, D), FF ** -0.5, 0.0625, ((0, 8),))
    b_out = centred(key_of[12], (D,), 0.3, 1.5)
    cotangent = centred(key_of[13], (BATCH, LEN, D), 1.0, 6.0, ((0, 4), (1, 8)))
    return dict(tokens=tokens, segment_ids=segment_ids, positions=positions, norm_gain=norm_gain, norm_shift=norm_shift, query_key_value_weight=query_key_value_weight, b_qkv=b_qkv, dense_weight=dense_weight, b_dense=b_dense, inward_weight=inward_weight, b_in=b_in, outward_weight=outward_weight, b_out=b_out, cotangent=cotangent)


epsilon = 1e-05
big_negative = -1e+30
rope_base = 10000.0
highest = lax.Precision.HIGHEST

@jax.custom_vjp
def low(v):
    return lax.optimization_barrier(v.astype(jnp.bfloat16)).astype(jnp.float32)

@jax.custom_vjp
def low_back(v):
    return v

def low_keep(v):
    return (low(v), None)

def low_pass(kept, grad):
    return (grad,)

def back_keep(v):
    return (v, None)

def back_low(kept, grad):
    return (low(grad),)
low.defvjp(low_keep, low_pass)
low_back.defvjp(back_keep, back_low)

def normalize(values, norm_gain, norm_shift):
    center = values - lax.optimization_barrier(jnp.mean(values, axis=-1, keepdims=True))
    spread = lax.optimization_barrier(jnp.mean(center * center, axis=-1, keepdims=True))
    return center * lax.rsqrt(spread + epsilon) * norm_gain + norm_shift

def rope_tables(positions, rot_dims):
    half_rot = rot_dims // 2
    frequency = rope_base ** (-2.0 * jnp.arange(half_rot, dtype=jnp.float32) / rot_dims)
    angles = positions.astype(jnp.float32)[..., None] * frequency
    return (jnp.cos(angles)[..., None, :], jnp.sin(angles)[..., None, :])

def rotate(field_in, cosine_table, sine_table):
    half_rot = cosine_table.shape[-1]
    first_part = field_in[..., :half_rot]
    second = field_in[..., half_rot:2 * half_rot]
    return jnp.concatenate([first_part * cosine_table - second * sine_table, second * cosine_table + first_part * sine_table, field_in[..., 2 * half_rot:]], axis=-1)

def attend_head(allowed, head_items):
    queries, keys_in, values_in = head_items
    scale = HD ** (-0.5)
    raw_scores = low_back(jnp.dot(queries, keys_in.T, precision=highest) * scale)
    scores = jnp.where(allowed, raw_scores, big_negative)
    soft_weights = jax.nn.softmax(scores, axis=-1)
    return jnp.dot(low(soft_weights), values_in, precision=highest)

def row_forward(segments, places, values, norm_gain, norm_shift, query_key_value_weight, b_qkv, dense_weight, b_dense, inward_weight, b_in, outward_weight, b_out):
    length = values.shape[0]
    normed = low(normalize(values, norm_gain, norm_shift))
    qkv = low_back(jnp.einsum('ld,dcf->lcf', normed, query_key_value_weight, precision=highest) + b_qkv)
    cosine_table, sine_table = rope_tables(places, ROT)
    queries = low(rotate(qkv[:, 0].reshape(length, H, HD), cosine_table, sine_table))
    keys_in = low(rotate(qkv[:, 1].reshape(length, H, HD), cosine_table, sine_table))
    values_in = low(qkv[:, 2].reshape(length, H, HD))
    order = jnp.arange(length)
    allowed = (segments[:, None] == segments[None, :]) & (order[:, None] >= order[None, :])
    heads_out = lax.map(jax.checkpoint(partial(attend_head, allowed)), (queries.transpose(1, 0, 2), keys_in.transpose(1, 0, 2), values_in.transpose(1, 0, 2)))
    attended = low(low_back(heads_out.transpose(1, 0, 2).reshape(length, H * HD)))
    attention = jnp.dot(attended, dense_weight, precision=highest) + b_dense
    hidden = low_back(jnp.dot(normed, inward_weight, precision=highest) + b_in)
    activated = low(jax.nn.gelu(hidden, approximate=True))
    mlp = jnp.dot(activated, outward_weight, precision=highest) + b_out
    return (values + attention + mlp, (attention, mlp))

def reference(tokens, segment_ids, positions, norm_gain, norm_shift, query_key_value_weight, b_qkv, dense_weight, b_dense, inward_weight, b_in, outward_weight, b_out, cotangent):
    params = tuple((item.astype(jnp.float32) for item in (norm_gain, norm_shift, query_key_value_weight, b_qkv, dense_weight, b_dense, inward_weight, b_in, outward_weight, b_out)))
    zero_sums = tuple((jnp.zeros_like(item) for item in params))

    def per_row(carried, row_items):
        grad_sums, squares = carried
        row_tokens, segments, places, row_cot = row_items
        values = row_tokens.astype(jnp.float32)
        out_row, pull, extras = jax.vjp(partial(row_forward, segments, places), values, *params, has_aux=True)
        attention, mlp = extras
        grads = pull(row_cot.astype(jnp.float32))
        grad_sums = tuple((left_sum + right_term for left_sum, right_term in zip(grad_sums, grads[1:])))
        squares = squares + jnp.stack([jnp.sum(values * values), jnp.sum(attention * attention), jnp.sum(mlp * mlp), jnp.sum(out_row * out_row)])
        return ((grad_sums, squares), (out_row.astype(jnp.bfloat16), grads[0].astype(jnp.bfloat16)))
    start_state = (zero_sums, jnp.zeros((4,), jnp.float32))
    final_state, outputs = lax.scan(per_row, start_state, (tokens, segment_ids, positions, cotangent))
    grad_sums, squares = final_state
    layer_out, input_grad = outputs
    rms_values = jnp.sqrt(squares / (BATCH * LEN * D))
    gain_grad, shift_grad, qkv_weight_grad, qkv_bias_grad, dense_weight_grad, dense_bias_grad, in_weight_grad, in_bias_grad, out_weight_grad, out_bias_grad = grad_sums
    return (layer_out, input_grad, gain_grad, shift_grad, qkv_weight_grad, qkv_bias_grad, dense_weight_grad, dense_bias_grad, in_weight_grad, in_bias_grad, out_weight_grad, out_bias_grad, rms_values)
```

```python
import functools

import jax
import jax.numpy as jnp
from jax import lax
from jax.experimental import pallas as pl
from jax.experimental.pallas import tpu as pltpu
from jax.sharding import PartitionSpec as P

HD = 64
ROT = 32
epsilon = 1e-05
big_negative = -1e30
rope_base = 10000.0
f32 = jnp.float32
bf16 = jnp.bfloat16
VMEM_LIMIT = 56 << 20


def dot(a, b, ca, cb):
    return lax.dot_general(a, b, (((ca,), (cb,)), ((), ())), preferred_element_type=f32)


def cost(flops, nbytes, trans=0):
    return pl.CostEstimate(flops=int(flops), bytes_accessed=int(nbytes), transcendentals=int(trans))


def params():
    return pltpu.CompilerParams(vmem_limit_bytes=VMEM_LIMIT)


def rope_swap(x):
    width = x.shape[-1]
    lane = lax.broadcasted_iota(jnp.int32, (1, width), 1) % HD
    up = pltpu.roll(x, width - ROT // 2, 1)
    down = pltpu.roll(x, ROT // 2, 1)
    return jnp.where(lane < ROT // 2, up, -down)


def qkv_kernel(x_ref, w_ref, b_ref, c_ref, s_ref, o_ref):
    x = x_ref[...]
    tile = c_ref.shape[-1]
    local = w_ref.shape[-1]
    cosine, sine = c_ref[...], s_ref[...]
    for part in range(3):
        full = dot(x, w_ref[part], 1, 0) + b_ref[part : part + 1, :]
        for at in range(0, local, tile):
            piece = full[:, at : at + tile]
            if part < 2:
                piece = piece * cosine - rope_swap(piece) * sine
            if part == 0:
                piece = piece * (HD**-0.5)
            o_ref[part, :, at : at + tile] = piece.astype(bf16)


def project_qkv(x, w3, bias, cosine, sine, tm=512):
    n, width = x.shape
    local = w3.shape[2]
    tile = cosine.shape[1]
    return pl.pallas_call(
        qkv_kernel,
        grid=(n // tm,),
        in_specs=[
            pl.BlockSpec((tm, width), lambda i: (i, 0)),
            pl.BlockSpec((3, width, local), lambda i: (0, 0, 0)),
            pl.BlockSpec((3, local), lambda i: (0, 0)),
            pl.BlockSpec((tm, tile), lambda i: (i, 0)),
            pl.BlockSpec((tm, tile), lambda i: (i, 0)),
        ],
        out_specs=pl.BlockSpec((3, tm, local), lambda i: (0, i, 0)),
        out_shape=jax.ShapeDtypeStruct((3, n, local), bf16),
        compiler_params=params(),
        cost_estimate=cost(6 * n * width * local, 2 * n * width + 6 * width * local + 6 * n * local),
        name="qkv_rope",
    )(x, w3, bias, cosine, sine)


def hidden_kernel(x_ref, w_ref, b_ref, act_ref, slope_ref):
    x = x_ref[...]
    width = w_ref.shape[1]
    step = min(256, width)
    for at in range(0, width, step):
        h = dot(x, w_ref[:, at : at + step], 1, 0) + b_ref[:, at : at + step]
        square = h * h
        inner = (0.7978845608028654 * h) * (1.0 + 0.044715 * square)
        t = jnp.tanh(inner)
        half = 0.5 + 0.5 * t
        act_ref[:, at : at + step] = (h * half).astype(bf16)
        slope = half + (0.3989422804014327 * h) * (1.0 - t * t) * (1.0 + 0.134145 * square)
        slope_ref[:, at : at + step] = slope.astype(bf16)


def mlp_hidden(x, w, bias, tm=512):
    n, width = x.shape
    units = w.shape[1]
    block = pl.BlockSpec((tm, units), lambda i: (i, 0))
    return pl.pallas_call(
        hidden_kernel,
        grid=(n // tm,),
        in_specs=[
            pl.BlockSpec((tm, width), lambda i: (i, 0)),
            pl.BlockSpec((width, units), lambda i: (0, 0)),
            pl.BlockSpec((1, units), lambda i: (0, 0)),
        ],
        out_specs=[block, block],
        out_shape=[jax.ShapeDtypeStruct((n, units), bf16)] * 2,
        compiler_params=params(),
        cost_estimate=cost(2 * n * width * units, 2 * n * width + 2 * width * units + 4 * n * units, n * units),
        name="mlp_hidden",
    )(x, w, bias)


def grad_in_kernel(g_ref, wo_ref, wd_ref, slope_ref, hg_ref, at_ref, sum_ref):
    g = g_ref[...]
    units = wo_ref.shape[0]
    step = min(256, units)
    ones = jnp.ones((8, g.shape[0]), bf16)

    @pl.when(pl.program_id(0) == 0)
    def _():
        sum_ref[...] = jnp.zeros_like(sum_ref)

    for at in range(0, units, step):
        slope = slope_ref[:, at : at + step].astype(f32)
        hg = (dot(g, wo_ref[at : at + step, :], 1, 1) * slope).astype(bf16)
        hg_ref[:, at : at + step] = hg
        sum_ref[:, at : at + step] += dot(ones, hg, 1, 0)
    at_ref[...] = dot(g, wd_ref[...], 1, 1).astype(bf16)


def grad_in(g, wo, wd, slope, tm=512):
    n, width = g.shape
    units, local = wo.shape[0], wd.shape[0]
    return pl.pallas_call(
        grad_in_kernel,
        grid=(n // tm,),
        in_specs=[
            pl.BlockSpec((tm, width), lambda i: (i, 0)),
            pl.BlockSpec((units, width), lambda i: (0, 0)),
            pl.BlockSpec((local, width), lambda i: (0, 0)),
            pl.BlockSpec((tm, units), lambda i: (i, 0)),
        ],
        out_specs=[
            pl.BlockSpec((tm, units), lambda i: (i, 0)),
            pl.BlockSpec((tm, local), lambda i: (i, 0)),
            pl.BlockSpec((8, units), lambda i: (0, 0)),
        ],
        out_shape=[
            jax.ShapeDtypeStruct((n, units), bf16),
            jax.ShapeDtypeStruct((n, local), bf16),
            jax.ShapeDtypeStruct((8, units), f32),
        ],
        compiler_params=params(),
        cost_estimate=cost(2 * n * width * (units + local), 2 * n * width + 2 * width * (units + local) + 4 * n * units),
        name="grad_in",
    )(g, wo, wd, slope)


def normed_grad_kernel(hg_ref, dq_ref, wi_ref, w3_ref, o_ref, sum_ref):
    @pl.when(pl.program_id(0) == 0)
    def _():
        sum_ref[...] = jnp.zeros_like(sum_ref)

    ones = jnp.ones((8, hg_ref.shape[0]), bf16)
    for part in range(3):
        sum_ref[part] += dot(ones, dq_ref[part], 1, 0)
    width = o_ref.shape[1]
    step = min(512, width)
    for at in range(0, width, step):
        total = dot(hg_ref[...], wi_ref[at : at + step, :], 1, 1)
        for part in range(3):
            total += dot(dq_ref[part], w3_ref[part, at : at + step, :], 1, 1)
        o_ref[:, at : at + step] = total.astype(bf16)


def normed_grad(hg, dqkv, wi, w3, tm=512):
    n, units = hg.shape
    width, local = w3.shape[1:]
    return pl.pallas_call(
        normed_grad_kernel,
        grid=(n // tm,),
        in_specs=[
            pl.BlockSpec((tm, units), lambda i: (i, 0)),
            pl.BlockSpec((3, tm, local), lambda i: (0, i, 0)),
            pl.BlockSpec((width, units), lambda i: (0, 0)),
            pl.BlockSpec((3, width, local), lambda i: (0, 0, 0)),
        ],
        out_specs=[
            pl.BlockSpec((tm, width), lambda i: (i, 0)),
            pl.BlockSpec((3, 8, local), lambda i: (0, 0, 0)),
        ],
        out_shape=[jax.ShapeDtypeStruct((n, width), bf16), jax.ShapeDtypeStruct((3, 8, local), f32)],
        compiler_params=params(),
        cost_estimate=cost(2 * n * width * (units + 3 * local), 2 * n * (width + units + 3 * local) + 2 * width * (units + 3 * local)),
        name="normed_grad",
    )(hg, dqkv, wi, w3)


def attention_kernel(start_ref, q_ref, k_ref, v_ref, do_ref, c_ref, s_ref, o_ref, g_ref, dk_acc, dv_acc, *, bq):
    span, width = q_ref.shape
    lane = lax.broadcasted_iota(jnp.int32, (1, width), 1) // HD
    zero = jnp.zeros((), bf16)

    def turn_back(x, at, n):
        return x * c_ref[at : at + n, :] + rope_swap(x) * s_ref[at : at + n, :]

    for block in range(span // bq):
        at = block * bq
        n = at + bq
        qb = q_ref[at:n, :]
        gb = do_ref[at:n, :]
        keys, vals = k_ref[0:n, :], v_ref[0:n, :]
        key = lax.broadcasted_iota(jnp.int32, (bq, n), 1)
        row = lax.broadcasted_iota(jnp.int32, (bq, n), 0) + at
        allowed = (key >= start_ref[at:n, :]) & (key <= row)
        out = jnp.zeros((bq, width), f32)
        dq = jnp.zeros((bq, width), f32)
        dk = jnp.zeros((n, width), f32)
        dv = jnp.zeros((n, width), f32)
        for head in range(width // HD):
            mine = lane == head
            qh, gh = jnp.where(mine, qb, zero), jnp.where(mine, gb, zero)
            kh, vh = jnp.where(mine, keys, zero), jnp.where(mine, vals, zero)
            scores = jnp.where(allowed, dot(qh, keys, 1, 1), big_negative)
            expd = jnp.exp(scores - jnp.max(scores, axis=1, keepdims=True))
            probs = expd * (1.0 / jnp.sum(expd, axis=1, keepdims=True))
            low = probs.astype(bf16)
            out = out + dot(low, vh, 1, 0)
            prob_grad = dot(gh, vals, 1, 1)
            inner = jnp.sum(probs * prob_grad, axis=1, keepdims=True)
            score_grad = (probs * (prob_grad - inner)).astype(bf16)
            dq = dq + dot(score_grad, kh, 1, 0)
            dk = dk + dot(score_grad, qh, 0, 0)
            dv = dv + dot(low, gh, 0, 0)
        o_ref[at:n, :] = out.astype(bf16)
        g_ref[0, at:n, :] = turn_back(dq * (HD**-0.5), at, bq).astype(bf16)
        if block:
            dk_acc[0:at, :] += dk[0:at]
            dv_acc[0:at, :] += dv[0:at]
        dk_acc[at:n, :] = dk[at:n]
        dv_acc[at:n, :] = dv[at:n]
    g_ref[1] = turn_back(dk_acc[...], 0, span).astype(bf16)
    g_ref[2] = dv_acc[...].astype(bf16)


def attention_both(start, qkv, grad, cosine, sine, span, bq=512):
    n, local = grad.shape
    width = cosine.shape[1]
    bq = min(bq, span)
    part = lambda which: pl.BlockSpec((None, span, width), lambda t, p: (which, t, p))
    table = pl.BlockSpec((span, width), lambda t, p: (t, 0))
    return pl.pallas_call(
        functools.partial(attention_kernel, bq=bq),
        grid=(n // span, local // width),
        in_specs=[
            pl.BlockSpec((span, 1), lambda t, p: (t, 0)),
            part(0),
            part(1),
            part(2),
            pl.BlockSpec((span, width), lambda t, p: (t, p)),
            table,
            table,
        ],
        out_specs=[
            pl.BlockSpec((span, width), lambda t, p: (t, p)),
            pl.BlockSpec((3, span, width), lambda t, p: (0, t, p)),
        ],
        out_shape=[jax.ShapeDtypeStruct((n, local), bf16), jax.ShapeDtypeStruct((3, n, local), bf16)],
        scratch_shapes=[pltpu.VMEM((span, width), f32)] * 2,
        compiler_params=params(),
        cost_estimate=cost(n * span * 0.75 * local * 2 * 6 * 4, 2 * n * local * 9, n * span * local // HD),
        name="attention_both",
    )(start, qkv, qkv, qkv, grad, cosine, sine)


def line_ok(size):
    return size >= 4 and size & (size - 1) == 0


def sum_rows(part, size):
    kind = part.dtype
    if not line_ok(size):
        return lax.psum(part, "rows").astype(kind)
    groups = range(0, size, 4)
    send = lambda a, perm: lax.ppermute(a, "rows", perm)
    add = lambda a, b: (a.astype(f32) + b.astype(f32)).astype(kind)
    part = add(part, send(part, [(g + a, g + b) for g in groups for a, b in ((0, 1), (3, 2))]))
    part = add(part, send(part, [(g + a, g + b) for g in groups for a, b in ((1, 2), (2, 1))]))
    hop = 4
    while hop < size:
        part = add(part, send(part, [(i, i ^ hop) for i in range(size)]))
        hop *= 2
    back = send(part, [(g + a, g + b) for g in groups for a, b in ((1, 0), (2, 3))])
    place = lax.axis_index("rows") % 4
    return jnp.where((place == 1) | (place == 2), part, back)


def sum_tp(part, size):
    if size & (size - 1):
        return lax.psum(part, "tp")
    hop = 1
    while hop < size:
        part = part + lax.ppermute(part, "tp", [(i, i ^ hop) for i in range(size)])
        hop *= 2
    return part


def body(
    tokens,
    segment_ids,
    positions,
    norm_gain,
    norm_shift,
    query_key_value_weight,
    b_qkv,
    dense_weight,
    b_dense,
    inward_weight,
    b_in,
    outward_weight,
    b_out,
    cotangent,
):
    rows, tp = lax.axis_size("rows"), lax.axis_size("tp")
    seqs, here, width = tokens.shape
    length = here * tp
    n = seqs * length
    local = query_key_value_weight.shape[2]
    tile = min(128, local)
    span = length // 2

    values = tokens.astype(f32)
    gain, shift = norm_gain.astype(f32), norm_shift.astype(f32)
    center = values - jnp.mean(values, axis=-1, keepdims=True)
    inverse = lax.rsqrt(jnp.mean(center * center, axis=-1, keepdims=True) + epsilon)
    unit = center * inverse
    normed_low = (unit * gain + shift).astype(bf16)
    gather = lambda a: lax.all_gather(a, "tp", axis=1, tiled=True).reshape(n, width)
    normed = gather(normed_low)
    grad = gather(cotangent)
    dense_full = lax.all_gather(dense_weight, "tp", axis=0, tiled=True)

    half_rot = ROT // 2
    frequency = rope_base ** (-2.0 * jnp.arange(half_rot, dtype=f32) / ROT)
    place = positions.reshape(n, 1)
    angles = place.astype(f32) * frequency
    heads = tile // HD
    rest = HD - ROT
    cosine, sine = jnp.cos(angles), jnp.sin(angles)
    ones, zeros = jnp.ones((n, rest), f32), jnp.zeros((n, rest), f32)
    cosine = jnp.concatenate([cosine, cosine, ones] * heads, axis=1)
    sine = jnp.concatenate([sine, sine, zeros] * heads, axis=1)
    start = jnp.arange(n, dtype=jnp.int32)[:, None] % span - place

    w3 = jnp.transpose(query_key_value_weight, (1, 0, 2))
    qkv = project_qkv(normed, w3, b_qkv.astype(f32), cosine, sine)
    act, slope = mlp_hidden(normed, inward_weight, b_in.astype(f32)[None])

    contract = lambda a, b: dot(a, b, 0, 0).astype(bf16)
    out_wg = sum_rows(contract(act, grad), rows)
    hidden_grad, attended_grad, in_bias = grad_in(grad, outward_weight, dense_weight, slope)
    in_wg = sum_rows(contract(normed, hidden_grad), rows)
    mlp_part = dot(act, outward_weight, 1, 0).astype(bf16).reshape(seqs, length, width)
    mlp_tok = lax.psum_scatter(mlp_part, "tp", scatter_dimension=1, tiled=True)

    attended, dqkv = attention_both(start, qkv, attended_grad, cosine, sine, span)
    mine = lax.all_to_all(attended.reshape(seqs, length, local), "tp", split_axis=1, concat_axis=2, tiled=True)
    part, qkv_bias = normed_grad(hidden_grad, dqkv, inward_weight, w3)
    back_tok = lax.psum_scatter(part.reshape(seqs, length, width), "tp", scatter_dimension=1, tiled=True)
    qkv_wg = jnp.stack([contract(normed, dqkv[i]) for i in range(3)])
    qkv_wg = sum_rows(qkv_wg, rows)
    dense_wg = sum_rows(contract(attended, grad), rows)

    attention = dot(mine.reshape(seqs * here, width), dense_full, 1, 0).reshape(seqs, here, width) + b_dense.astype(f32)
    mlp = mlp_tok.astype(f32) + b_out.astype(f32)
    layer_sum = values + attention + mlp
    layer_out = layer_sum.astype(bf16)
    squares = jnp.stack([jnp.sum(a * a) for a in (values, attention, mlp, layer_sum)])

    bias_cols = lax.dynamic_slice_in_dim(grad, lax.axis_index("tp") * (width // tp), width // tp, 1)
    out_bias = jnp.sum(bias_cols.astype(f32), axis=0)
    units = in_bias.shape[1]
    small = jnp.concatenate([in_bias[0], qkv_bias[:, 0].reshape(-1), out_bias])
    small = sum_rows(small.reshape(-1, 128), rows).reshape(-1)
    in_bias_grad = small[:units]
    qkv_bias_grad = small[units : units + 3 * local].reshape(3, local)
    out_bias_grad = small[units + 3 * local :]

    normed_back = back_tok.astype(f32)
    unit_grad = normed_back * gain
    mean_grad = jnp.mean(unit_grad, axis=-1, keepdims=True)
    mean_both = jnp.mean(unit_grad * unit, axis=-1, keepdims=True)
    value_grad = (unit_grad - mean_grad - unit * mean_both) * inverse
    input_grad = (cotangent.astype(f32) + value_grad).astype(bf16)
    gain_part = jnp.sum(normed_back * unit, axis=(0, 1))
    shift_part = jnp.sum(normed_back, axis=(0, 1))
    pad = jnp.zeros((124,), f32)
    packed = jnp.concatenate([gain_part, shift_part, squares, pad]).reshape(-1, 128)
    packed = sum_rows(sum_tp(packed, tp), rows).reshape(-1)
    slice_at = lambda a: lax.dynamic_slice_in_dim(a, lax.axis_index("tp") * (width // tp), width // tp, 0)
    gain_grad, shift_grad = slice_at(packed[:width]), slice_at(packed[width : 2 * width])
    rms_values = jnp.sqrt(packed[2 * width : 2 * width + 4] / (seqs * rows * length * width))

    return (
        layer_out,
        input_grad,
        gain_grad,
        shift_grad,
        jnp.transpose(qkv_wg.astype(f32), (1, 0, 2)),
        qkv_bias_grad,
        dense_wg.astype(f32),
        out_bias_grad,
        in_wg.astype(f32),
        in_bias_grad,
        out_wg.astype(f32),
        out_bias_grad,
        rms_values,
    )


def solution(mesh):
    in_specs = (
        P("rows", "tp", None),
        P("rows", None),
        P("rows", None),
        P(),
        P(),
        P(None, None, "tp"),
        P(None, "tp"),
        P("tp", None),
        P(),
        P(None, "tp"),
        P("tp"),
        P("tp", None),
        P(),
        P("rows", "tp", None),
    )
    out_specs = (
        P("rows", "tp", None),
        P("rows", "tp", None),
        P("tp"),
        P("tp"),
        P(None, None, "tp"),
        P(None, "tp"),
        P("tp", None),
        P("tp"),
        P(None, "tp"),
        P("tp"),
        P("tp", None),
        P("tp"),
        P(),
    )
    return jax.shard_map(body, mesh=mesh, in_specs=in_specs, out_specs=out_specs, check_vma=False)
```

```python
import functools

import jax
import jax.numpy as jnp
from jax import lax
from jax.experimental import pallas as pl
from jax.experimental.pallas import tpu as pltpu
from jax.sharding import PartitionSpec as P

HD = 64
ROT = 32
epsilon = 1e-05
big_negative = -1e30
rope_base = 10000.0
f32 = jnp.float32
bf16 = jnp.bfloat16
VMEM_LIMIT = 56 << 20
FINISH_WEIGHT = int(1.45e11)


def dot(a, b, ca, cb):
    return lax.dot_general(a, b, (((ca,), (cb,)), ((), ())), preferred_element_type=f32)


SMALL = pl.CostEstimate(flops=1, bytes_accessed=1, transcendentals=0)


def params():
    return pltpu.CompilerParams(vmem_limit_bytes=VMEM_LIMIT)


class Order:
    def __init__(self):
        self.last = ()

    def __call__(self, op, *operands):
        operands, _ = lax.optimization_barrier((operands, self.last))
        result = op(*operands)
        self.last = jax.tree.leaves(result)
        return result


def rope_swap(x):
    width = x.shape[-1]
    lane = lax.broadcasted_iota(jnp.int32, (1, width), 1) % HD
    up = pltpu.roll(x, width - ROT // 2, 1)
    down = pltpu.roll(x, ROT // 2, 1)
    return jnp.where(lane < ROT // 2, up, -down)


def qkv_kernel(x_ref, w_ref, b_ref, c_ref, s_ref, o_ref):
    x = x_ref[...]
    tile = c_ref.shape[-1]
    local = w_ref.shape[-1]
    cosine, sine = c_ref[...], s_ref[...]
    for part in range(3):
        full = dot(x, w_ref[part], 1, 0) + b_ref[part : part + 1, :]
        for at in range(0, local, tile):
            piece = full[:, at : at + tile]
            if part < 2:
                piece = piece * cosine - rope_swap(piece) * sine
            if part == 0:
                piece = piece * (HD**-0.5)
            o_ref[part, :, at : at + tile] = piece.astype(bf16)


def project_qkv(x, w3, bias, cosine, sine, tm=512):
    n, width = x.shape
    local = w3.shape[2]
    tile = cosine.shape[1]
    return pl.pallas_call(
        qkv_kernel,
        grid=(n // tm,),
        in_specs=[
            pl.BlockSpec((tm, width), lambda i: (i, 0)),
            pl.BlockSpec((3, width, local), lambda i: (0, 0, 0)),
            pl.BlockSpec((3, local), lambda i: (0, 0)),
            pl.BlockSpec((tm, tile), lambda i: (i, 0)),
            pl.BlockSpec((tm, tile), lambda i: (i, 0)),
        ],
        out_specs=pl.BlockSpec((3, tm, local), lambda i: (0, i, 0)),
        out_shape=jax.ShapeDtypeStruct((3, n, local), bf16),
        compiler_params=params(),
        cost_estimate=SMALL,
        name="qkv_rope",
    )(x, w3, bias, cosine, sine)


def hidden_kernel(x_ref, w_ref, b_ref, act_ref, slope_ref):
    x = x_ref[...]
    width = w_ref.shape[1]
    step = min(256, width)
    for at in range(0, width, step):
        h = dot(x, w_ref[:, at : at + step], 1, 0) + b_ref[:, at : at + step]
        square = h * h
        inner = (0.7978845608028654 * h) * (1.0 + 0.044715 * square)
        t = jnp.tanh(inner)
        half = 0.5 + 0.5 * t
        act_ref[:, at : at + step] = (h * half).astype(bf16)
        slope = half + (0.3989422804014327 * h) * (1.0 - t * t) * (1.0 + 0.134145 * square)
        slope_ref[:, at : at + step] = slope.astype(bf16)


def mlp_hidden(x, w, bias, tm=512):
    n, width = x.shape
    units = w.shape[1]
    block = pl.BlockSpec((tm, units), lambda i: (i, 0))
    return pl.pallas_call(
        hidden_kernel,
        grid=(n // tm,),
        in_specs=[
            pl.BlockSpec((tm, width), lambda i: (i, 0)),
            pl.BlockSpec((width, units), lambda i: (0, 0)),
            pl.BlockSpec((1, units), lambda i: (0, 0)),
        ],
        out_specs=[block, block],
        out_shape=[jax.ShapeDtypeStruct((n, units), bf16)] * 2,
        compiler_params=params(),
        cost_estimate=SMALL,
        name="mlp_hidden",
    )(x, w, bias)


def grad_in_kernel(g_ref, wo_ref, wd_ref, slope_ref, hg_ref, at_ref, sum_ref):
    g = g_ref[...]
    units = wo_ref.shape[0]
    step = min(256, units)

    @pl.when(pl.program_id(0) == 0)
    def _():
        sum_ref[...] = jnp.zeros_like(sum_ref)

    for at in range(0, units, step):
        slope = slope_ref[:, at : at + step].astype(f32)
        hg = (dot(g, wo_ref[at : at + step, :], 1, 1) * slope).astype(bf16)
        hg_ref[:, at : at + step] = hg
        sum_ref[0:1, at : at + step] += jnp.sum(hg.astype(f32), axis=0, keepdims=True)
    at_ref[...] = dot(g, wd_ref[...], 1, 1).astype(bf16)


def grad_in(g, wo, wd, slope, tm=512):
    n, width = g.shape
    units, local = wo.shape[0], wd.shape[0]
    return pl.pallas_call(
        grad_in_kernel,
        grid=(n // tm,),
        in_specs=[
            pl.BlockSpec((tm, width), lambda i: (i, 0)),
            pl.BlockSpec((units, width), lambda i: (0, 0)),
            pl.BlockSpec((local, width), lambda i: (0, 0)),
            pl.BlockSpec((tm, units), lambda i: (i, 0)),
        ],
        out_specs=[
            pl.BlockSpec((tm, units), lambda i: (i, 0)),
            pl.BlockSpec((tm, local), lambda i: (i, 0)),
            pl.BlockSpec((8, units), lambda i: (0, 0)),
        ],
        out_shape=[
            jax.ShapeDtypeStruct((n, units), bf16),
            jax.ShapeDtypeStruct((n, local), bf16),
            jax.ShapeDtypeStruct((8, units), f32),
        ],
        compiler_params=params(),
        cost_estimate=SMALL,
        name="grad_in",
    )(g, wo, wd, slope)


def tokens_kernel(x_ref, w_ref, o_ref):
    width = w_ref.shape[1]
    step = min(512, width)
    for at in range(0, width, step):
        o_ref[:, at : at + step] = dot(x_ref[...], w_ref[:, at : at + step], 1, 0).astype(o_ref.dtype)


def tokens_by_weight(x, w, tm=512):
    n, depth = x.shape
    width = w.shape[1]
    return pl.pallas_call(
        tokens_kernel,
        grid=(n // tm,),
        in_specs=[pl.BlockSpec((tm, depth), lambda i: (i, 0)), pl.BlockSpec((depth, width), lambda i: (0, 0))],
        out_specs=pl.BlockSpec((tm, width), lambda i: (i, 0)),
        out_shape=jax.ShapeDtypeStruct((n, width), bf16),
        compiler_params=params(),
        cost_estimate=SMALL,
        name="tokens_by_weight",
    )(x, w)


def weight_grad_kernel(a_ref, b_ref, *o_refs):
    full = dot(a_ref[...], b_ref[...], 0, 0).astype(bf16)
    high = full.shape[0] // len(o_refs)
    for i, o_ref in enumerate(o_refs):
        o_ref[...] = full[i * high : (i + 1) * high]


def weight_grad(a, b, pieces, tile=512):
    n, rows = a.shape
    cols = b.shape[1]
    tile = min(tile, cols)
    high = rows // pieces
    return pl.pallas_call(
        weight_grad_kernel,
        grid=(cols // tile,),
        in_specs=[
            pl.BlockSpec((n, rows), lambda j: (0, 0), pipeline_mode=pl.Buffered(1)),
            pl.BlockSpec((n, tile), lambda j: (0, j)),
        ],
        out_specs=[pl.BlockSpec((high, tile), lambda j: (0, j))] * pieces,
        out_shape=[jax.ShapeDtypeStruct((high, cols), bf16)] * pieces,
        compiler_params=params(),
        cost_estimate=SMALL,
        name="weight_grad",
    )(a, b)


def weight_grad_rows_kernel(a_ref, b_ref, *o_refs, counts):
    full = dot(a_ref[...], b_ref[...], 0, 0).astype(bf16)
    step = pl.program_id(0)
    first = 0
    for o_ref, count in zip(o_refs, counts):

        @pl.when((step >= first) & (step < first + count))
        def _(o_ref=o_ref):
            o_ref[...] = full

        first += count


def weight_grad_rows(a, b, shares, tile=512):
    n, rows = a.shape
    cols = b.shape[1]
    counts = [rows * share // sum(shares) // tile for share in shares]
    firsts = [sum(counts[:i]) for i in range(len(counts))]
    out = lambda i: pl.BlockSpec((tile, cols), lambda j: (jnp.clip(j - firsts[i], 0, counts[i] - 1), 0))
    return pl.pallas_call(
        functools.partial(weight_grad_rows_kernel, counts=counts),
        grid=(rows // tile,),
        in_specs=[
            pl.BlockSpec((n, tile), lambda j: (0, j)),
            pl.BlockSpec((n, cols), lambda j: (0, 0), pipeline_mode=pl.Buffered(1)),
        ],
        out_specs=[out(i) for i in range(len(counts))],
        out_shape=[jax.ShapeDtypeStruct((count * tile, cols), bf16) for count in counts],
        compiler_params=params(),
        cost_estimate=SMALL,
        name="weight_grad_rows",
    )(a, b)


def weight_grad_parts_kernel(a_ref, b_ref, *o_refs):
    for part, o_ref in enumerate(o_refs):
        o_ref[...] = dot(a_ref[...], b_ref[part], 0, 0).astype(bf16)


def weight_grad_parts(a, b, tile=512):
    n, rows = a.shape
    parts, _, cols = b.shape
    return pl.pallas_call(
        weight_grad_parts_kernel,
        grid=(rows // tile,),
        in_specs=[
            pl.BlockSpec((n, tile), lambda j: (0, j)),
            pl.BlockSpec((parts, n, cols), lambda j: (0, 0, 0), pipeline_mode=pl.Buffered(1)),
        ],
        out_specs=[pl.BlockSpec((tile, cols), lambda j: (j, 0))] * parts,
        out_shape=[jax.ShapeDtypeStruct((rows, cols), bf16)] * parts,
        compiler_params=params(),
        cost_estimate=SMALL,
        name="weight_grad_parts",
    )(a, b)


def normed_grad_kernel(hg_ref, dq_ref, wi_ref, w3_ref, x_ref, shift_ref, o_ref, sum_ref, norm_ref):
    @pl.when(pl.program_id(0) == 0)
    def _():
        sum_ref[...] = jnp.zeros_like(sum_ref)
        norm_ref[...] = jnp.zeros_like(norm_ref)

    for part in range(3):
        sum_ref[part, 0:1] += jnp.sum(dq_ref[part].astype(f32), axis=0, keepdims=True)
    width = o_ref.shape[1]
    step = min(512, width)
    for at in range(0, width, step):
        cut = slice(at, at + step)
        total = dot(hg_ref[...], wi_ref[cut, :], 1, 1)
        for part in range(3):
            total += dot(dq_ref[part], w3_ref[part, cut, :], 1, 1)
        o_ref[:, cut] = total.astype(bf16)
        scaled = x_ref[:, cut].astype(f32) - shift_ref[:, cut]
        norm_ref[0:1, cut] += jnp.sum(total * scaled, axis=0, keepdims=True)
        norm_ref[1:2, cut] += jnp.sum(total, axis=0, keepdims=True)


def normed_grad(hg, dqkv, wi, w3, x, shift, tm=512):
    n, units = hg.shape
    width, local = w3.shape[1:]
    return pl.pallas_call(
        normed_grad_kernel,
        grid=(n // tm,),
        in_specs=[
            pl.BlockSpec((tm, units), lambda i: (i, 0)),
            pl.BlockSpec((3, tm, local), lambda i: (0, i, 0)),
            pl.BlockSpec((width, units), lambda i: (0, 0)),
            pl.BlockSpec((3, width, local), lambda i: (0, 0, 0)),
            pl.BlockSpec((tm, width), lambda i: (i, 0)),
            pl.BlockSpec((1, width), lambda i: (0, 0)),
        ],
        out_specs=[
            pl.BlockSpec((tm, width), lambda i: (i, 0)),
            pl.BlockSpec((3, 8, local), lambda i: (0, 0, 0)),
            pl.BlockSpec((8, width), lambda i: (0, 0)),
        ],
        out_shape=[
            jax.ShapeDtypeStruct((n, width), bf16),
            jax.ShapeDtypeStruct((3, 8, local), f32),
            jax.ShapeDtypeStruct((8, width), f32),
        ],
        compiler_params=params(),
        cost_estimate=SMALL,
        name="normed_grad",
    )(hg, dqkv, wi, w3, x, shift)


def attention_kernel(start_ref, q_ref, k_ref, v_ref, do_ref, c_ref, s_ref, o_ref, by_owner_ref, g_ref, dk_acc, dv_acc, *, bq):
    span, width = q_ref.shape
    lane = lax.broadcasted_iota(jnp.int32, (1, width), 1) // HD
    zero = jnp.zeros((), bf16)

    def turn_back(x, at, n):
        return x * c_ref[at : at + n, :] + rope_swap(x) * s_ref[at : at + n, :]

    for block in range(span // bq):
        at = block * bq
        n = at + bq
        qb = q_ref[at:n, :]
        gb = do_ref[at:n, :]
        keys, vals = k_ref[0:n, :], v_ref[0:n, :]
        key = lax.broadcasted_iota(jnp.int32, (bq, n), 1)
        row = lax.broadcasted_iota(jnp.int32, (bq, n), 0) + at
        allowed = (key >= start_ref[at:n, :]) & (key <= row)
        out = jnp.zeros((bq, width), f32)
        dq = jnp.zeros((bq, width), f32)
        dk = jnp.zeros((n, width), f32)
        dv = jnp.zeros((n, width), f32)
        for head in range(width // HD):
            mine = lane == head
            qh, gh = jnp.where(mine, qb, zero), jnp.where(mine, gb, zero)
            kh, vh = jnp.where(mine, keys, zero), jnp.where(mine, vals, zero)
            scores = jnp.where(allowed, dot(qh, keys, 1, 1), big_negative)
            expd = jnp.exp(scores - jnp.max(scores, axis=1, keepdims=True))
            probs = expd * (1.0 / jnp.sum(expd, axis=1, keepdims=True))
            low = probs.astype(bf16)
            out = out + dot(low, vh, 1, 0)
            prob_grad = dot(gh, vals, 1, 1)
            inner = jnp.sum(probs * prob_grad, axis=1, keepdims=True)
            score_grad = (probs * (prob_grad - inner)).astype(bf16)
            dq = dq + dot(score_grad, kh, 1, 0)
            dk = dk + dot(score_grad, qh, 0, 0)
            dv = dv + dot(low, gh, 0, 0)
        out = out.astype(bf16)
        o_ref[at:n, :] = out
        here = by_owner_ref.shape[1]
        for own in range(bq // here):
            by_owner_ref[at // here + own] = out[own * here : (own + 1) * here]
        g_ref[0, at:n, :] = turn_back(dq * (HD**-0.5), at, bq).astype(bf16)
        if block:
            dk_acc[0:at, :] += dk[0:at]
            dv_acc[0:at, :] += dv[0:at]
        dk_acc[at:n, :] = dk[at:n]
        dv_acc[at:n, :] = dv[at:n]
    g_ref[1] = turn_back(dk_acc[...], 0, span).astype(bf16)
    g_ref[2] = dv_acc[...].astype(bf16)


def attention_both(start, qkv, grad, cosine, sine, span, owners, bq=512):
    n, local = grad.shape
    here = 2 * span // owners
    width = cosine.shape[1]
    bq = min(bq, span)
    part = lambda which: pl.BlockSpec((None, span, width), lambda t, p: (which, t, p))
    table = pl.BlockSpec((span, width), lambda t, p: (t, 0))
    return pl.pallas_call(
        functools.partial(attention_kernel, bq=bq),
        grid=(n // span, local // width),
        in_specs=[
            pl.BlockSpec((span, 1), lambda t, p: (t, 0)),
            part(0),
            part(1),
            part(2),
            pl.BlockSpec((span, width), lambda t, p: (t, p)),
            table,
            table,
        ],
        out_specs=[
            pl.BlockSpec((span, width), lambda t, p: (t, p)),
            pl.BlockSpec((owners // 2, None, here, width), lambda t, p: (t % 2, t // 2, 0, p)),
            pl.BlockSpec((3, span, width), lambda t, p: (0, t, p)),
        ],
        out_shape=[
            jax.ShapeDtypeStruct((n, local), bf16),
            jax.ShapeDtypeStruct((owners, n // (2 * span), here, local), bf16),
            jax.ShapeDtypeStruct((3, n, local), bf16),
        ],
        scratch_shapes=[pltpu.VMEM((span, width), f32)] * 2,
        compiler_params=params(),
        cost_estimate=SMALL,
        name="attention_both",
    )(start, qkv, qkv, qkv, grad, cosine, sine)


def own_kernel(x_ref, w_ref, b_ref, o_ref):
    owners, seqs, here, local = x_ref.shape
    total = jnp.zeros(o_ref.shape, f32) + b_ref[...]
    for owner in range(owners):
        x = x_ref[owner].reshape(seqs * here, local)
        total += dot(x, w_ref[owner * local : (owner + 1) * local, :], 1, 0)
    o_ref[...] = total


def project_own(x, w, bias, tile=512):
    owners, seqs, here, local = x.shape
    width = w.shape[1]
    return pl.pallas_call(
        own_kernel,
        grid=(width // tile,),
        in_specs=[
            pl.BlockSpec(x.shape, lambda j: (0, 0, 0, 0)),
            pl.BlockSpec((owners * local, tile), lambda j: (0, j)),
            pl.BlockSpec((1, tile), lambda j: (0, j)),
        ],
        out_specs=pl.BlockSpec((seqs * here, tile), lambda j: (0, j)),
        out_shape=jax.ShapeDtypeStruct((seqs * here, width), f32),
        compiler_params=params(),
        cost_estimate=SMALL,
        name="project_own",
    )(x, w, bias)


def line_ok(size):
    return size >= 4 and size & (size - 1) == 0


class RowSum:
    def __init__(self, part, size):
        self.part, self.size, self.axis = part, size, "rows"
        groups = range(0, size, 4)
        pairs = lambda *ends: [(g + a, g + b) for g in groups for a, b in ends]
        self.hops = [pairs((0, 1), (3, 2)), pairs((1, 2), (2, 1))]
        hop = 4
        while hop < size:
            self.hops.append([(i, i ^ hop) for i in range(size)])
            hop *= 2
        self.hops.append(pairs((1, 0), (2, 3)))
        self.send()

    def send(self):
        if line_ok(self.size):
            self.came = lax.ppermute(self.part, self.axis, self.hops.pop(0))

    def fold(self, order):
        if line_ok(self.size) and self.hops:
            add = lambda a, b: (a.astype(f32) + b.astype(f32)).astype(a.dtype)
            self.part = order(add, self.part, self.came)
            self.send()

    def complete(self, order):
        while self.hops:
            self.fold(order)

    def result(self, order=None):
        if not line_ok(self.size):
            return lax.psum(self.part.astype(f32), "rows")
        self.complete(order or Order())
        place = lax.axis_index("rows") % 4
        return jnp.where((place == 1) | (place == 2), self.part, self.came).astype(f32)


def finish_kernel(inner_ref, *refs, counts):
    o_ref = refs[-1]
    step = pl.program_id(0)
    first = 0
    for i, count in enumerate(counts):
        kept, came = refs[2 * i], refs[2 * i + 1]
        mine = (step >= first) & (step < first + count)

        @pl.when(mine & (inner_ref[0] == 1))
        def _(kept=kept):
            o_ref[...] = kept[...].astype(f32)

        @pl.when(mine & (inner_ref[0] == 0))
        def _(came=came):
            o_ref[...] = came[...].astype(f32)

        first += count


def finish_rows(sums, order, tile=256, weight=1):
    if not line_ok(sums[0].size):
        return jnp.concatenate([a.result() for a in sums])
    for a in sums:
        a.complete(order)
    cols = sums[0].part.shape[1]
    tile = min([tile] + [a.part.shape[0] for a in sums])
    counts = [a.part.shape[0] // tile for a in sums]
    firsts = [sum(counts[:i]) for i in range(len(counts))]
    pair = lambda i: [pl.BlockSpec((tile, cols), lambda j: (jnp.clip(j - firsts[i], 0, counts[i] - 1), 0))] * 2
    place = lax.axis_index("rows") % 4
    inner = ((place == 1) | (place == 2)).astype(jnp.int32).reshape(1)
    call = pl.pallas_call(
        functools.partial(finish_kernel, counts=counts),
        grid=(sum(counts),),
        in_specs=[pl.BlockSpec(memory_space=pltpu.SMEM)] + [b for i in range(len(sums)) for b in pair(i)],
        out_specs=pl.BlockSpec((tile, cols), lambda j: (j, 0)),
        out_shape=jax.ShapeDtypeStruct((sum(counts) * tile, cols), f32),
        compiler_params=params(),
        cost_estimate=pl.CostEstimate(flops=int(weight), bytes_accessed=1, transcendentals=0),
        name="finish_rows",
    )
    return order(lambda *a: call(inner, *a), *[b for a in sums for b in (a.part, a.came)])


class Gather:
    core, x, y = 1, 2, 4

    def __init__(self, piece, size):
        self.piece, self.size = piece, size
        self.exchange = size == 8
        if self.exchange:
            self.from_x, self.from_y = self.send(piece, self.x), self.send(piece, self.y)
            self.from_core = self.send(piece, self.core)

    def send(self, a, step):
        return lax.ppermute(a, "tp", [(i, i ^ step) for i in range(self.size)])

    def forward(self, order):
        if self.exchange:
            half = self.piece.shape[1] // 2
            cut = lambda a, b: (a, b, a[:, :half], b[:, half:])
            self.from_x, self.from_y, low, high = order(cut, self.from_x, self.from_y)
            self.low, self.high = self.send(low, self.y), self.send(high, self.x)
            self.pair_x, self.pair_y = self.send(self.from_x, self.core), self.send(self.from_y, self.core)

    def near(self, order):
        if self.exchange:
            steps = (0, self.core, self.x, self.y, self.x | self.core, self.y | self.core)
            pieces = (self.piece, self.from_core, self.from_x, self.from_y, self.pair_x, self.pair_y)
            self.full = order(lambda *a: place_pieces(None, a, steps, (0,) * 6, self.size), *pieces)

    def near_pairs(self):
        if self.exchange:
            self.pair_low, self.pair_high = self.send(self.low, self.core), self.send(self.high, self.core)

    def far(self, order):
        seqs, here, width = self.piece.shape
        if not self.exchange:
            full = lax.all_gather(self.piece, "tp", axis=1, tiled=True)
            return full.reshape(seqs * self.size * here, width)
        far, half = self.x | self.y, here // 2
        steps, ats = (far, far, far | self.core, far | self.core), (0, half, 0, half)
        place = lambda full, *a: place_pieces(full, a, steps, ats, self.size)
        full = order(place, self.full, self.low, self.high, self.pair_low, self.pair_high)
        return full.reshape(seqs * self.size * here, width)


def place_kernel(me_ref, *refs, counts, held):
    pieces, o_ref = refs[held:-1], refs[-1]
    step = pl.program_id(0)
    first = 0
    for piece, count in zip(pieces, counts):

        @pl.when((step >= first) & (step < first + count))
        def _(piece=piece):
            o_ref[...] = piece[...]

        first += count


def place_pieces(full, pieces, steps, ats, size):
    seqs, _, width = pieces[0].shape
    here = max(a.shape[1] for a in pieces) if full is None else full.shape[2]
    held = 0 if full is None else 1
    unit = min(a.shape[1] for a in pieces)
    counts = [a.shape[1] // unit for a in pieces]
    firsts = [sum(counts[:i]) for i in range(len(counts))]

    def piece_spec(i):
        return pl.BlockSpec((seqs, unit, width), lambda j, me: (0, jnp.clip(j - firsts[i], 0, counts[i] - 1), 0))

    def target(j, me):
        device, at = me[0] ^ steps[0], j + ats[0] // unit
        for i in range(1, len(pieces)):
            device = jnp.where(j >= firsts[i], me[0] ^ steps[i], device)
            at = jnp.where(j >= firsts[i], j - firsts[i] + ats[i] // unit, at)
        return 0, device, at, 0

    hbm = pl.BlockSpec(memory_space=pl.ANY)
    me = lax.axis_index("tp").astype(jnp.int32).reshape(1)
    return pl.pallas_call(
        functools.partial(place_kernel, counts=counts, held=held),
        grid_spec=pltpu.PrefetchScalarGridSpec(
            num_scalar_prefetch=1,
            grid=(sum(counts),),
            in_specs=[hbm] * held + [piece_spec(i) for i in range(len(pieces))],
            out_specs=pl.BlockSpec((seqs, None, unit, width), target),
        ),
        out_shape=jax.ShapeDtypeStruct((seqs, size, here, width), bf16),
        input_output_aliases={1: 0} if held else {},
        compiler_params=params(),
        cost_estimate=SMALL,
        name="place_pieces",
    )(me, *([full] if held else []), *pieces)


class TpSum:
    def __init__(self, part, size):
        self.part, self.size, self.hop = part, size, 1
        self.send()

    def send(self):
        if self.size & (self.size - 1) == 0 and self.hop < self.size:
            self.came = lax.ppermute(self.part, "tp", [(i, i ^ self.hop) for i in range(self.size)])

    def fold(self, order):
        if self.size & (self.size - 1):
            self.part, self.size = lax.psum(self.part, "tp"), 1
        elif self.hop < self.size:
            self.part = order(lambda a, b: a + b, self.part, self.came)
            self.hop *= 2
            self.send()

    def result(self, order):
        while self.hop < self.size:
            self.fold(order)
        return self.part


def body(
    tokens,
    segment_ids,
    positions,
    norm_gain,
    norm_shift,
    query_key_value_weight,
    b_qkv,
    dense_weight,
    b_dense,
    inward_weight,
    b_in,
    outward_weight,
    b_out,
    cotangent,
):
    rows, tp = lax.axis_size("rows"), lax.axis_size("tp")
    seqs, here, width = tokens.shape
    length = here * tp
    n = seqs * length
    local = query_key_value_weight.shape[2]
    tile = min(128, local)
    span = length // 2

    order = Order()
    values = tokens.astype(f32)
    gain, shift = norm_gain.astype(f32), norm_shift.astype(f32)
    center = values - jnp.mean(values, axis=-1, keepdims=True)
    inverse = lax.rsqrt(jnp.mean(center * center, axis=-1, keepdims=True) + epsilon)
    unit = center * inverse
    normed_low = (unit * gain + shift).astype(bf16)
    gather_normed = Gather(normed_low, tp)

    def tables(positions, weight):
        half_rot = ROT // 2
        frequency = rope_base ** (-2.0 * jnp.arange(half_rot, dtype=f32) / ROT)
        place = positions.reshape(n, 1)
        angles = place.astype(f32) * frequency
        heads = tile // HD
        rest = HD - ROT
        cosine, sine = jnp.cos(angles), jnp.sin(angles)
        ones, zeros = jnp.ones((n, rest), f32), jnp.zeros((n, rest), f32)
        cosine = jnp.concatenate([cosine, cosine, ones] * heads, axis=1)
        sine = jnp.concatenate([sine, sine, zeros] * heads, axis=1)
        start = jnp.arange(n, dtype=jnp.int32)[:, None] % span - place
        return cosine, sine, start, jnp.transpose(weight, (1, 0, 2))

    order.last = [normed_low]
    cosine, sine, start, w3 = order(tables, positions, query_key_value_weight)
    gather_normed.forward(order)
    gather_normed.near(order)
    gather_grad = Gather(order(lambda a: a, cotangent), tp)
    gather_normed.near_pairs()
    normed = gather_normed.far(order)

    act, slope = order(mlp_hidden, normed, inward_weight, b_in.astype(f32)[None])
    gather_grad.forward(order)
    qkv = order(project_qkv, normed, w3, b_qkv.astype(f32), cosine, sine)
    gather_grad.near(order)
    gather_grad.near_pairs()
    mlp_part = order(tokens_by_weight, act, outward_weight)
    grad = gather_grad.far(order)
    mlp_part, dense_ready, _ = lax.optimization_barrier((mlp_part, dense_weight, grad))
    mlp_tok = lax.psum_scatter(mlp_part.reshape(seqs, length, width), "tp", scatter_dimension=1, tiled=True)
    dense_full = lax.all_gather(dense_ready, "tp", axis=0, tiled=True)

    row_sum = lambda parts: [RowSum(part, rows) for part in parts]
    o0, o1 = row_sum(order(lambda a, b: weight_grad(a, b, 2), act, grad))
    hidden_grad, attended_grad, in_bias = order(grad_in, grad, outward_weight, dense_weight, slope)
    i0, i1, i2 = row_sum(order(lambda a, b: weight_grad_rows(a, b, (2, 1, 1)), normed, hidden_grad))
    o0.fold(order)
    both = lambda *a: attention_both(*a, span, tp)
    attended, by_owner, dqkv = order(both, start, qkv, attended_grad, cosine, sine)
    mine = lax.all_to_all(by_owner, "tp", split_axis=0, concat_axis=0, tiled=True)
    o1.fold(order)
    o0.fold(order)
    back = lambda *a: normed_grad(*a, shift[None])
    part, qkv_bias, norm_sums = order(back, hidden_grad, dqkv, inward_weight, w3, normed)
    back_tok = lax.psum_scatter(part.reshape(seqs, length, width), "tp", scatter_dimension=1, tiled=True)
    i0.fold(order)
    o1.fold(order)
    qs, ks, vs = row_sum(order(weight_grad_parts, normed, dqkv))
    i1.fold(order)
    i0.fold(order)
    (ds,) = row_sum(order(lambda a, b: weight_grad(a, b, 1), attended, grad))

    units = in_bias.shape[1]
    cols = width // tp

    def column_sums(grad):
        mine = lax.dynamic_slice_in_dim(grad, lax.axis_index("tp") * cols, cols, 1)
        return jnp.sum(mine.astype(f32), axis=0)

    out_bias = order(column_sums, grad)
    i2.fold(order)
    out_grad = finish_rows([o0, o1], order, weight=FINISH_WEIGHT)
    qs.fold(order)
    i1.fold(order)

    def branch_sums(attention, mlp_tok, tokens):
        values = tokens.astype(f32)
        mlp = mlp_tok.astype(f32) + b_out.astype(f32)
        total = values + attention.reshape(values.shape) + mlp
        squares = jnp.stack([jnp.sum(a * a) for a in (values, attention, mlp, total)])
        return total.astype(bf16), squares

    own = order(project_own, mine, dense_full, b_dense.astype(f32)[None])
    layer_out, squares = order(branch_sums, own, mlp_tok, tokens)
    pad = jnp.zeros((124,), f32)
    packed = jnp.concatenate([norm_sums[0] / gain, norm_sums[1], squares, pad]).reshape(-1, 128)
    packed = TpSum(packed, tp)
    i2.fold(order)
    ks.fold(order)
    packed.fold(order)
    qs.fold(order)
    packed.fold(order)
    vs.fold(order)
    small = jnp.concatenate([in_bias[0], qkv_bias[:, 0].reshape(-1), out_bias]).reshape(-1, 128)
    small = RowSum(jnp.concatenate([packed.result(order), small]), rows)
    ks.fold(order)
    ds.fold(order)
    in_grad = finish_rows([i0, i1, i2], order)
    small.fold(order)
    vs.fold(order)
    ds.fold(order)

    def norm_back(back_tok, tokens, cotangent):
        values = tokens.astype(f32)
        center = values - jnp.mean(values, axis=-1, keepdims=True)
        inverse = lax.rsqrt(jnp.mean(center * center, axis=-1, keepdims=True) + epsilon)
        unit = center * inverse
        unit_grad = back_tok.astype(f32) * gain
        mean_grad = jnp.mean(unit_grad, axis=-1, keepdims=True)
        mean_both = jnp.mean(unit_grad * unit, axis=-1, keepdims=True)
        value_grad = (unit_grad - mean_grad - unit * mean_both) * inverse
        return (cotangent.astype(f32) + value_grad).astype(bf16)

    input_grad = order(norm_back, back_tok, tokens, cotangent)
    small.fold(order)
    qkv_grad = jnp.stack([a.result() for a in (qs, ks, vs)], axis=1)
    dense_grad = finish_rows([ds], order)
    small = small.result().reshape(-1)
    slice_at = lambda a: lax.dynamic_slice_in_dim(a, lax.axis_index("tp") * cols, cols, 0)
    gain_grad, shift_grad = slice_at(small[:width]), slice_at(small[width : 2 * width])
    rms_values = jnp.sqrt(small[2 * width : 2 * width + 4] / (seqs * rows * length * width))
    small = small[2 * width + 128 :]
    in_bias_grad = small[:units]
    qkv_bias_grad = small[units : units + 3 * local].reshape(3, local)
    out_bias_grad = small[units + 3 * local :]

    return (
        layer_out,
        input_grad,
        gain_grad,
        shift_grad,
        qkv_grad,
        qkv_bias_grad,
        dense_grad,
        out_bias_grad,
        in_grad,
        in_bias_grad,
        out_grad,
        out_bias_grad,
        rms_values,
    )


def solution(mesh):
    in_specs = (
        P("rows", "tp", None),
        P("rows", None),
        P("rows", None),
        P(),
        P(),
        P(None, None, "tp"),
        P(None, "tp"),
        P("tp", None),
        P(),
        P(None, "tp"),
        P("tp"),
        P("tp", None),
        P(),
        P("rows", "tp", None),
    )
    out_specs = (
        P("rows", "tp", None),
        P("rows", "tp", None),
        P("tp"),
        P("tp"),
        P(None, None, "tp"),
        P(None, "tp"),
        P("tp", None),
        P("tp"),
        P(None, "tp"),
        P("tp"),
        P("tp", None),
        P("tp"),
        P(),
    )
    return jax.shard_map(body, mesh=mesh, in_specs=in_specs, out_specs=out_specs, check_vma=False)
```

```python
import functools

import jax
import jax.numpy as jnp
from jax import lax
from jax.experimental import pallas as pl
from jax.experimental.pallas import tpu as pltpu
from jax.sharding import PartitionSpec as P

HD = 64
ROT = 32
epsilon = 1e-05
big_negative = -1e30
rope_base = 10000.0
f32 = jnp.float32
bf16 = jnp.bfloat16
VMEM_LIMIT = 56 << 20
ORDER_WEIGHT = int(1.85e11)
EARLY_WEIGHT = 1


def dot(a, b, ca, cb):
    return lax.dot_general(a, b, (((ca,), (cb,)), ((), ())), preferred_element_type=f32)


SMALL = pl.CostEstimate(flops=1, bytes_accessed=1, transcendentals=0)


def params():
    return pltpu.CompilerParams(vmem_limit_bytes=VMEM_LIMIT)


class Order:
    def __init__(self):
        self.last = ()

    def __call__(self, op, *operands):
        operands, _ = lax.optimization_barrier((operands, self.last))
        result = op(*operands)
        self.last = jax.tree.leaves(result)
        return result


def rope_swap(x):
    width = x.shape[-1]
    lane = lax.broadcasted_iota(jnp.int32, (1, width), 1) % HD
    up = pltpu.roll(x, width - ROT // 2, 1)
    down = pltpu.roll(x, ROT // 2, 1)
    return jnp.where(lane < ROT // 2, up, -down)


def norm_kernel(x_ref, gain_ref, shift_ref, first_ref, second_ref, *, per):
    x = x_ref[...].astype(f32)
    center = x - jnp.mean(x, axis=-1, keepdims=True)
    inverse = lax.rsqrt(jnp.mean(center * center, axis=-1, keepdims=True) + epsilon)
    out = (center * inverse * gain_ref[...] + shift_ref[...]).astype(bf16)

    @pl.when(pl.program_id(0) < per)
    def _():
        first_ref[...] = out

    @pl.when(pl.program_id(0) >= per)
    def _():
        second_ref[...] = out


def norm_halves(x, gain, shift, tm=128):
    n, width = x.shape
    per = n // 2 // tm
    vector = pl.BlockSpec((1, width), lambda i: (0, 0))
    return pl.pallas_call(
        functools.partial(norm_kernel, per=per),
        grid=(2 * per,),
        in_specs=[pl.BlockSpec((tm, width), lambda i: (i, 0)), vector, vector],
        out_specs=[
            pl.BlockSpec((tm, width), lambda i: (jnp.minimum(i, per - 1), 0)),
            pl.BlockSpec((tm, width), lambda i: (jnp.maximum(i - per, 0), 0)),
        ],
        out_shape=[jax.ShapeDtypeStruct((n // 2, width), bf16)] * 2,
        compiler_params=params(),
        cost_estimate=SMALL,
        name="norm_halves",
    )(x, gain[None], shift[None])


def table_kernel(place_ref, frequency_ref, c_ref, s_ref):
    angle = place_ref[...].astype(f32) * frequency_ref[...]
    lane = lax.broadcasted_iota(jnp.int32, angle.shape, 1) % HD
    turned = lane < ROT
    c_ref[...] = jnp.where(turned, jnp.cos(angle), 1.0)
    s_ref[...] = jnp.where(turned, jnp.sin(angle), 0.0)


def rope_tables(place, tile, tm=1024):
    n = place.shape[0]
    lane = jnp.arange(tile, dtype=jnp.int32) % (ROT // 2)
    frequency = (rope_base ** (-2.0 * lane.astype(f32) / ROT))[None]
    table = pl.BlockSpec((tm, tile), lambda i: (i, 0))
    return pl.pallas_call(
        table_kernel,
        grid=(n // tm,),
        in_specs=[pl.BlockSpec((tm, 1), lambda i: (i, 0)), pl.BlockSpec((1, tile), lambda i: (0, 0))],
        out_specs=[table, table],
        out_shape=[jax.ShapeDtypeStruct((n, tile), f32)] * 2,
        compiler_params=params(),
        cost_estimate=SMALL,
        name="rope_tables",
    )(place, frequency)


def qkv_kernel(x_ref, w_ref, b_ref, c_ref, s_ref, o_ref):
    x = x_ref[...]
    tile = c_ref.shape[-1]
    local = w_ref.shape[-1]
    cosine, sine = c_ref[...], s_ref[...]
    for part in range(3):
        full = dot(x, w_ref[part], 1, 0) + b_ref[part : part + 1, :]
        for at in range(0, local, tile):
            piece = full[:, at : at + tile]
            if part < 2:
                piece = piece * cosine - rope_swap(piece) * sine
            if part == 0:
                piece = piece * (HD**-0.5)
            o_ref[part, :, at : at + tile] = piece.astype(bf16)


def project_qkv(x, w3, bias, cosine, sine, tm=512):
    n, width = x.shape
    local = w3.shape[2]
    tile = cosine.shape[1]
    return pl.pallas_call(
        qkv_kernel,
        grid=(n // tm,),
        in_specs=[
            pl.BlockSpec((tm, width), lambda i: (i, 0)),
            pl.BlockSpec((3, width, local), lambda i: (0, 0, 0)),
            pl.BlockSpec((3, local), lambda i: (0, 0)),
            pl.BlockSpec((tm, tile), lambda i: (i, 0)),
            pl.BlockSpec((tm, tile), lambda i: (i, 0)),
        ],
        out_specs=pl.BlockSpec((3, tm, local), lambda i: (0, i, 0)),
        out_shape=jax.ShapeDtypeStruct((3, n, local), bf16),
        compiler_params=params(),
        cost_estimate=SMALL,
        name="qkv_rope",
    )(x, w3, bias, cosine, sine)


def chosen_kernel(me_ref, *refs, held):
    x_ref, w_ref, b_ref, act_ref, slope_ref = refs[held:]
    seqs, here, width = x_ref.shape
    x = x_ref[...].reshape(seqs * here, width)
    units = w_ref.shape[1]
    step = min(256, units)
    for at in range(0, units, step):
        cut = slice(at, at + step)
        h = dot(x, w_ref[:, cut], 1, 0) + b_ref[:, cut]
        square = h * h
        t = jnp.tanh(h * (0.7978845608028654 + 0.035677408136300125 * square))
        half = 0.5 + 0.5 * t
        act = h * half
        slope = half + (act - act * half) * (1.5957691216057308 + 0.21406444881780074 * square)
        act_ref[:, :, cut] = act.astype(bf16).reshape(seqs, here, step)
        slope_ref[:, :, cut] = slope.astype(bf16).reshape(seqs, here, step)


def mlp_hidden_of(x, w, bias, steps, before=()):
    seqs, owners, here, width = x.shape
    units = w.shape[1]
    held = len(before)

    def device(j, me):
        chosen = me[0] ^ steps[0]
        for i in range(1, len(steps)):
            chosen = jnp.where(j == i, me[0] ^ steps[i], chosen)
        return 0, chosen, 0, 0

    out = pl.BlockSpec((seqs, None, here, units), device)
    me = lax.axis_index("tp").astype(jnp.int32).reshape(1)
    return pl.pallas_call(
        functools.partial(chosen_kernel, held=held),
        grid_spec=pltpu.PrefetchScalarGridSpec(
            num_scalar_prefetch=1,
            grid=(len(steps),),
            in_specs=[pl.BlockSpec(memory_space=pl.ANY)] * held
            + [
                pl.BlockSpec((seqs, None, here, width), device),
                pl.BlockSpec((width, units), lambda j, me: (0, 0)),
                pl.BlockSpec((1, units), lambda j, me: (0, 0)),
            ],
            out_specs=[out, out],
        ),
        out_shape=[jax.ShapeDtypeStruct((seqs, owners, here, units), bf16)] * 2,
        input_output_aliases={1 + i: i for i in range(held)},
        compiler_params=params(),
        cost_estimate=SMALL,
        name="mlp_hidden_of",
    )(me, *before, x, w, bias)


def grad_in_kernel(g_ref, wo_ref, wd_ref, slope_ref, hg_ref, at_ref, sum_ref):
    g = g_ref[...]
    units = wo_ref.shape[0]
    step = min(256, units)

    @pl.when(pl.program_id(0) == 0)
    def _():
        sum_ref[...] = jnp.zeros_like(sum_ref)

    for at in range(0, units, step):
        slope = slope_ref[:, at : at + step].astype(f32)
        hg = (dot(g, wo_ref[at : at + step, :], 1, 1) * slope).astype(bf16)
        hg_ref[:, at : at + step] = hg
        sum_ref[0:1, at : at + step] += jnp.sum(hg.astype(f32), axis=0, keepdims=True)
    at_ref[...] = dot(g, wd_ref[...], 1, 1).astype(bf16)


def grad_in(g, wo, wd, slope, tm=512):
    n, width = g.shape
    units, local = wo.shape[0], wd.shape[0]
    return pl.pallas_call(
        grad_in_kernel,
        grid=(n // tm,),
        in_specs=[
            pl.BlockSpec((tm, width), lambda i: (i, 0)),
            pl.BlockSpec((units, width), lambda i: (0, 0)),
            pl.BlockSpec((local, width), lambda i: (0, 0)),
            pl.BlockSpec((tm, units), lambda i: (i, 0)),
        ],
        out_specs=[
            pl.BlockSpec((tm, units), lambda i: (i, 0)),
            pl.BlockSpec((tm, local), lambda i: (i, 0)),
            pl.BlockSpec((8, units), lambda i: (0, 0)),
        ],
        out_shape=[
            jax.ShapeDtypeStruct((n, units), bf16),
            jax.ShapeDtypeStruct((n, local), bf16),
            jax.ShapeDtypeStruct((8, units), f32),
        ],
        compiler_params=params(),
        cost_estimate=SMALL,
        name="grad_in",
    )(g, wo, wd, slope)


def tokens_kernel(x_ref, w_ref, o_ref):
    width = w_ref.shape[1]
    step = min(512, width)
    for at in range(0, width, step):
        o_ref[:, at : at + step] = dot(x_ref[...], w_ref[:, at : at + step], 1, 0).astype(o_ref.dtype)


def tokens_by_weight(x, w, share, shares, tm=512):
    n, depth = x.shape
    n //= shares
    width = w.shape[1]
    first = share * (n // tm)
    return pl.pallas_call(
        tokens_kernel,
        grid=(n // tm,),
        in_specs=[pl.BlockSpec((tm, depth), lambda i: (first + i, 0)), pl.BlockSpec((depth, width), lambda i: (0, 0))],
        out_specs=pl.BlockSpec((tm, width), lambda i: (i, 0)),
        out_shape=jax.ShapeDtypeStruct((n, width), bf16),
        compiler_params=params(),
        cost_estimate=SMALL,
        name="tokens_by_weight",
    )(x, w)


def weight_grad_kernel(a_ref, b_ref, o_ref):
    o_ref[...] = dot(a_ref[...], b_ref[...], 0, 0).astype(bf16)


def weight_grad(a, b, share=0, shares=1, tile=512, weight=1):
    n, rows = a.shape
    rows //= shares
    cols = b.shape[1]
    tile = min(tile, cols)
    return pl.pallas_call(
        weight_grad_kernel,
        grid=(cols // tile,),
        in_specs=[
            pl.BlockSpec((n, rows), lambda j: (0, share), pipeline_mode=pl.Buffered(1)),
            pl.BlockSpec((n, tile), lambda j: (0, j)),
        ],
        out_specs=pl.BlockSpec((rows, tile), lambda j: (0, j)),
        out_shape=jax.ShapeDtypeStruct((rows, cols), bf16),
        compiler_params=params(),
        cost_estimate=pl.CostEstimate(flops=int(weight), bytes_accessed=1, transcendentals=0),
        name="weight_grad",
    )(a, b)


def weight_grad_rows_kernel(a_ref, b_ref, *o_refs, counts):
    full = dot(a_ref[...], b_ref[...], 0, 0).astype(bf16)
    step = pl.program_id(0)
    first = 0
    for o_ref, count in zip(o_refs, counts):

        @pl.when((step >= first) & (step < first + count))
        def _(o_ref=o_ref):
            o_ref[...] = full

        first += count


def weight_grad_rows(a, b, shares, tile=512):
    n, rows = a.shape
    cols = b.shape[1]
    counts = [rows * share // sum(shares) // tile for share in shares]
    firsts = [sum(counts[:i]) for i in range(len(counts))]
    out = lambda i: pl.BlockSpec((tile, cols), lambda j: (jnp.clip(j - firsts[i], 0, counts[i] - 1), 0))
    return pl.pallas_call(
        functools.partial(weight_grad_rows_kernel, counts=counts),
        grid=(rows // tile,),
        in_specs=[
            pl.BlockSpec((n, tile), lambda j: (0, j)),
            pl.BlockSpec((n, cols), lambda j: (0, 0), pipeline_mode=pl.Buffered(1)),
        ],
        out_specs=[out(i) for i in range(len(counts))],
        out_shape=[jax.ShapeDtypeStruct((count * tile, cols), bf16) for count in counts],
        compiler_params=params(),
        cost_estimate=SMALL,
        name="weight_grad_rows",
    )(a, b)


def weight_grad_parts_kernel(a_ref, b_ref, first_ref, last_ref):
    for part in range(2):
        first_ref[part] = dot(a_ref[...], b_ref[part], 0, 0).astype(bf16)
    last_ref[...] = dot(a_ref[...], b_ref[2], 0, 0).astype(bf16)


def weight_grad_parts(a, b, tile=512, weight=1):
    n, rows = a.shape
    parts, _, cols = b.shape
    return pl.pallas_call(
        weight_grad_parts_kernel,
        grid=(rows // tile,),
        in_specs=[
            pl.BlockSpec((n, tile), lambda j: (0, j)),
            pl.BlockSpec((parts, n, cols), lambda j: (0, 0, 0), pipeline_mode=pl.Buffered(1)),
        ],
        out_specs=[pl.BlockSpec((2, tile, cols), lambda j: (0, j, 0)), pl.BlockSpec((tile, cols), lambda j: (j, 0))],
        out_shape=[jax.ShapeDtypeStruct((2, rows, cols), bf16), jax.ShapeDtypeStruct((rows, cols), bf16)],
        compiler_params=params(),
        cost_estimate=pl.CostEstimate(flops=int(weight), bytes_accessed=1, transcendentals=0),
        name="weight_grad_parts",
    )(a, b)


def normed_grad_kernel(*refs, held):
    hg_ref, dq_ref, wi_ref, w3_ref, x_ref, shift_ref, o_ref, sum_ref, norm_ref = refs[held:]

    @pl.when(pl.program_id(0) == 0)
    def _():
        sum_ref[...] = jnp.zeros_like(sum_ref)
        norm_ref[...] = jnp.zeros_like(norm_ref)

    for part in range(3):
        sum_ref[part, 0:1] += jnp.sum(dq_ref[part].astype(f32), axis=0, keepdims=True)
    width = o_ref.shape[1]
    step = min(512, width)
    for at in range(0, width, step):
        cut = slice(at, at + step)
        total = dot(hg_ref[...], wi_ref[cut, :], 1, 1)
        for part in range(3):
            total += dot(dq_ref[part], w3_ref[part, cut, :], 1, 1)
        o_ref[:, cut] = total.astype(bf16)
        scaled = x_ref[:, cut].astype(f32) - shift_ref[:, cut]
        norm_ref[0:1, cut] += jnp.sum(total * scaled, axis=0, keepdims=True)
        norm_ref[1:2, cut] += jnp.sum(total, axis=0, keepdims=True)


def normed_grad(hg, dqkv, wi, w3, x, shift, share, shares, before=(), tm=512):
    n, units = hg.shape
    held = len(before)
    steps = n // shares // tm
    first = share * steps
    width, local = w3.shape[1:]
    return pl.pallas_call(
        functools.partial(normed_grad_kernel, held=held),
        grid=(steps,),
        in_specs=[pl.BlockSpec(memory_space=pl.ANY)] * held
        + [
            pl.BlockSpec((tm, units), lambda i: (first + i, 0)),
            pl.BlockSpec((3, tm, local), lambda i: (0, first + i, 0)),
            pl.BlockSpec((width, units), lambda i: (0, 0)),
            pl.BlockSpec((3, width, local), lambda i: (0, 0, 0)),
            pl.BlockSpec((tm, width), lambda i: (first + i, 0)),
            pl.BlockSpec((1, width), lambda i: (0, 0)),
        ],
        out_specs=[
            pl.BlockSpec((tm, width), lambda i: (first + i, 0)),
            pl.BlockSpec((3, 8, local), lambda i: (0, 0, 0)),
            pl.BlockSpec((8, width), lambda i: (0, 0)),
        ],
        out_shape=[
            jax.ShapeDtypeStruct((n, width), bf16),
            jax.ShapeDtypeStruct((3, 8, local), f32),
            jax.ShapeDtypeStruct((8, width), f32),
        ],
        input_output_aliases={i: i for i in range(held)},
        compiler_params=params(),
        cost_estimate=SMALL,
        name="normed_grad",
    )(*before, hg, dqkv, wi, w3, x, shift)


def attention_kernel(*refs, bq, held):
    start_ref, q_ref, k_ref, v_ref, do_ref, c_ref, s_ref, o_ref, by_owner_ref, g_ref, dk_acc, dv_acc = refs[held:]
    span, width = q_ref.shape
    lane = lax.broadcasted_iota(jnp.int32, (1, width), 1) // HD
    zero = jnp.zeros((), bf16)

    def turn_back(x, at, n):
        return x * c_ref[at : at + n, :] + rope_swap(x) * s_ref[at : at + n, :]

    for block in range(span // bq):
        at = block * bq
        n = at + bq
        qb = q_ref[at:n, :]
        gb = do_ref[at:n, :]
        keys, vals = k_ref[0:n, :], v_ref[0:n, :]
        key = lax.broadcasted_iota(jnp.int32, (bq, n), 1)
        row = lax.broadcasted_iota(jnp.int32, (bq, n), 0) + at
        allowed = (key >= start_ref[at:n, :]) & (key <= row)
        out = jnp.zeros((bq, width), f32)
        dq = jnp.zeros((bq, width), f32)
        dk = jnp.zeros((n, width), f32)
        dv = jnp.zeros((n, width), f32)
        for head in range(width // HD):
            mine = lane == head
            qh, gh = jnp.where(mine, qb, zero), jnp.where(mine, gb, zero)
            kh, vh = jnp.where(mine, keys, zero), jnp.where(mine, vals, zero)
            scores = jnp.where(allowed, dot(qh, keys, 1, 1), big_negative)
            expd = jnp.exp(scores - jnp.max(scores, axis=1, keepdims=True))
            probs = expd * (1.0 / jnp.sum(expd, axis=1, keepdims=True))
            low = probs.astype(bf16)
            out = out + dot(low, vh, 1, 0)
            prob_grad = dot(gh, vals, 1, 1)
            inner = jnp.sum(probs * prob_grad, axis=1, keepdims=True)
            score_grad = (probs * (prob_grad - inner)).astype(bf16)
            dq = dq + dot(score_grad, kh, 1, 0)
            dk = dk + dot(score_grad, qh, 0, 0)
            dv = dv + dot(low, gh, 0, 0)
        out = out.astype(bf16)
        o_ref[at:n, :] = out
        here = by_owner_ref.shape[1]
        for own in range(bq // here):
            by_owner_ref[at // here + own] = out[own * here : (own + 1) * here]
        g_ref[0, at:n, :] = turn_back(dq * (HD**-0.5), at, bq).astype(bf16)
        if block:
            dk_acc[0:at, :] += dk[0:at]
            dv_acc[0:at, :] += dv[0:at]
        dk_acc[at:n, :] = dk[at:n]
        dv_acc[at:n, :] = dv[at:n]
    g_ref[1] = turn_back(dk_acc[...], 0, span).astype(bf16)
    g_ref[2] = dv_acc[...].astype(bf16)


def attention_both(start, qkv, grad, cosine, sine, span, owners, row, before=(), bq=512):
    n, local = grad.shape
    here = 2 * span // owners
    width = cosine.shape[1]
    bq = min(bq, span)
    held = len(before)
    first = 2 * row
    part = lambda which: pl.BlockSpec((None, span, width), lambda t, p: (which, first + t, p))
    table = pl.BlockSpec((span, width), lambda t, p: (first + t, 0))
    return pl.pallas_call(
        functools.partial(attention_kernel, bq=bq, held=held),
        grid=(2, local // width),
        in_specs=[pl.BlockSpec(memory_space=pl.ANY)] * held
        + [
            pl.BlockSpec((span, 1), lambda t, p: (first + t, 0)),
            part(0),
            part(1),
            part(2),
            pl.BlockSpec((span, width), lambda t, p: (first + t, p)),
            table,
            table,
        ],
        out_specs=[
            pl.BlockSpec((span, width), lambda t, p: (first + t, p)),
            pl.BlockSpec((owners // 2, None, here, width), lambda t, p: (t, row, 0, p)),
            pl.BlockSpec((3, span, width), lambda t, p: (0, first + t, p)),
        ],
        out_shape=[
            jax.ShapeDtypeStruct((n, local), bf16),
            jax.ShapeDtypeStruct((owners, n // (2 * span), here, local), bf16),
            jax.ShapeDtypeStruct((3, n, local), bf16),
        ],
        scratch_shapes=[pltpu.VMEM((span, width), f32)] * 2,
        input_output_aliases={i: i for i in range(held)},
        compiler_params=params(),
        cost_estimate=SMALL,
        name="attention_both",
    )(*before, start, qkv, qkv, qkv, grad, cosine, sine)


def own_kernel(x_ref, w_ref, bd_ref, bo_ref, token_ref, *refs):
    *mlp_refs, o_ref, sum_ref = refs
    owners, seqs, here, local = x_ref.shape
    attention = jnp.zeros((seqs * here, w_ref.shape[1]), f32) + bd_ref[...]
    for owner in range(owners):
        x = x_ref[owner].reshape(seqs * here, local)
        attention += dot(x, w_ref[owner * local : (owner + 1) * local, :], 1, 0)
    tokens = token_ref[...].astype(f32)
    mlp = jnp.concatenate([a[...] for a in mlp_refs], axis=0).astype(f32) + bo_ref[...]
    total = tokens + attention + mlp
    o_ref[...] = total.astype(bf16)

    @pl.when(pl.program_id(0) == 0)
    def _():
        sum_ref[...] = jnp.zeros_like(sum_ref)

    for i, a in enumerate((tokens, attention, mlp, total)):
        sum_ref[i : i + 1, :] += jnp.sum(a * a, axis=0, keepdims=True)


def project_own(x, w, bd, bo, tokens, mlp_parts, tile=512):
    owners, seqs, here, local = x.shape
    width = w.shape[1]
    rows = seqs * here
    column = lambda high: pl.BlockSpec((high, tile), lambda j: (0, j))
    return pl.pallas_call(
        own_kernel,
        grid=(width // tile,),
        in_specs=[
            pl.BlockSpec(x.shape, lambda j: (0, 0, 0, 0)),
            column(owners * local),
            column(1),
            column(1),
            column(rows),
        ]
        + [column(a.shape[0]) for a in mlp_parts],
        out_specs=[column(rows), pl.BlockSpec((8, tile), lambda j: (0, 0))],
        out_shape=[jax.ShapeDtypeStruct((rows, width), bf16), jax.ShapeDtypeStruct((8, tile), f32)],
        compiler_params=params(),
        cost_estimate=SMALL,
        name="project_own",
    )(x, w, bd, bo, tokens, *mlp_parts)


def line_ok(size):
    return size >= 4 and size & (size - 1) == 0


class RowSum:
    def __init__(self, part, size):
        self.part, self.size, self.axis = part, size, "rows"
        groups = range(0, size, 4)
        pairs = lambda *ends: [(g + a, g + b) for g in groups for a, b in ends]
        self.hops = [pairs((0, 1), (3, 2)), pairs((1, 2), (2, 1))]
        hop = 4
        while hop < size:
            self.hops.append([(i, i ^ hop) for i in range(size)])
            hop *= 2
        self.hops.append(pairs((1, 0), (2, 3)))
        self.send()

    def send(self):
        if line_ok(self.size):
            self.came = lax.ppermute(self.part, self.axis, self.hops.pop(0))

    def fold(self, order):
        if line_ok(self.size) and self.hops:
            add = lambda a, b: (a.astype(f32) + b.astype(f32)).astype(a.dtype)
            self.part = order(add, self.part, self.came)
            self.send()

    def complete(self, order):
        while self.hops:
            self.fold(order)

    def result(self, order=None):
        if not line_ok(self.size):
            return lax.psum(self.part.astype(f32), "rows")
        self.complete(order or Order())
        place = lax.axis_index("rows") % 4
        return jnp.where((place == 1) | (place == 2), self.part, self.came).astype(f32)


def finish_kernel(inner_ref, kept_ref, came_ref, *refs):
    o_ref = refs[-1]

    @pl.when(inner_ref[0] == 1)
    def _():
        o_ref[...] = kept_ref[...].astype(f32)

    @pl.when(inner_ref[0] == 0)
    def _():
        o_ref[...] = came_ref[...].astype(f32)


def finish(total, order, high, first=0, before=None, tile=512):
    flat = lambda a: a.reshape(-1, a.shape[-1])
    rows, cols = flat(total.part).shape
    if not line_ok(total.size):
        before = jnp.zeros((high, cols), f32) if before is None else before
        return lax.dynamic_update_slice(before, flat(total.result()), (first, 0))
    total.complete(order)
    tile = min(tile, rows)
    held = [] if before is None else [before]
    block = pl.BlockSpec((tile, cols), lambda j: (j, 0))
    place = lax.axis_index("rows") % 4
    inner = ((place == 1) | (place == 2)).astype(jnp.int32).reshape(1)
    call = pl.pallas_call(
        finish_kernel,
        grid=(rows // tile,),
        in_specs=[pl.BlockSpec(memory_space=pltpu.SMEM), block, block] + [pl.BlockSpec(memory_space=pl.ANY)] * len(held),
        out_specs=pl.BlockSpec((tile, cols), lambda j: (first // tile + j, 0)),
        out_shape=jax.ShapeDtypeStruct((high, cols), f32),
        input_output_aliases={3: 0} if held else {},
        compiler_params=params(),
        cost_estimate=SMALL,
        name="finish",
    )
    return order(lambda *a: call(inner, *a), flat(total.part), flat(total.came), *held)


class Gather:
    core, x, y = 1, 2, 4

    def __init__(self, first, second, size):
        self.first, self.second, self.size = first, second, size
        self.x0, self.y1 = self.send(first, self.x), self.send(second, self.y)

    def send(self, a, step):
        return lax.ppermute(a, "tp", [(i, i ^ step) for i in range(self.size)])

    def others(self, order=None):
        first, second = self.first, self.second
        if order:
            first, second = order(lambda a, b: (a, b), first, second)
        self.x1, self.y0 = self.send(second, self.x), self.send(first, self.y)
        self.c0 = self.send(first, self.core)

    def forward(self, order):
        came = (self.x0, self.y1, self.c0, self.second)
        self.x0, self.y1, self.c0, self.second = order(lambda *a: a, *came)
        self.c1 = self.send(self.second, self.core)
        self.d0, self.d1 = self.send(self.x0, self.y), self.send(self.y1, self.x)

    def pairs(self, order):
        came = (self.x0, self.y1, self.x1, self.y0, self.c1)
        self.x0, self.y1, self.x1, self.y0, self.c1 = order(lambda *a: a, *came)
        self.px0, self.py1 = self.send(self.x0, self.core), self.send(self.y1, self.core)
        self.px1, self.py0 = self.send(self.x1, self.core), self.send(self.y0, self.core)

    def near(self, order):
        steps = [step for step in (0, self.core, self.x, self.y, self.x | self.core, self.y | self.core) for _ in range(2)]
        pieces = (self.first, self.second, self.c0, self.c1, self.x0, self.x1, self.y0, self.y1)
        pieces += (self.px0, self.px1, self.py0, self.py1)
        self.full = order(lambda *a: place_pieces(None, a, steps, (0, 1) * 6, self.size), *pieces)

    def far_pairs(self, order):
        self.d0, self.d1 = order(lambda a, b: (a, b), self.d0, self.d1)
        self.pd0, self.pd1 = self.send(self.d0, self.core), self.send(self.d1, self.core)

    def far(self, order):
        far = self.x | self.y
        steps = (far, far, far | self.core, far | self.core)
        place = lambda full, *a: place_pieces(full, a, steps, (0, 1, 0, 1), self.size)
        self.full = order(place, self.full, self.d0, self.d1, self.pd0, self.pd1)
        return self.full


def place_kernel(me_ref, *refs, held):
    pieces, o_ref = refs[held:-1], refs[-1]
    for i, piece in enumerate(pieces):

        @pl.when(pl.program_id(0) == i)
        def _(piece=piece):
            o_ref[...] = piece[...].reshape(o_ref.shape)


def place_pieces(full, pieces, steps, halves, size):
    held = 0 if full is None else 1
    here, width = pieces[0].shape

    def target(j, me):
        device, half = me[0] ^ steps[0], halves[0]
        for i in range(1, len(pieces)):
            device = jnp.where(j == i, me[0] ^ steps[i], device)
            half = jnp.where(j == i, halves[i], half)
        return half, device, 0, 0

    hbm = pl.BlockSpec(memory_space=pl.ANY)
    me = lax.axis_index("tp").astype(jnp.int32).reshape(1)
    return pl.pallas_call(
        functools.partial(place_kernel, held=held),
        grid_spec=pltpu.PrefetchScalarGridSpec(
            num_scalar_prefetch=1,
            grid=(len(pieces),),
            in_specs=[hbm] * held + [pl.BlockSpec((here, width), lambda j, me: (0, 0))] * len(pieces),
            out_specs=pl.BlockSpec((1, None, here, width), target),
        ),
        out_shape=jax.ShapeDtypeStruct((2, size, here, width), bf16),
        input_output_aliases={1: 0} if held else {},
        compiler_params=params(),
        cost_estimate=SMALL,
        name="place_pieces",
    )(me, *([full] if held else []), *pieces)


class TpSum:
    def __init__(self, part, size):
        self.part, self.size, self.hop = part, size, 1
        self.send()

    def send(self):
        if self.size & (self.size - 1) == 0 and self.hop < self.size:
            self.came = lax.ppermute(self.part, "tp", [(i, i ^ self.hop) for i in range(self.size)])

    def fold(self, order):
        if self.size & (self.size - 1):
            self.part, self.size = lax.psum(self.part, "tp"), 1
        elif self.hop < self.size:
            self.part = order(lambda a, b: a + b, self.part, self.came)
            self.hop *= 2
            self.send()

    def result(self, order):
        while self.hop < self.size:
            self.fold(order)
        return self.part


def body(
    tokens,
    segment_ids,
    positions,
    norm_gain,
    norm_shift,
    query_key_value_weight,
    b_qkv,
    dense_weight,
    b_dense,
    inward_weight,
    b_in,
    outward_weight,
    b_out,
    cotangent,
):
    rows, tp = lax.axis_size("rows"), lax.axis_size("tp")
    seqs, here, width = tokens.shape
    length = here * tp
    n = seqs * length
    local = query_key_value_weight.shape[2]
    tile = min(128, local)
    span = length // 2

    exchange = tp == 8 and seqs == 2

    order = Order()
    gain, shift = norm_gain.astype(f32), norm_shift.astype(f32)
    norm = lambda a: norm_halves(a.reshape(seqs * here, width), gain, shift)
    halves = order(norm, tokens)

    if exchange:
        gather_normed = Gather(*halves, tp)
        gather_normed.others()

    def tables(positions, weight):
        place = positions.reshape(n, 1)
        cosine, sine = rope_tables(place, tile)
        start = jnp.arange(n, dtype=jnp.int32)[:, None] % span - place
        return cosine, sine, start, jnp.transpose(weight, (1, 0, 2))

    cosine, sine, start, w3 = order(tables, positions, query_key_value_weight)
    in_bias_row = b_in.astype(f32)[None]
    token_rows = lambda a: a.reshape(n, a.shape[-1])
    later = lambda a: lax.all_gather(order(lambda b: b, a), "tp", axis=1, tiled=True).reshape(n, width)
    if exchange:
        gather_normed.forward(order)
        gather_normed.pairs(order)
        grad = later(cotangent)
        gather_normed.near(order)
        hidden_of = lambda *a: mlp_hidden_of(*a, tuple(range(6)))
        hidden = order(hidden_of, gather_normed.full, inward_weight, in_bias_row)
        gather_normed.far_pairs(order)
        normed_full = gather_normed.far(order)
        hidden_of = lambda x, w, b, *before: mlp_hidden_of(x, w, b, (6, 7), before)
        act, slope = order(hidden_of, normed_full, inward_weight, in_bias_row, *hidden)
    else:
        normed_full = jnp.concatenate(halves).reshape(seqs, here, width)
        normed_full = lax.all_gather(normed_full, "tp", axis=1).reshape(seqs, tp, here, width)
        grad = later(cotangent)
        hidden_of = lambda *a: mlp_hidden_of(*a, tuple(range(tp)))
        act, slope = order(hidden_of, normed_full, inward_weight, in_bias_row)
    normed, act, slope = token_rows(normed_full), token_rows(act), token_rows(slope)
    qkv = order(project_qkv, normed, w3, b_qkv.astype(f32), cosine, sine)
    mlp_part = order(lambda *a: tokens_by_weight(*a, 0, 1), act, outward_weight).reshape(seqs, length, width)
    mlp_part, dense_ready, _ = lax.optimization_barrier((mlp_part, dense_weight, grad))
    mlp_tok = lax.psum_scatter(mlp_part, "tp", scatter_dimension=1, tiled=True).reshape(seqs * here, width)
    dense_full = lax.all_gather(dense_ready, "tp", axis=0, tiled=True)

    o0 = RowSum(order(lambda *a: weight_grad(*a, 0, 2), act, grad), rows)
    o1 = RowSum(order(lambda *a: weight_grad(*a, 1, 2), act, grad), rows)
    row_sum = lambda parts: [RowSum(part, rows) for part in parts]
    hidden_grad, attended_grad, in_bias = order(grad_in, grad, outward_weight, dense_weight, slope)
    o0.fold(order)
    i0, i1 = row_sum(order(lambda a, b: weight_grad_rows(a, b, (1, 1)), normed, hidden_grad))
    both = lambda row: lambda s, q, g, c, t, *before: attention_both(s, q, g, c, t, span, tp, row, before)
    attended, by_owner, dqkv = order(both(0), start, qkv, attended_grad, cosine, sine)
    o1.fold(order)
    o0.fold(order)
    for row in range(1, seqs):
        kept = (attended, by_owner, dqkv)
        attended, by_owner, dqkv = order(both(row), start, qkv, attended_grad, cosine, sine, *kept)
    mine = lax.all_to_all(by_owner, "tp", split_axis=0, concat_axis=0, tiled=True)
    i0.fold(order)
    o1.fold(order)
    qs, vs = row_sum(order(lambda a, b: weight_grad_parts(a, b, weight=EARLY_WEIGHT), normed, dqkv))
    units = in_bias.shape[1]
    out_grad = finish(o0, order, units)
    back = lambda share: lambda *a: normed_grad(*a[:5], shift[None], share, 2, a[5:])
    part, bias_a, norm_a = order(back(0), hidden_grad, dqkv, inward_weight, w3, normed)
    i1.fold(order)
    i0.fold(order)
    out_grad = finish(o1, order, units, units // 2, out_grad)
    part, bias_b, norm_b = order(back(1), hidden_grad, dqkv, inward_weight, w3, normed, part)
    back_tok = lax.psum_scatter(part.reshape(seqs, length, width), "tp", scatter_dimension=1, tiled=True)
    qs.fold(order)
    i1.fold(order)
    vs.fold(order)
    in_grad = finish(i0, order, width)
    (ds,) = row_sum([order(lambda a, b: weight_grad(a, b, weight=ORDER_WEIGHT), attended, grad)])

    cols = width // tp

    def column_sums(grad):
        mine = lax.dynamic_slice_in_dim(grad, lax.axis_index("tp") * cols, cols, 1)
        return jnp.sum(mine.astype(f32), axis=0)

    out_bias = order(column_sums, grad)
    rows_of = lambda a: a.reshape(seqs * here, width)
    own = lambda x, w, t, *m: project_own(x, w, b_dense.astype(f32)[None], b_out.astype(f32)[None], rows_of(t), m)
    layer_out, squares = order(own, mine, dense_full, tokens, mlp_tok)
    layer_out = layer_out.reshape(tokens.shape)

    def pack(norm_a, norm_b, squares):
        norm_sums = norm_a + norm_b
        squares = jnp.sum(squares[:4], axis=1)
        pad = jnp.zeros((124,), f32)
        return jnp.concatenate([norm_sums[0] / gain, norm_sums[1], squares, pad]).reshape(-1, 128)

    packed = TpSum(order(pack, norm_a, norm_b, squares), tp)
    qs.fold(order)
    packed.fold(order)
    vs.fold(order)
    in_grad = finish(i1, order, width, width // 2, in_grad)
    packed.fold(order)
    ds.fold(order)
    qkv_bias = bias_a + bias_b
    small = jnp.concatenate([in_bias[0], qkv_bias[:, 0].reshape(-1), out_bias]).reshape(-1, 128)
    small = RowSum(jnp.concatenate([packed.result(order), small]), rows)
    qkv_grad = finish(qs, order, 3 * width)
    ds.fold(order)
    small.fold(order)
    qkv_grad = finish(vs, order, 3 * width, 2 * width, qkv_grad)
    small.fold(order)

    def norm_back(back_tok, tokens, cotangent):
        values = tokens.astype(f32)
        center = values - jnp.mean(values, axis=-1, keepdims=True)
        inverse = lax.rsqrt(jnp.mean(center * center, axis=-1, keepdims=True) + epsilon)
        unit = center * inverse
        unit_grad = back_tok.astype(f32) * gain
        mean_grad = jnp.mean(unit_grad, axis=-1, keepdims=True)
        mean_both = jnp.mean(unit_grad * unit, axis=-1, keepdims=True)
        value_grad = (unit_grad - mean_grad - unit * mean_both) * inverse
        return (cotangent.astype(f32) + value_grad).astype(bf16)

    input_grad = order(norm_back, back_tok, tokens, cotangent)
    qkv_grad = jnp.transpose(qkv_grad.reshape(3, width, local), (1, 0, 2))
    dense_grad = finish(ds, order, local)
    small = small.result().reshape(-1)
    slice_at = lambda a: lax.dynamic_slice_in_dim(a, lax.axis_index("tp") * cols, cols, 0)
    gain_grad, shift_grad = slice_at(small[:width]), slice_at(small[width : 2 * width])
    rms_values = jnp.sqrt(small[2 * width : 2 * width + 4] / (seqs * rows * length * width))
    small = small[2 * width + 128 :]
    in_bias_grad = small[:units]
    qkv_bias_grad = small[units : units + 3 * local].reshape(3, local)
    out_bias_grad = small[units + 3 * local :]

    return (
        layer_out,
        input_grad,
        gain_grad,
        shift_grad,
        qkv_grad,
        qkv_bias_grad,
        dense_grad,
        out_bias_grad,
        in_grad,
        in_bias_grad,
        out_grad,
        out_bias_grad,
        rms_values,
    )


def solution(mesh):
    in_specs = (
        P("rows", "tp", None),
        P("rows", None),
        P("rows", None),
        P(),
        P(),
        P(None, None, "tp"),
        P(None, "tp"),
        P("tp", None),
        P(),
        P(None, "tp"),
        P("tp"),
        P("tp", None),
        P(),
        P("rows", "tp", None),
    )
    out_specs = (
        P("rows", "tp", None),
        P("rows", "tp", None),
        P("tp"),
        P("tp"),
        P(None, None, "tp"),
        P(None, "tp"),
        P("tp", None),
        P("tp"),
        P(None, "tp"),
        P("tp"),
        P("tp", None),
        P("tp"),
        P(),
    )
    return jax.shard_map(body, mesh=mesh, in_specs=in_specs, out_specs=out_specs, check_vma=False)
```

```python
import functools

import jax
import jax.numpy as jnp
from jax import lax
from jax.experimental import pallas as pl
from jax.experimental.pallas import tpu as pltpu
from jax.sharding import PartitionSpec as P

HD = 64
ROT = 32
epsilon = 1e-05
big_negative = -1e30
rope_base = 10000.0
f32 = jnp.float32
bf16 = jnp.bfloat16
VMEM_LIMIT = 56 << 20
ORDER_WEIGHT = int(2e11)
EARLY_WEIGHT = int(2.1e11)


def dot(a, b, ca, cb):
    return lax.dot_general(a, b, (((ca,), (cb,)), ((), ())), preferred_element_type=f32)


SMALL = pl.CostEstimate(flops=1, bytes_accessed=1, transcendentals=0)


def params():
    return pltpu.CompilerParams(vmem_limit_bytes=VMEM_LIMIT)


class Order:
    def __init__(self):
        self.last = ()

    def __call__(self, op, *operands):
        operands, _ = lax.optimization_barrier((operands, self.last))
        result = op(*operands)
        self.last = jax.tree.leaves(result)
        return result


def rope_swap(x):
    width = x.shape[-1]
    lane = lax.broadcasted_iota(jnp.int32, (1, width), 1) % HD
    up = pltpu.roll(x, width - ROT // 2, 1)
    down = pltpu.roll(x, ROT // 2, 1)
    return jnp.where(lane < ROT // 2, up, -down)


def norm_kernel(x_ref, gain_ref, shift_ref, first_ref, second_ref, *, per):
    x = x_ref[...].astype(f32)
    center = x - jnp.mean(x, axis=-1, keepdims=True)
    inverse = lax.rsqrt(jnp.mean(center * center, axis=-1, keepdims=True) + epsilon)
    out = (center * inverse * gain_ref[...] + shift_ref[...]).astype(bf16)

    @pl.when(pl.program_id(0) < per)
    def _():
        first_ref[...] = out

    @pl.when(pl.program_id(0) >= per)
    def _():
        second_ref[...] = out


def norm_halves(x, gain, shift, tm=128):
    n, width = x.shape
    per = n // 2 // tm
    vector = pl.BlockSpec((1, width), lambda i: (0, 0))
    return pl.pallas_call(
        functools.partial(norm_kernel, per=per),
        grid=(2 * per,),
        in_specs=[pl.BlockSpec((tm, width), lambda i: (i, 0)), vector, vector],
        out_specs=[
            pl.BlockSpec((tm, width), lambda i: (jnp.minimum(i, per - 1), 0)),
            pl.BlockSpec((tm, width), lambda i: (jnp.maximum(i - per, 0), 0)),
        ],
        out_shape=[jax.ShapeDtypeStruct((n // 2, width), bf16)] * 2,
        compiler_params=params(),
        cost_estimate=SMALL,
        name="norm_halves",
    )(x, gain[None], shift[None])


def table_kernel(place_ref, frequency_ref, c_ref, s_ref):
    angle = place_ref[...].astype(f32) * frequency_ref[...]
    lane = lax.broadcasted_iota(jnp.int32, angle.shape, 1) % HD
    turned = lane < ROT
    c_ref[...] = jnp.where(turned, jnp.cos(angle), 1.0)
    s_ref[...] = jnp.where(turned, jnp.sin(angle), 0.0)


def rope_tables(place, tile, tm=1024):
    n = place.shape[0]
    lane = jnp.arange(tile, dtype=jnp.int32) % (ROT // 2)
    frequency = (rope_base ** (-2.0 * lane.astype(f32) / ROT))[None]
    table = pl.BlockSpec((tm, tile), lambda i: (i, 0))
    return pl.pallas_call(
        table_kernel,
        grid=(n // tm,),
        in_specs=[pl.BlockSpec((tm, 1), lambda i: (i, 0)), pl.BlockSpec((1, tile), lambda i: (0, 0))],
        out_specs=[table, table],
        out_shape=[jax.ShapeDtypeStruct((n, tile), f32)] * 2,
        compiler_params=params(),
        cost_estimate=SMALL,
        name="rope_tables",
    )(place, frequency)


def qkv_kernel(x_ref, w_ref, b_ref, c_ref, s_ref, o_ref):
    x = x_ref[...]
    tile = c_ref.shape[-1]
    local = w_ref.shape[-1]
    cosine, sine = c_ref[...], s_ref[...]
    for part in range(3):
        full = dot(x, w_ref[part], 1, 0) + b_ref[part : part + 1, :]
        for at in range(0, local, tile):
            piece = full[:, at : at + tile]
            if part < 2:
                piece = piece * cosine - rope_swap(piece) * sine
            if part == 0:
                piece = piece * (HD**-0.5)
            o_ref[part, :, at : at + tile] = piece.astype(bf16)


def project_qkv(x, w3, bias, cosine, sine, tm=512):
    n, width = x.shape
    local = w3.shape[2]
    tile = cosine.shape[1]
    return pl.pallas_call(
        qkv_kernel,
        grid=(n // tm,),
        in_specs=[
            pl.BlockSpec((tm, width), lambda i: (i, 0)),
            pl.BlockSpec((3, width, local), lambda i: (0, 0, 0)),
            pl.BlockSpec((3, local), lambda i: (0, 0)),
            pl.BlockSpec((tm, tile), lambda i: (i, 0)),
            pl.BlockSpec((tm, tile), lambda i: (i, 0)),
        ],
        out_specs=pl.BlockSpec((3, tm, local), lambda i: (0, i, 0)),
        out_shape=jax.ShapeDtypeStruct((3, n, local), bf16),
        compiler_params=params(),
        cost_estimate=SMALL,
        name="qkv_rope",
    )(x, w3, bias, cosine, sine)


def chosen_kernel(me_ref, *refs, held):
    x_ref, w_ref, b_ref, act_ref, slope_ref = refs[held:]
    seqs, here, width = x_ref.shape
    x = x_ref[...].reshape(seqs * here, width)
    units = w_ref.shape[1]
    step = min(256, units)
    for at in range(0, units, step):
        cut = slice(at, at + step)
        h = dot(x, w_ref[:, cut], 1, 0) + b_ref[:, cut]
        square = h * h
        t = jnp.tanh(h * (0.7978845608028654 + 0.035677408136300125 * square))
        half = 0.5 + 0.5 * t
        act = h * half
        slope = half + (act - act * half) * (1.5957691216057308 + 0.21406444881780074 * square)
        act_ref[:, :, cut] = act.astype(bf16).reshape(seqs, here, step)
        slope_ref[:, :, cut] = slope.astype(bf16).reshape(seqs, here, step)


def mlp_hidden_of(x, w, bias, steps, before=(), weight=1):
    seqs, owners, here, width = x.shape
    units = w.shape[1]
    held = len(before)

    def device(j, me):
        chosen = me[0] ^ steps[0]
        for i in range(1, len(steps)):
            chosen = jnp.where(j == i, me[0] ^ steps[i], chosen)
        return 0, chosen, 0, 0

    out = pl.BlockSpec((seqs, None, here, units), device)
    me = lax.axis_index("tp").astype(jnp.int32).reshape(1)
    return pl.pallas_call(
        functools.partial(chosen_kernel, held=held),
        grid_spec=pltpu.PrefetchScalarGridSpec(
            num_scalar_prefetch=1,
            grid=(len(steps),),
            in_specs=[pl.BlockSpec(memory_space=pl.ANY)] * held
            + [
                pl.BlockSpec((seqs, None, here, width), device),
                pl.BlockSpec((width, units), lambda j, me: (0, 0)),
                pl.BlockSpec((1, units), lambda j, me: (0, 0)),
            ],
            out_specs=[out, out],
        ),
        out_shape=[jax.ShapeDtypeStruct((seqs, owners, here, units), bf16)] * 2,
        input_output_aliases={1 + i: i for i in range(held)},
        compiler_params=params(),
        cost_estimate=pl.CostEstimate(flops=int(weight), bytes_accessed=1, transcendentals=0),
        name="mlp_hidden_of",
    )(me, *before, x, w, bias)


def grad_in_kernel(g_ref, wo_ref, wd_ref, slope_ref, hg_ref, at_ref, sum_ref):
    g = g_ref[...]
    units = wo_ref.shape[0]
    step = min(256, units)

    @pl.when(pl.program_id(0) == 0)
    def _():
        sum_ref[...] = jnp.zeros_like(sum_ref)

    for at in range(0, units, step):
        slope = slope_ref[:, at : at + step].astype(f32)
        hg = (dot(g, wo_ref[at : at + step, :], 1, 1) * slope).astype(bf16)
        hg_ref[:, at : at + step] = hg
        sum_ref[0:1, at : at + step] += jnp.sum(hg.astype(f32), axis=0, keepdims=True)
    at_ref[...] = dot(g, wd_ref[...], 1, 1).astype(bf16)


def grad_in(g, wo, wd, slope, tm=512):
    n, width = g.shape
    units, local = wo.shape[0], wd.shape[0]
    return pl.pallas_call(
        grad_in_kernel,
        grid=(n // tm,),
        in_specs=[
            pl.BlockSpec((tm, width), lambda i: (i, 0)),
            pl.BlockSpec((units, width), lambda i: (0, 0)),
            pl.BlockSpec((local, width), lambda i: (0, 0)),
            pl.BlockSpec((tm, units), lambda i: (i, 0)),
        ],
        out_specs=[
            pl.BlockSpec((tm, units), lambda i: (i, 0)),
            pl.BlockSpec((tm, local), lambda i: (i, 0)),
            pl.BlockSpec((8, units), lambda i: (0, 0)),
        ],
        out_shape=[
            jax.ShapeDtypeStruct((n, units), bf16),
            jax.ShapeDtypeStruct((n, local), bf16),
            jax.ShapeDtypeStruct((8, units), f32),
        ],
        compiler_params=params(),
        cost_estimate=SMALL,
        name="grad_in",
    )(g, wo, wd, slope)


def tokens_kernel(x_ref, w_ref, o_ref):
    width = w_ref.shape[1]
    step = min(512, width)
    for at in range(0, width, step):
        o_ref[:, at : at + step] = dot(x_ref[...], w_ref[:, at : at + step], 1, 0).astype(o_ref.dtype)


def tokens_by_weight(x, w, share, shares, tm=512):
    n, depth = x.shape
    n //= shares
    width = w.shape[1]
    first = share * (n // tm)
    return pl.pallas_call(
        tokens_kernel,
        grid=(n // tm,),
        in_specs=[pl.BlockSpec((tm, depth), lambda i: (first + i, 0)), pl.BlockSpec((depth, width), lambda i: (0, 0))],
        out_specs=pl.BlockSpec((tm, width), lambda i: (i, 0)),
        out_shape=jax.ShapeDtypeStruct((n, width), bf16),
        compiler_params=params(),
        cost_estimate=SMALL,
        name="tokens_by_weight",
    )(x, w)


def weight_grad_kernel(a_ref, b_ref, o_ref):
    o_ref[...] = dot(a_ref[...], b_ref[...], 0, 0).astype(bf16)


def weight_grad(a, b, share=0, shares=1, tile=512, weight=1):
    n, rows = a.shape
    rows //= shares
    cols = b.shape[1]
    tile = min(tile, cols)
    return pl.pallas_call(
        weight_grad_kernel,
        grid=(cols // tile,),
        in_specs=[
            pl.BlockSpec((n, rows), lambda j: (0, share), pipeline_mode=pl.Buffered(1)),
            pl.BlockSpec((n, tile), lambda j: (0, j)),
        ],
        out_specs=pl.BlockSpec((rows, tile), lambda j: (0, j)),
        out_shape=jax.ShapeDtypeStruct((rows, cols), bf16),
        compiler_params=params(),
        cost_estimate=pl.CostEstimate(flops=int(weight), bytes_accessed=1, transcendentals=0),
        name="weight_grad",
    )(a, b)


def weight_grad_rows_kernel(a_ref, b_ref, *o_refs, counts):
    full = dot(a_ref[...], b_ref[...], 0, 0).astype(bf16)
    step = pl.program_id(0)
    first = 0
    for o_ref, count in zip(o_refs, counts):

        @pl.when((step >= first) & (step < first + count))
        def _(o_ref=o_ref):
            o_ref[...] = full

        first += count


def weight_grad_rows(a, b, shares, tile=512):
    n, rows = a.shape
    cols = b.shape[1]
    counts = [rows * share // sum(shares) // tile for share in shares]
    firsts = [sum(counts[:i]) for i in range(len(counts))]
    out = lambda i: pl.BlockSpec((tile, cols), lambda j: (jnp.clip(j - firsts[i], 0, counts[i] - 1), 0))
    return pl.pallas_call(
        functools.partial(weight_grad_rows_kernel, counts=counts),
        grid=(rows // tile,),
        in_specs=[
            pl.BlockSpec((n, tile), lambda j: (0, j)),
            pl.BlockSpec((n, cols), lambda j: (0, 0), pipeline_mode=pl.Buffered(1)),
        ],
        out_specs=[out(i) for i in range(len(counts))],
        out_shape=[jax.ShapeDtypeStruct((count * tile, cols), bf16) for count in counts],
        compiler_params=params(),
        cost_estimate=SMALL,
        name="weight_grad_rows",
    )(a, b)


def weight_grad_parts_kernel(a_ref, b_ref, first_ref, last_ref):
    for part in range(2):
        first_ref[part] = dot(a_ref[...], b_ref[part], 0, 0).astype(bf16)
    last_ref[...] = dot(a_ref[...], b_ref[2], 0, 0).astype(bf16)


def weight_grad_parts(a, b, tile=512, weight=1):
    n, rows = a.shape
    parts, _, cols = b.shape
    return pl.pallas_call(
        weight_grad_parts_kernel,
        grid=(rows // tile,),
        in_specs=[
            pl.BlockSpec((n, tile), lambda j: (0, j)),
            pl.BlockSpec((parts, n, cols), lambda j: (0, 0, 0), pipeline_mode=pl.Buffered(1)),
        ],
        out_specs=[pl.BlockSpec((2, tile, cols), lambda j: (0, j, 0)), pl.BlockSpec((tile, cols), lambda j: (j, 0))],
        out_shape=[jax.ShapeDtypeStruct((2, rows, cols), bf16), jax.ShapeDtypeStruct((rows, cols), bf16)],
        compiler_params=params(),
        cost_estimate=pl.CostEstimate(flops=int(weight), bytes_accessed=1, transcendentals=0),
        name="weight_grad_parts",
    )(a, b)


def normed_grad_kernel(*refs, held):
    hg_ref, dq_ref, wi_ref, w3_ref, x_ref, shift_ref, o_ref, sum_ref, norm_ref = refs[held:]

    @pl.when(pl.program_id(0) == 0)
    def _():
        sum_ref[...] = jnp.zeros_like(sum_ref)
        norm_ref[...] = jnp.zeros_like(norm_ref)

    for part in range(3):
        sum_ref[part, 0:1] += jnp.sum(dq_ref[part].astype(f32), axis=0, keepdims=True)
    width = o_ref.shape[1]
    step = min(512, width)
    for at in range(0, width, step):
        cut = slice(at, at + step)
        total = dot(hg_ref[...], wi_ref[cut, :], 1, 1)
        for part in range(3):
            total += dot(dq_ref[part], w3_ref[part, cut, :], 1, 1)
        o_ref[:, cut] = total.astype(bf16)
        scaled = x_ref[:, cut].astype(f32) - shift_ref[:, cut]
        norm_ref[0:1, cut] += jnp.sum(total * scaled, axis=0, keepdims=True)
        norm_ref[1:2, cut] += jnp.sum(total, axis=0, keepdims=True)


def normed_grad(hg, dqkv, wi, w3, x, shift, share, shares, before=(), tm=512):
    n, units = hg.shape
    held = len(before)
    steps = n // shares // tm
    first = share * steps
    width, local = w3.shape[1:]
    return pl.pallas_call(
        functools.partial(normed_grad_kernel, held=held),
        grid=(steps,),
        in_specs=[pl.BlockSpec(memory_space=pl.ANY)] * held
        + [
            pl.BlockSpec((tm, units), lambda i: (first + i, 0)),
            pl.BlockSpec((3, tm, local), lambda i: (0, first + i, 0)),
            pl.BlockSpec((width, units), lambda i: (0, 0)),
            pl.BlockSpec((3, width, local), lambda i: (0, 0, 0)),
            pl.BlockSpec((tm, width), lambda i: (first + i, 0)),
            pl.BlockSpec((1, width), lambda i: (0, 0)),
        ],
        out_specs=[
            pl.BlockSpec((tm, width), lambda i: (first + i, 0)),
            pl.BlockSpec((3, 8, local), lambda i: (0, 0, 0)),
            pl.BlockSpec((8, width), lambda i: (0, 0)),
        ],
        out_shape=[
            jax.ShapeDtypeStruct((n, width), bf16),
            jax.ShapeDtypeStruct((3, 8, local), f32),
            jax.ShapeDtypeStruct((8, width), f32),
        ],
        input_output_aliases={i: i for i in range(held)},
        compiler_params=params(),
        cost_estimate=SMALL,
        name="normed_grad",
    )(*before, hg, dqkv, wi, w3, x, shift)


def attention_kernel(*refs, bq, held):
    start_ref, q_ref, k_ref, v_ref, do_ref, c_ref, s_ref, o_ref, by_owner_ref, g_ref, dk_acc, dv_acc = refs[held:]
    span, width = q_ref.shape
    here = by_owner_ref.shape[1]
    lane = lax.broadcasted_iota(jnp.int32, (1, width), 1) // HD
    zero = jnp.zeros((), bf16)
    heads = range(width // HD)
    cuts = [slice(head * HD, (head + 1) * HD) for head in heads]
    blocks = span // bq
    keys_across, vals_across = k_ref[...].T, v_ref[...].T

    def turn_back(x, at, n):
        return x * c_ref[at : at + n, :] + rope_swap(x) * s_ref[at : at + n, :]

    def products(block):
        at, n = block * bq, (block + 1) * bq
        keys, vals = k_ref[0:n, :], v_ref[0:n, :]
        queries = [jnp.where(lane == head, q_ref[at:n, :], zero) for head in heads]
        grads = [jnp.where(lane == head, do_ref[at:n, :], zero) for head in heads]
        return queries, grads, [dot(keys, q, 1, 1) for q in queries], [dot(vals, g, 1, 1) for g in grads]

    ahead = products(0)
    for block in range(blocks):
        at, n = block * bq, (block + 1) * bq
        queries, grads, scores, prob_grads = ahead
        key = lax.broadcasted_iota(jnp.int32, (n, bq), 0)
        place = lax.broadcasted_iota(jnp.int32, (1, bq), 1) + at
        allowed = (key >= start_ref[:, at:n]) & (key <= place)
        if block + 1 < blocks:
            ahead = products(block + 1)
        probs = []
        for head in heads:
            score = jnp.where(allowed, scores[head], big_negative)
            expd = jnp.exp(score - jnp.max(score, axis=0, keepdims=True))
            probs.append(expd * (1.0 / jnp.sum(expd, axis=0, keepdims=True)))
        low = [p.astype(bf16) for p in probs]
        out = [dot(vals_across[cut, 0:n], p, 1, 0) for cut, p in zip(cuts, low)]
        dv = sum(dot(p, g, 1, 0) for p, g in zip(low, grads))
        score_grads = []
        for p, g in zip(probs, prob_grads):
            both = p * g
            score_grads.append((both - p * jnp.sum(both, axis=0, keepdims=True)).astype(bf16))
        dq = [dot(keys_across[cut, 0:n], g, 1, 0) for cut, g in zip(cuts, score_grads)]
        dk = sum(dot(g, q, 1, 0) for g, q in zip(score_grads, queries))
        out = jnp.concatenate(out, axis=0).T.astype(bf16)
        o_ref[at:n, :] = out
        by_owner_ref[at // here, at % here : at % here + bq] = out
        g_ref[0, at:n, :] = turn_back(jnp.concatenate(dq, axis=0).T * (HD**-0.5), at, bq).astype(bf16)
        if block:
            dk_acc[0:at, :] += dk[0:at]
            dv_acc[0:at, :] += dv[0:at]
        dk_acc[at:n, :] = dk[at:n]
        dv_acc[at:n, :] = dv[at:n]
    g_ref[1] = turn_back(dk_acc[...], 0, span).astype(bf16)
    g_ref[2] = dv_acc[...].astype(bf16)


def attention_both(start, qkv, grad, cosine, sine, span, owners, row, before=(), bq=128):
    n, local = grad.shape
    here = 2 * span // owners
    width = cosine.shape[1]
    bq = min(bq, here)
    held = len(before)
    first = 2 * row
    part = lambda which: pl.BlockSpec((None, span, width), lambda t, p: (which, first + t, p))
    table = pl.BlockSpec((span, width), lambda t, p: (first + t, 0))
    return pl.pallas_call(
        functools.partial(attention_kernel, bq=bq, held=held),
        grid=(2, local // width),
        in_specs=[pl.BlockSpec(memory_space=pl.ANY)] * held
        + [
            pl.BlockSpec((1, span), lambda t, p: (0, first + t)),
            part(0),
            part(1),
            part(2),
            pl.BlockSpec((span, width), lambda t, p: (first + t, p)),
            table,
            table,
        ],
        out_specs=[
            pl.BlockSpec((span, width), lambda t, p: (first + t, p)),
            pl.BlockSpec((owners // 2, None, here, width), lambda t, p: (t, row, 0, p)),
            pl.BlockSpec((3, span, width), lambda t, p: (0, first + t, p)),
        ],
        out_shape=[
            jax.ShapeDtypeStruct((n, local), bf16),
            jax.ShapeDtypeStruct((owners, n // (2 * span), here, local), bf16),
            jax.ShapeDtypeStruct((3, n, local), bf16),
        ],
        scratch_shapes=[pltpu.VMEM((span, width), f32)] * 2,
        input_output_aliases={i: i for i in range(held)},
        compiler_params=params(),
        cost_estimate=SMALL,
        name="attention_both",
    )(*before, start, qkv, qkv, qkv, grad, cosine, sine)


def own_kernel(x_ref, w_ref, bd_ref, bo_ref, token_ref, *refs):
    *mlp_refs, o_ref, sum_ref = refs
    owners, seqs, here, local = x_ref.shape
    attention = jnp.zeros((seqs * here, w_ref.shape[1]), f32) + bd_ref[...]
    for owner in range(owners):
        x = x_ref[owner].reshape(seqs * here, local)
        attention += dot(x, w_ref[owner * local : (owner + 1) * local, :], 1, 0)
    tokens = token_ref[...].astype(f32)
    mlp = jnp.concatenate([a[...] for a in mlp_refs], axis=0).astype(f32) + bo_ref[...]
    total = tokens + attention + mlp
    o_ref[...] = total.astype(bf16)

    @pl.when(pl.program_id(0) == 0)
    def _():
        sum_ref[...] = jnp.zeros_like(sum_ref)

    for i, a in enumerate((tokens, attention, mlp, total)):
        sum_ref[i : i + 1, :] += jnp.sum(a * a, axis=0, keepdims=True)


def project_own(x, w, bd, bo, tokens, mlp_parts, tile=512, weight=1):
    owners, seqs, here, local = x.shape
    width = w.shape[1]
    rows = seqs * here
    column = lambda high: pl.BlockSpec((high, tile), lambda j: (0, j))
    return pl.pallas_call(
        own_kernel,
        grid=(width // tile,),
        in_specs=[
            pl.BlockSpec(x.shape, lambda j: (0, 0, 0, 0)),
            column(owners * local),
            column(1),
            column(1),
            column(rows),
        ]
        + [column(a.shape[0]) for a in mlp_parts],
        out_specs=[column(rows), pl.BlockSpec((8, tile), lambda j: (0, 0))],
        out_shape=[jax.ShapeDtypeStruct((rows, width), bf16), jax.ShapeDtypeStruct((8, tile), f32)],
        compiler_params=params(),
        cost_estimate=pl.CostEstimate(flops=int(weight), bytes_accessed=1, transcendentals=0),
        name="project_own",
    )(x, w, bd, bo, tokens, *mlp_parts)


def line_ok(size):
    return size >= 4 and size & (size - 1) == 0


class RowSum:
    def __init__(self, part, size):
        self.part, self.size, self.axis = part, size, "rows"
        groups = range(0, size, 4)
        pairs = lambda *ends: [(g + a, g + b) for g in groups for a, b in ends]
        self.hops = [pairs((0, 1), (3, 2)), pairs((1, 2), (2, 1))]
        hop = 4
        while hop < size:
            self.hops.append([(i, i ^ hop) for i in range(size)])
            hop *= 2
        self.hops.append(pairs((1, 0), (2, 3)))
        self.send()

    def send(self):
        if line_ok(self.size):
            self.came = lax.ppermute(self.part, self.axis, self.hops.pop(0))

    def fold(self, order):
        if line_ok(self.size) and self.hops:
            add = lambda a, b: (a.astype(f32) + b.astype(f32)).astype(a.dtype)
            self.part = order(add, self.part, self.came)
            self.send()

    def settle(self, order):
        if line_ok(self.size):
            self.came = order(lambda a: a, self.came)

    def complete(self, order):
        while self.hops:
            self.fold(order)

    def result(self, order=None):
        if not line_ok(self.size):
            return lax.psum(self.part.astype(f32), "rows")
        self.complete(order or Order())
        place = lax.axis_index("rows") % 4
        return jnp.where((place == 1) | (place == 2), self.part, self.came).astype(f32)


def finish_kernel(inner_ref, kept_ref, came_ref, *refs):
    o_ref = refs[-1]

    @pl.when(inner_ref[0] == 1)
    def _():
        o_ref[...] = kept_ref[...].astype(f32)

    @pl.when(inner_ref[0] == 0)
    def _():
        o_ref[...] = came_ref[...].astype(f32)


def finish(total, order, high, first=0, before=None, tile=512):
    flat = lambda a: a.reshape(-1, a.shape[-1])
    rows, cols = flat(total.part).shape
    if not line_ok(total.size):
        before = jnp.zeros((high, cols), f32) if before is None else before
        return lax.dynamic_update_slice(before, flat(total.result()), (first, 0))
    total.complete(order)
    tile = min(tile, rows)
    held = [] if before is None else [before]
    block = pl.BlockSpec((tile, cols), lambda j: (j, 0))
    place = lax.axis_index("rows") % 4
    inner = ((place == 1) | (place == 2)).astype(jnp.int32).reshape(1)
    call = pl.pallas_call(
        finish_kernel,
        grid=(rows // tile,),
        in_specs=[pl.BlockSpec(memory_space=pltpu.SMEM), block, block] + [pl.BlockSpec(memory_space=pl.ANY)] * len(held),
        out_specs=pl.BlockSpec((tile, cols), lambda j: (first // tile + j, 0)),
        out_shape=jax.ShapeDtypeStruct((high, cols), f32),
        input_output_aliases={3: 0} if held else {},
        compiler_params=params(),
        cost_estimate=SMALL,
        name="finish",
    )
    return order(lambda *a: call(inner, *a), flat(total.part), flat(total.came), *held)


class Gather:
    core, x, y = 1, 2, 4

    def __init__(self, first, second, size):
        self.first, self.second, self.size = first, second, size
        self.x0, self.y1 = self.send(first, self.x), self.send(second, self.y)

    def send(self, a, step):
        return lax.ppermute(a, "tp", [(i, i ^ step) for i in range(self.size)])

    def others(self, order=None):
        first, second = self.first, self.second
        if order:
            first, second = order(lambda a, b: (a, b), first, second)
        self.x1, self.y0 = self.send(second, self.x), self.send(first, self.y)
        self.c0 = self.send(first, self.core)

    def forward(self, order):
        came = (self.x0, self.y1, self.c0, self.second)
        self.x0, self.y1, self.c0, self.second = order(lambda *a: a, *came)
        self.c1 = self.send(self.second, self.core)
        self.d0, self.d1 = self.send(self.x0, self.y), self.send(self.y1, self.x)

    def pairs(self, order):
        came = (self.x0, self.y1, self.x1, self.y0, self.c1)
        self.x0, self.y1, self.x1, self.y0, self.c1 = order(lambda *a: a, *came)
        self.px0, self.py1 = self.send(self.x0, self.core), self.send(self.y1, self.core)
        self.px1, self.py0 = self.send(self.x1, self.core), self.send(self.y0, self.core)

    def near(self, order):
        steps = [step for step in (0, self.core, self.x, self.y, self.x | self.core, self.y | self.core) for _ in range(2)]
        pieces = (self.first, self.second, self.c0, self.c1, self.x0, self.x1, self.y0, self.y1)
        pieces += (self.px0, self.px1, self.py0, self.py1)
        self.full = order(lambda *a: place_pieces(None, a, steps, (0, 1) * 6, self.size), *pieces)

    def far_pairs(self, order):
        self.d0, self.d1 = order(lambda a, b: (a, b), self.d0, self.d1)
        self.pd0, self.pd1 = self.send(self.d0, self.core), self.send(self.d1, self.core)

    def far(self, order):
        far = self.x | self.y
        steps = (far, far, far | self.core, far | self.core)
        place = lambda full, *a: place_pieces(full, a, steps, (0, 1, 0, 1), self.size)
        self.full = order(place, self.full, self.d0, self.d1, self.pd0, self.pd1)
        return self.full


def place_kernel(me_ref, *refs, held):
    pieces, o_ref = refs[held:-1], refs[-1]
    for i, piece in enumerate(pieces):

        @pl.when(pl.program_id(0) == i)
        def _(piece=piece):
            o_ref[...] = piece[...].reshape(o_ref.shape)


def place_pieces(full, pieces, steps, halves, size):
    held = 0 if full is None else 1
    here, width = pieces[0].shape

    def target(j, me):
        device, half = me[0] ^ steps[0], halves[0]
        for i in range(1, len(pieces)):
            device = jnp.where(j == i, me[0] ^ steps[i], device)
            half = jnp.where(j == i, halves[i], half)
        return half, device, 0, 0

    hbm = pl.BlockSpec(memory_space=pl.ANY)
    me = lax.axis_index("tp").astype(jnp.int32).reshape(1)
    return pl.pallas_call(
        functools.partial(place_kernel, held=held),
        grid_spec=pltpu.PrefetchScalarGridSpec(
            num_scalar_prefetch=1,
            grid=(len(pieces),),
            in_specs=[hbm] * held + [pl.BlockSpec((here, width), lambda j, me: (0, 0))] * len(pieces),
            out_specs=pl.BlockSpec((1, None, here, width), target),
        ),
        out_shape=jax.ShapeDtypeStruct((2, size, here, width), bf16),
        input_output_aliases={1: 0} if held else {},
        compiler_params=params(),
        cost_estimate=SMALL,
        name="place_pieces",
    )(me, *([full] if held else []), *pieces)


class TpSum:
    def __init__(self, part, size):
        self.part, self.size, self.hop = part, size, 1
        self.send()

    def send(self):
        if self.size & (self.size - 1) == 0 and self.hop < self.size:
            self.came = lax.ppermute(self.part, "tp", [(i, i ^ self.hop) for i in range(self.size)])

    def fold(self, order):
        if self.size & (self.size - 1):
            self.part, self.size = lax.psum(self.part, "tp"), 1
        elif self.hop < self.size:
            self.part = order(lambda a, b: a + b, self.part, self.came)
            self.hop *= 2
            self.send()

    def result(self, order):
        while self.hop < self.size:
            self.fold(order)
        return self.part


def body(
    tokens,
    segment_ids,
    positions,
    norm_gain,
    norm_shift,
    query_key_value_weight,
    b_qkv,
    dense_weight,
    b_dense,
    inward_weight,
    b_in,
    outward_weight,
    b_out,
    cotangent,
):
    rows, tp = lax.axis_size("rows"), lax.axis_size("tp")
    seqs, here, width = tokens.shape
    length = here * tp
    n = seqs * length
    local = query_key_value_weight.shape[2]
    tile = min(128, local)
    span = length // 2

    exchange = tp == 8 and seqs == 2

    order = Order()
    gain, shift = norm_gain.astype(f32), norm_shift.astype(f32)
    norm = lambda a: norm_halves(a.reshape(seqs * here, width), gain, shift)
    halves = order(norm, tokens)

    if exchange:
        gather_normed = Gather(*halves, tp)
        gather_normed.others()

    def tables(positions, weight):
        place = positions.reshape(n, 1)
        cosine, sine = rope_tables(place, tile)
        start = jnp.arange(n, dtype=jnp.int32)[None] % span - positions.reshape(1, n)
        return cosine, sine, start, jnp.transpose(weight, (1, 0, 2))

    cosine, sine, start, w3 = order(tables, positions, query_key_value_weight)
    in_bias_row = b_in.astype(f32)[None]
    token_rows = lambda a: a.reshape(n, a.shape[-1])
    later = lambda a: lax.all_gather(order(lambda b: b, a), "tp", axis=1, tiled=True).reshape(n, width)
    if exchange:
        gather_normed.forward(order)
        gather_normed.pairs(order)
        grad = later(cotangent)
        gather_normed.near(order)
        hidden_of = lambda *a: mlp_hidden_of(*a, tuple(range(6)))
        hidden = order(hidden_of, gather_normed.full, inward_weight, in_bias_row)
        gather_normed.far_pairs(order)
        normed_full = gather_normed.far(order)
        hidden_of = lambda x, w, b, *before: mlp_hidden_of(x, w, b, (6, 7), before)
        act, slope = order(hidden_of, normed_full, inward_weight, in_bias_row, *hidden)
    else:
        normed_full = jnp.concatenate(halves).reshape(seqs, here, width)
        normed_full = lax.all_gather(normed_full, "tp", axis=1).reshape(seqs, tp, here, width)
        grad = later(cotangent)
        hidden_of = lambda *a: mlp_hidden_of(*a, tuple(range(tp)))
        act, slope = order(hidden_of, normed_full, inward_weight, in_bias_row)
    normed, act, slope = token_rows(normed_full), token_rows(act), token_rows(slope)
    qkv = order(project_qkv, normed, w3, b_qkv.astype(f32), cosine, sine)
    dense_ready, _ = lax.optimization_barrier((dense_weight, act))
    dense_full = lax.all_gather(dense_ready, "tp", axis=0, tiled=True)
    o0 = RowSum(order(lambda *a: weight_grad(*a, 0, 2), act, grad), rows)
    o1 = RowSum(order(lambda *a: weight_grad(*a, 1, 2), act, grad), rows)
    row_sum = lambda parts: [RowSum(part, rows) for part in parts]
    hidden_grad, attended_grad, in_bias = order(grad_in, grad, outward_weight, dense_weight, slope)
    o0.fold(order)
    mlp_part = order(lambda *a: tokens_by_weight(*a, 0, 1), act, outward_weight).reshape(seqs, length, width)
    mlp_tok = lax.psum_scatter(mlp_part, "tp", scatter_dimension=1, tiled=True).reshape(seqs * here, width)
    i0, i1 = row_sum(order(lambda a, b: weight_grad_rows(a, b, (1, 1)), normed, hidden_grad))
    o1.fold(order)
    o0.fold(order)
    both = lambda row: lambda s, q, g, c, t, *before: attention_both(s, q, g, c, t, span, tp, row, before)
    attended, by_owner, dqkv = order(both(0), start, qkv, attended_grad, cosine, sine)
    for row in range(1, seqs):
        kept = (attended, by_owner, dqkv)
        attended, by_owner, dqkv = order(both(row), start, qkv, attended_grad, cosine, sine, *kept)
    mine = lax.all_to_all(by_owner, "tp", split_axis=0, concat_axis=0, tiled=True)
    o1.fold(order)
    i0.fold(order)
    o0.settle(order)
    qs, vs = row_sum(order(lambda a, b: weight_grad_parts(a, b, weight=EARLY_WEIGHT), normed, dqkv))
    units = in_bias.shape[1]
    back = lambda share: lambda *a: normed_grad(*a[:5], shift[None], share, 2, a[5:])
    i1.fold(order)
    part, bias_a, norm_a = order(back(0), hidden_grad, dqkv, inward_weight, w3, normed)
    i0.fold(order)
    o1.settle(order)
    part, bias_b, norm_b = order(back(1), hidden_grad, dqkv, inward_weight, w3, normed, part)
    back_tok = lax.psum_scatter(part.reshape(seqs, length, width), "tp", scatter_dimension=1, tiled=True)
    i1.fold(order)
    qs.fold(order)
    (ds,) = row_sum([order(weight_grad, attended, grad)])
    vs.fold(order)
    i0.settle(order)

    cols = width // tp

    def column_sums(grad):
        mine = lax.dynamic_slice_in_dim(grad, lax.axis_index("tp") * cols, cols, 1)
        return jnp.sum(mine.astype(f32), axis=0)

    out_bias = order(column_sums, grad)
    rows_of = lambda a: a.reshape(seqs * here, width)
    bias_rows = (b_dense.astype(f32)[None], b_out.astype(f32)[None])
    own = lambda x, w, t, *m: project_own(x, w, *bias_rows, rows_of(t), m, weight=ORDER_WEIGHT)
    layer_out, squares = order(own, mine, dense_full, tokens, mlp_tok)
    layer_out = layer_out.reshape(tokens.shape)

    def pack(norm_a, norm_b, squares):
        norm_sums = norm_a + norm_b
        squares = jnp.sum(squares[:4], axis=1)
        pad = jnp.zeros((124,), f32)
        return jnp.concatenate([norm_sums[0] / gain, norm_sums[1], squares, pad]).reshape(-1, 128)

    packed = TpSum(order(pack, norm_a, norm_b, squares), tp)
    ds.fold(order)
    qs.fold(order)
    vs.fold(order)
    packed.fold(order)
    out_grad = finish(o0, order, units)
    packed.fold(order)
    out_grad = finish(o1, order, units, units // 2, out_grad)
    packed.fold(order)
    qkv_bias = bias_a + bias_b
    small = jnp.concatenate([in_bias[0], qkv_bias[:, 0].reshape(-1), out_bias]).reshape(-1, 128)
    small = RowSum(jnp.concatenate([packed.result(order), small]), rows)
    in_grad = finish(i0, order, width)
    ds.fold(order)
    in_grad = finish(i1, order, width, width // 2, in_grad)
    small.fold(order)
    small.fold(order)
    qkv_grad = finish(qs, order, 3 * width)
    qkv_grad = finish(vs, order, 3 * width, 2 * width, qkv_grad)

    def norm_back(back_tok, tokens, cotangent):
        values = tokens.astype(f32)
        center = values - jnp.mean(values, axis=-1, keepdims=True)
        inverse = lax.rsqrt(jnp.mean(center * center, axis=-1, keepdims=True) + epsilon)
        unit = center * inverse
        unit_grad = back_tok.astype(f32) * gain
        mean_grad = jnp.mean(unit_grad, axis=-1, keepdims=True)
        mean_both = jnp.mean(unit_grad * unit, axis=-1, keepdims=True)
        value_grad = (unit_grad - mean_grad - unit * mean_both) * inverse
        return (cotangent.astype(f32) + value_grad).astype(bf16)

    input_grad = order(norm_back, back_tok, tokens, cotangent)
    qkv_grad = jnp.transpose(qkv_grad.reshape(3, width, local), (1, 0, 2))
    dense_grad = finish(ds, order, local)
    small = small.result().reshape(-1)
    slice_at = lambda a: lax.dynamic_slice_in_dim(a, lax.axis_index("tp") * cols, cols, 0)
    gain_grad, shift_grad = slice_at(small[:width]), slice_at(small[width : 2 * width])
    rms_values = jnp.sqrt(small[2 * width : 2 * width + 4] / (seqs * rows * length * width))
    small = small[2 * width + 128 :]
    in_bias_grad = small[:units]
    qkv_bias_grad = small[units : units + 3 * local].reshape(3, local)
    out_bias_grad = small[units + 3 * local :]

    return (
        layer_out,
        input_grad,
        gain_grad,
        shift_grad,
        qkv_grad,
        qkv_bias_grad,
        dense_grad,
        out_bias_grad,
        in_grad,
        in_bias_grad,
        out_grad,
        out_bias_grad,
        rms_values,
    )


def solution(mesh):
    in_specs = (
        P("rows", "tp", None),
        P("rows", None),
        P("rows", None),
        P(),
        P(),
        P(None, None, "tp"),
        P(None, "tp"),
        P("tp", None),
        P(),
        P(None, "tp"),
        P("tp"),
        P("tp", None),
        P(),
        P("rows", "tp", None),
    )
    out_specs = (
        P("rows", "tp", None),
        P("rows", "tp", None),
        P("tp"),
        P("tp"),
        P(None, None, "tp"),
        P(None, "tp"),
        P("tp", None),
        P("tp"),
        P(None, "tp"),
        P("tp"),
        P("tp", None),
        P("tp"),
        P(),
    )
    return jax.shard_map(body, mesh=mesh, in_specs=in_specs, out_specs=out_specs, check_vma=False)
```

```python
import functools

import jax
import jax.numpy as jnp
from jax import lax
from jax.experimental import pallas as pl
from jax.experimental.pallas import tpu as pltpu
from jax.sharding import PartitionSpec as P

HD = 64
ROT = 32
epsilon = 1e-05
big_negative = -1e30
rope_base = 10000.0
f32 = jnp.float32
bf16 = jnp.bfloat16
VMEM_LIMIT = 56 << 20
ORDER_WEIGHT = int(2.1e11)
EARLY_WEIGHT = int(2.2e11)


def dot(a, b, ca, cb):
    return lax.dot_general(a, b, (((ca,), (cb,)), ((), ())), preferred_element_type=f32)


SMALL = pl.CostEstimate(flops=1, bytes_accessed=1, transcendentals=0)


def params():
    return pltpu.CompilerParams(vmem_limit_bytes=VMEM_LIMIT)


class Order:
    def __init__(self):
        self.last = ()

    def __call__(self, op, *operands):
        operands, _ = lax.optimization_barrier((operands, self.last))
        result = op(*operands)
        self.last = jax.tree.leaves(result)
        return result


def rope_swap(x):
    width = x.shape[-1]
    lane = lax.broadcasted_iota(jnp.int32, (1, width), 1) % HD
    up = pltpu.roll(x, width - ROT // 2, 1)
    down = pltpu.roll(x, ROT // 2, 1)
    return jnp.where(lane < ROT // 2, up, -down)


def norm_kernel(x_ref, gain_ref, shift_ref, first_ref, second_ref, *, per):
    x = x_ref[...].astype(f32)
    center = x - jnp.mean(x, axis=-1, keepdims=True)
    inverse = lax.rsqrt(jnp.mean(center * center, axis=-1, keepdims=True) + epsilon)
    out = (center * inverse * gain_ref[...] + shift_ref[...]).astype(bf16)

    @pl.when(pl.program_id(0) < per)
    def _():
        first_ref[...] = out

    @pl.when(pl.program_id(0) >= per)
    def _():
        second_ref[...] = out


def norm_halves(x, gain, shift, tm=128):
    n, width = x.shape
    per = n // 2 // tm
    vector = pl.BlockSpec((1, width), lambda i: (0, 0))
    return pl.pallas_call(
        functools.partial(norm_kernel, per=per),
        grid=(2 * per,),
        in_specs=[pl.BlockSpec((tm, width), lambda i: (i, 0)), vector, vector],
        out_specs=[
            pl.BlockSpec((tm, width), lambda i: (jnp.minimum(i, per - 1), 0)),
            pl.BlockSpec((tm, width), lambda i: (jnp.maximum(i - per, 0), 0)),
        ],
        out_shape=[jax.ShapeDtypeStruct((n // 2, width), bf16)] * 2,
        compiler_params=params(),
        cost_estimate=SMALL,
        name="norm_halves",
    )(x, gain[None], shift[None])


def table_kernel(place_ref, frequency_ref, c_ref, s_ref):
    angle = place_ref[...].astype(f32) * frequency_ref[...]
    lane = lax.broadcasted_iota(jnp.int32, angle.shape, 1) % HD
    turned = lane < ROT
    c_ref[...] = jnp.where(turned, jnp.cos(angle), 1.0)
    s_ref[...] = jnp.where(turned, jnp.sin(angle), 0.0)


def rope_tables(place, tile, tm=1024):
    n = place.shape[0]
    lane = jnp.arange(tile, dtype=jnp.int32) % (ROT // 2)
    frequency = (rope_base ** (-2.0 * lane.astype(f32) / ROT))[None]
    table = pl.BlockSpec((tm, tile), lambda i: (i, 0))
    return pl.pallas_call(
        table_kernel,
        grid=(n // tm,),
        in_specs=[pl.BlockSpec((tm, 1), lambda i: (i, 0)), pl.BlockSpec((1, tile), lambda i: (0, 0))],
        out_specs=[table, table],
        out_shape=[jax.ShapeDtypeStruct((n, tile), f32)] * 2,
        compiler_params=params(),
        cost_estimate=SMALL,
        name="rope_tables",
    )(place, frequency)


def qkv_kernel(x_ref, w_ref, b_ref, c_ref, s_ref, o_ref):
    x = x_ref[...]
    tile = c_ref.shape[-1]
    local = w_ref.shape[-1]
    cosine, sine = c_ref[...], s_ref[...]
    for part in range(3):
        full = dot(x, w_ref[part], 1, 0) + b_ref[part : part + 1, :]
        for at in range(0, local, tile):
            piece = full[:, at : at + tile]
            if part < 2:
                piece = piece * cosine - rope_swap(piece) * sine
            if part == 0:
                piece = piece * (HD**-0.5)
            o_ref[part, :, at : at + tile] = piece.astype(bf16)


def project_qkv(x, w3, bias, cosine, sine, tm=512):
    n, width = x.shape
    local = w3.shape[2]
    tile = cosine.shape[1]
    return pl.pallas_call(
        qkv_kernel,
        grid=(n // tm,),
        in_specs=[
            pl.BlockSpec((tm, width), lambda i: (i, 0)),
            pl.BlockSpec((3, width, local), lambda i: (0, 0, 0)),
            pl.BlockSpec((3, local), lambda i: (0, 0)),
            pl.BlockSpec((tm, tile), lambda i: (i, 0)),
            pl.BlockSpec((tm, tile), lambda i: (i, 0)),
        ],
        out_specs=pl.BlockSpec((3, tm, local), lambda i: (0, i, 0)),
        out_shape=jax.ShapeDtypeStruct((3, n, local), bf16),
        compiler_params=params(),
        cost_estimate=SMALL,
        name="qkv_rope",
    )(x, w3, bias, cosine, sine)


def chosen_kernel(me_ref, *refs, held):
    x_ref, w_ref, b_ref, act_ref, slope_ref = refs[held:]
    seqs, here, width = x_ref.shape
    x = x_ref[...].reshape(seqs * here, width)
    units = w_ref.shape[1]
    step = min(256, units)
    for at in range(0, units, step):
        cut = slice(at, at + step)
        h = dot(x, w_ref[:, cut], 1, 0) + b_ref[:, cut]
        square = h * h
        t = jnp.tanh(h * (0.7978845608028654 + 0.035677408136300125 * square))
        half = 0.5 + 0.5 * t
        act = h * half
        slope = half + (act - act * half) * (1.5957691216057308 + 0.21406444881780074 * square)
        act_ref[:, :, cut] = act.astype(bf16).reshape(seqs, here, step)
        slope_ref[:, :, cut] = slope.astype(bf16).reshape(seqs, here, step)


def mlp_hidden_of(x, w, bias, steps, before=(), weight=1):
    seqs, owners, here, width = x.shape
    units = w.shape[1]
    held = len(before)

    def device(j, me):
        chosen = me[0] ^ steps[0]
        for i in range(1, len(steps)):
            chosen = jnp.where(j == i, me[0] ^ steps[i], chosen)
        return 0, chosen, 0, 0

    out = pl.BlockSpec((seqs, None, here, units), device)
    me = lax.axis_index("tp").astype(jnp.int32).reshape(1)
    return pl.pallas_call(
        functools.partial(chosen_kernel, held=held),
        grid_spec=pltpu.PrefetchScalarGridSpec(
            num_scalar_prefetch=1,
            grid=(len(steps),),
            in_specs=[pl.BlockSpec(memory_space=pl.ANY)] * held
            + [
                pl.BlockSpec((seqs, None, here, width), device),
                pl.BlockSpec((width, units), lambda j, me: (0, 0)),
                pl.BlockSpec((1, units), lambda j, me: (0, 0)),
            ],
            out_specs=[out, out],
        ),
        out_shape=[jax.ShapeDtypeStruct((seqs, owners, here, units), bf16)] * 2,
        input_output_aliases={1 + i: i for i in range(held)},
        compiler_params=params(),
        cost_estimate=pl.CostEstimate(flops=int(weight), bytes_accessed=1, transcendentals=0),
        name="mlp_hidden_of",
    )(me, *before, x, w, bias)


def grad_in_kernel(g_ref, wo_ref, wd_ref, slope_ref, hg_ref, at_ref, sum_ref):
    g = g_ref[...]
    units = wo_ref.shape[0]
    step = min(256, units)

    @pl.when(pl.program_id(0) == 0)
    def _():
        sum_ref[...] = jnp.zeros_like(sum_ref)

    for at in range(0, units, step):
        slope = slope_ref[:, at : at + step].astype(f32)
        hg = (dot(g, wo_ref[at : at + step, :], 1, 1) * slope).astype(bf16)
        hg_ref[:, at : at + step] = hg
        sum_ref[0:1, at : at + step] += jnp.sum(hg.astype(f32), axis=0, keepdims=True)
    at_ref[...] = dot(g, wd_ref[...], 1, 1).astype(bf16)


def grad_in(g, wo, wd, slope, tm=512):
    n, width = g.shape
    units, local = wo.shape[0], wd.shape[0]
    return pl.pallas_call(
        grad_in_kernel,
        grid=(n // tm,),
        in_specs=[
            pl.BlockSpec((tm, width), lambda i: (i, 0)),
            pl.BlockSpec((units, width), lambda i: (0, 0)),
            pl.BlockSpec((local, width), lambda i: (0, 0)),
            pl.BlockSpec((tm, units), lambda i: (i, 0)),
        ],
        out_specs=[
            pl.BlockSpec((tm, units), lambda i: (i, 0)),
            pl.BlockSpec((tm, local), lambda i: (i, 0)),
            pl.BlockSpec((8, units), lambda i: (0, 0)),
        ],
        out_shape=[
            jax.ShapeDtypeStruct((n, units), bf16),
            jax.ShapeDtypeStruct((n, local), bf16),
            jax.ShapeDtypeStruct((8, units), f32),
        ],
        compiler_params=params(),
        cost_estimate=SMALL,
        name="grad_in",
    )(g, wo, wd, slope)


def tokens_kernel(x_ref, w_ref, o_ref):
    width = w_ref.shape[1]
    step = min(512, width)
    for at in range(0, width, step):
        o_ref[:, at : at + step] = dot(x_ref[...], w_ref[:, at : at + step], 1, 0).astype(o_ref.dtype)


def tokens_by_weight(x, w, share, shares, tm=512):
    n, depth = x.shape
    n //= shares
    width = w.shape[1]
    first = share * (n // tm)
    return pl.pallas_call(
        tokens_kernel,
        grid=(n // tm,),
        in_specs=[pl.BlockSpec((tm, depth), lambda i: (first + i, 0)), pl.BlockSpec((depth, width), lambda i: (0, 0))],
        out_specs=pl.BlockSpec((tm, width), lambda i: (i, 0)),
        out_shape=jax.ShapeDtypeStruct((n, width), bf16),
        compiler_params=params(),
        cost_estimate=SMALL,
        name="tokens_by_weight",
    )(x, w)


def weight_grad_kernel(a_ref, b_ref, o_ref):
    o_ref[...] = dot(a_ref[...], b_ref[...], 0, 0).astype(bf16)


def weight_grad(a, b, share=0, shares=1, tile=512, weight=1):
    n, rows = a.shape
    rows //= shares
    cols = b.shape[1]
    tile = min(tile, cols)
    return pl.pallas_call(
        weight_grad_kernel,
        grid=(cols // tile,),
        in_specs=[
            pl.BlockSpec((n, rows), lambda j: (0, share), pipeline_mode=pl.Buffered(1)),
            pl.BlockSpec((n, tile), lambda j: (0, j)),
        ],
        out_specs=pl.BlockSpec((rows, tile), lambda j: (0, j)),
        out_shape=jax.ShapeDtypeStruct((rows, cols), bf16),
        compiler_params=params(),
        cost_estimate=pl.CostEstimate(flops=int(weight), bytes_accessed=1, transcendentals=0),
        name="weight_grad",
    )(a, b)


def weight_grad_rows_kernel(a_ref, b_ref, *o_refs, counts):
    full = dot(a_ref[...], b_ref[...], 0, 0).astype(bf16)
    step = pl.program_id(0)
    first = 0
    for o_ref, count in zip(o_refs, counts):

        @pl.when((step >= first) & (step < first + count))
        def _(o_ref=o_ref):
            o_ref[...] = full

        first += count


def weight_grad_rows(a, b, shares, tile=512):
    n, rows = a.shape
    cols = b.shape[1]
    counts = [rows * share // sum(shares) // tile for share in shares]
    firsts = [sum(counts[:i]) for i in range(len(counts))]
    out = lambda i: pl.BlockSpec((tile, cols), lambda j: (jnp.clip(j - firsts[i], 0, counts[i] - 1), 0))
    return pl.pallas_call(
        functools.partial(weight_grad_rows_kernel, counts=counts),
        grid=(rows // tile,),
        in_specs=[
            pl.BlockSpec((n, tile), lambda j: (0, j)),
            pl.BlockSpec((n, cols), lambda j: (0, 0), pipeline_mode=pl.Buffered(1)),
        ],
        out_specs=[out(i) for i in range(len(counts))],
        out_shape=[jax.ShapeDtypeStruct((count * tile, cols), bf16) for count in counts],
        compiler_params=params(),
        cost_estimate=SMALL,
        name="weight_grad_rows",
    )(a, b)


def weight_grad_parts_kernel(a_ref, b_ref, first_ref, last_ref):
    for part in range(2):
        first_ref[part] = dot(a_ref[...], b_ref[part], 0, 0).astype(bf16)
    last_ref[...] = dot(a_ref[...], b_ref[2], 0, 0).astype(bf16)


def weight_grad_parts(a, b, tile=512, weight=1):
    n, rows = a.shape
    parts, _, cols = b.shape
    return pl.pallas_call(
        weight_grad_parts_kernel,
        grid=(rows // tile,),
        in_specs=[
            pl.BlockSpec((n, tile), lambda j: (0, j)),
            pl.BlockSpec((parts, n, cols), lambda j: (0, 0, 0), pipeline_mode=pl.Buffered(1)),
        ],
        out_specs=[pl.BlockSpec((2, tile, cols), lambda j: (0, j, 0)), pl.BlockSpec((tile, cols), lambda j: (j, 0))],
        out_shape=[jax.ShapeDtypeStruct((2, rows, cols), bf16), jax.ShapeDtypeStruct((rows, cols), bf16)],
        compiler_params=params(),
        cost_estimate=pl.CostEstimate(flops=int(weight), bytes_accessed=1, transcendentals=0),
        name="weight_grad_parts",
    )(a, b)


def normed_grad_kernel(*refs, held):
    hg_ref, dq_ref, wi_ref, w3_ref, x_ref, shift_ref, o_ref, sum_ref, norm_ref = refs[held:]

    @pl.when(pl.program_id(0) == 0)
    def _():
        sum_ref[...] = jnp.zeros_like(sum_ref)
        norm_ref[...] = jnp.zeros_like(norm_ref)

    for part in range(3):
        sum_ref[part, 0:1] += jnp.sum(dq_ref[part].astype(f32), axis=0, keepdims=True)
    width = o_ref.shape[1]
    step = min(512, width)
    for at in range(0, width, step):
        cut = slice(at, at + step)
        total = dot(hg_ref[...], wi_ref[cut, :], 1, 1)
        for part in range(3):
            total += dot(dq_ref[part], w3_ref[part, cut, :], 1, 1)
        o_ref[:, cut] = total.astype(bf16)
        scaled = x_ref[:, cut].astype(f32) - shift_ref[:, cut]
        norm_ref[0:1, cut] += jnp.sum(total * scaled, axis=0, keepdims=True)
        norm_ref[1:2, cut] += jnp.sum(total, axis=0, keepdims=True)


def normed_grad(hg, dqkv, wi, w3, x, shift, share, shares, before=(), tm=512):
    n, units = hg.shape
    held = len(before)
    steps = n // shares // tm
    first = share * steps
    width, local = w3.shape[1:]
    return pl.pallas_call(
        functools.partial(normed_grad_kernel, held=held),
        grid=(steps,),
        in_specs=[pl.BlockSpec(memory_space=pl.ANY)] * held
        + [
            pl.BlockSpec((tm, units), lambda i: (first + i, 0)),
            pl.BlockSpec((3, tm, local), lambda i: (0, first + i, 0)),
            pl.BlockSpec((width, units), lambda i: (0, 0)),
            pl.BlockSpec((3, width, local), lambda i: (0, 0, 0)),
            pl.BlockSpec((tm, width), lambda i: (first + i, 0)),
            pl.BlockSpec((1, width), lambda i: (0, 0)),
        ],
        out_specs=[
            pl.BlockSpec((tm, width), lambda i: (first + i, 0)),
            pl.BlockSpec((3, 8, local), lambda i: (0, 0, 0)),
            pl.BlockSpec((8, width), lambda i: (0, 0)),
        ],
        out_shape=[
            jax.ShapeDtypeStruct((n, width), bf16),
            jax.ShapeDtypeStruct((3, 8, local), f32),
            jax.ShapeDtypeStruct((8, width), f32),
        ],
        input_output_aliases={i: i for i in range(held)},
        compiler_params=params(),
        cost_estimate=SMALL,
        name="normed_grad",
    )(*before, hg, dqkv, wi, w3, x, shift)


def attention_kernel(*refs, bq, held):
    start_ref, q_ref, k_ref, v_ref, do_ref, c_ref, s_ref, o_ref, by_owner_ref, g_ref, dk_acc, dv_acc = refs[held:]
    span, width = q_ref.shape
    here = by_owner_ref.shape[1]
    lane = lax.broadcasted_iota(jnp.int32, (1, width), 1) // HD
    zero = jnp.zeros((), bf16)
    heads = range(width // HD)
    cuts = [slice(head * HD, (head + 1) * HD) for head in heads]
    blocks = span // bq
    keys_across, vals_across = k_ref[...].T, v_ref[...].T

    def turn_back(x, at, n):
        return x * c_ref[at : at + n, :] + rope_swap(x) * s_ref[at : at + n, :]

    def products(block):
        at, n = block * bq, (block + 1) * bq
        keys, vals = k_ref[0:n, :], v_ref[0:n, :]
        queries = [jnp.where(lane == head, q_ref[at:n, :], zero) for head in heads]
        grads = [jnp.where(lane == head, do_ref[at:n, :], zero) for head in heads]
        return queries, grads, [dot(keys, q, 1, 1) for q in queries], [dot(vals, g, 1, 1) for g in grads]

    ahead = products(0)
    for block in range(blocks):
        at, n = block * bq, (block + 1) * bq
        queries, grads, scores, prob_grads = ahead
        key = lax.broadcasted_iota(jnp.int32, (n, bq), 0)
        place = lax.broadcasted_iota(jnp.int32, (1, bq), 1) + at
        allowed = (key >= start_ref[:, at:n]) & (key <= place)
        if block + 1 < blocks:
            ahead = products(block + 1)
        probs = []
        for head in heads:
            score = jnp.where(allowed, scores[head], big_negative)
            expd = jnp.exp(score - jnp.max(score, axis=0, keepdims=True))
            probs.append(expd * (1.0 / jnp.sum(expd, axis=0, keepdims=True)))
        low = [p.astype(bf16) for p in probs]
        out = [dot(vals_across[cut, 0:n], p, 1, 0) for cut, p in zip(cuts, low)]
        dv = sum(dot(p, g, 1, 0) for p, g in zip(low, grads))
        score_grads = []
        for p, g in zip(probs, prob_grads):
            both = p * g
            score_grads.append((both - p * jnp.sum(both, axis=0, keepdims=True)).astype(bf16))
        dq = [dot(keys_across[cut, 0:n], g, 1, 0) for cut, g in zip(cuts, score_grads)]
        dk = sum(dot(g, q, 1, 0) for g, q in zip(score_grads, queries))
        out = jnp.concatenate(out, axis=0).T.astype(bf16)
        o_ref[at:n, :] = out
        by_owner_ref[at // here, at % here : at % here + bq] = out
        g_ref[0, at:n, :] = turn_back(jnp.concatenate(dq, axis=0).T * (HD**-0.5), at, bq).astype(bf16)
        if block:
            dk_acc[0:at, :] += dk[0:at]
            dv_acc[0:at, :] += dv[0:at]
        dk_acc[at:n, :] = dk[at:n]
        dv_acc[at:n, :] = dv[at:n]
    g_ref[1] = turn_back(dk_acc[...], 0, span).astype(bf16)
    g_ref[2] = dv_acc[...].astype(bf16)


def attention_both(start, qkv, grad, cosine, sine, span, owners, row, before=(), bq=128):
    n, local = grad.shape
    here = 2 * span // owners
    width = cosine.shape[1]
    bq = min(bq, here)
    held = len(before)
    first = 2 * row
    part = lambda which: pl.BlockSpec((None, span, width), lambda t, p: (which, first + t, p))
    table = pl.BlockSpec((span, width), lambda t, p: (first + t, 0))
    return pl.pallas_call(
        functools.partial(attention_kernel, bq=bq, held=held),
        grid=(2, local // width),
        in_specs=[pl.BlockSpec(memory_space=pl.ANY)] * held
        + [
            pl.BlockSpec((1, span), lambda t, p: (0, first + t)),
            part(0),
            part(1),
            part(2),
            pl.BlockSpec((span, width), lambda t, p: (first + t, p)),
            table,
            table,
        ],
        out_specs=[
            pl.BlockSpec((span, width), lambda t, p: (first + t, p)),
            pl.BlockSpec((owners // 2, None, here, width), lambda t, p: (t, row, 0, p)),
            pl.BlockSpec((3, span, width), lambda t, p: (0, first + t, p)),
        ],
        out_shape=[
            jax.ShapeDtypeStruct((n, local), bf16),
            jax.ShapeDtypeStruct((owners, n // (2 * span), here, local), bf16),
            jax.ShapeDtypeStruct((3, n, local), bf16),
        ],
        scratch_shapes=[pltpu.VMEM((span, width), f32)] * 2,
        input_output_aliases={i: i for i in range(held)},
        compiler_params=params(),
        cost_estimate=SMALL,
        name="attention_both",
    )(*before, start, qkv, qkv, qkv, grad, cosine, sine)


def own_kernel(x_ref, w_ref, bd_ref, bo_ref, token_ref, *refs):
    *mlp_refs, o_ref, sum_ref = refs
    owners, seqs, here, local = x_ref.shape
    attention = jnp.zeros((seqs * here, w_ref.shape[1]), f32) + bd_ref[...]
    for owner in range(owners):
        x = x_ref[owner].reshape(seqs * here, local)
        attention += dot(x, w_ref[owner * local : (owner + 1) * local, :], 1, 0)
    tokens = token_ref[...].astype(f32)
    mlp = jnp.concatenate([a[...] for a in mlp_refs], axis=0).astype(f32) + bo_ref[...]
    total = tokens + attention + mlp
    o_ref[...] = total.astype(bf16)

    @pl.when(pl.program_id(0) == 0)
    def _():
        sum_ref[...] = jnp.zeros_like(sum_ref)

    for i, a in enumerate((tokens, attention, mlp, total)):
        sum_ref[i : i + 1, :] += jnp.sum(a * a, axis=0, keepdims=True)


def project_own(x, w, bd, bo, tokens, mlp_parts, tile=512, weight=1):
    owners, seqs, here, local = x.shape
    width = w.shape[1]
    rows = seqs * here
    column = lambda high: pl.BlockSpec((high, tile), lambda j: (0, j))
    return pl.pallas_call(
        own_kernel,
        grid=(width // tile,),
        in_specs=[
            pl.BlockSpec(x.shape, lambda j: (0, 0, 0, 0)),
            column(owners * local),
            column(1),
            column(1),
            column(rows),
        ]
        + [column(a.shape[0]) for a in mlp_parts],
        out_specs=[column(rows), pl.BlockSpec((8, tile), lambda j: (0, 0))],
        out_shape=[jax.ShapeDtypeStruct((rows, width), bf16), jax.ShapeDtypeStruct((8, tile), f32)],
        compiler_params=params(),
        cost_estimate=pl.CostEstimate(flops=int(weight), bytes_accessed=1, transcendentals=0),
        name="project_own",
    )(x, w, bd, bo, tokens, *mlp_parts)


def line_ok(size):
    return size >= 4 and size & (size - 1) == 0


class RowSum:
    def __init__(self, part, size):
        self.part, self.size, self.axis = part, size, "rows"
        groups = range(0, size, 4)
        pairs = lambda *ends: [(g + a, g + b) for g in groups for a, b in ends]
        self.hops = [pairs((0, 1), (3, 2)), pairs((1, 2), (2, 1))]
        hop = 4
        while hop < size:
            self.hops.append([(i, i ^ hop) for i in range(size)])
            hop *= 2
        self.hops.append(pairs((1, 0), (2, 3)))
        self.send()

    def send(self):
        if line_ok(self.size):
            self.came = lax.ppermute(self.part, self.axis, self.hops.pop(0))

    def fold(self, order):
        if line_ok(self.size) and self.hops:
            add = lambda a, b: (a.astype(f32) + b.astype(f32)).astype(a.dtype)
            self.part = order(add, self.part, self.came)
            self.send()

    def settle(self, order):
        if line_ok(self.size):
            self.came = order(lambda a: a, self.came)

    def complete(self, order):
        while self.hops:
            self.fold(order)

    def result(self, order=None):
        if not line_ok(self.size):
            return lax.psum(self.part.astype(f32), "rows")
        self.complete(order or Order())
        place = lax.axis_index("rows") % 4
        return jnp.where((place == 1) | (place == 2), self.part, self.came).astype(f32)


def finish_kernel(inner_ref, kept_ref, came_ref, *refs):
    o_ref = refs[-1]

    @pl.when(inner_ref[0] == 1)
    def _():
        o_ref[...] = kept_ref[...].astype(f32)

    @pl.when(inner_ref[0] == 0)
    def _():
        o_ref[...] = came_ref[...].astype(f32)


def finish(total, order, high, first=0, before=None, tile=512):
    flat = lambda a: a.reshape(-1, a.shape[-1])
    rows, cols = flat(total.part).shape
    if not line_ok(total.size):
        before = jnp.zeros((high, cols), f32) if before is None else before
        return lax.dynamic_update_slice(before, flat(total.result()), (first, 0))
    total.complete(order)
    tile = min(tile, rows)
    held = [] if before is None else [before]
    block = pl.BlockSpec((tile, cols), lambda j: (j, 0))
    place = lax.axis_index("rows") % 4
    inner = ((place == 1) | (place == 2)).astype(jnp.int32).reshape(1)
    call = pl.pallas_call(
        finish_kernel,
        grid=(rows // tile,),
        in_specs=[pl.BlockSpec(memory_space=pltpu.SMEM), block, block] + [pl.BlockSpec(memory_space=pl.ANY)] * len(held),
        out_specs=pl.BlockSpec((tile, cols), lambda j: (first // tile + j, 0)),
        out_shape=jax.ShapeDtypeStruct((high, cols), f32),
        input_output_aliases={3: 0} if held else {},
        compiler_params=params(),
        cost_estimate=SMALL,
        name="finish",
    )
    return order(lambda *a: call(inner, *a), flat(total.part), flat(total.came), *held)


class Gather:
    core, x, y = 1, 2, 4

    def __init__(self, first, second, size):
        self.first, self.second, self.size = first, second, size
        self.x0, self.y1 = self.send(first, self.x), self.send(second, self.y)

    def send(self, a, step):
        return lax.ppermute(a, "tp", [(i, i ^ step) for i in range(self.size)])

    def others(self, order=None):
        first, second = self.first, self.second
        if order:
            first, second = order(lambda a, b: (a, b), first, second)
        self.x1, self.y0 = self.send(second, self.x), self.send(first, self.y)
        self.c0 = self.send(first, self.core)

    def forward(self, order):
        came = (self.x0, self.y1, self.c0, self.second)
        self.x0, self.y1, self.c0, self.second = order(lambda *a: a, *came)
        self.c1 = self.send(self.second, self.core)
        self.d0, self.d1 = self.send(self.x0, self.y), self.send(self.y1, self.x)

    def pairs(self, order):
        came = (self.x0, self.y1, self.x1, self.y0, self.c1)
        self.x0, self.y1, self.x1, self.y0, self.c1 = order(lambda *a: a, *came)
        self.px0, self.py1 = self.send(self.x0, self.core), self.send(self.y1, self.core)
        self.px1, self.py0 = self.send(self.x1, self.core), self.send(self.y0, self.core)

    def near(self, order):
        steps = [step for step in (0, self.core, self.x, self.y, self.x | self.core, self.y | self.core) for _ in range(2)]
        pieces = (self.first, self.second, self.c0, self.c1, self.x0, self.x1, self.y0, self.y1)
        pieces += (self.px0, self.px1, self.py0, self.py1)
        self.full = order(lambda *a: place_pieces(None, a, steps, (0, 1) * 6, self.size), *pieces)

    def far_pairs(self, order):
        self.d0, self.d1 = order(lambda a, b: (a, b), self.d0, self.d1)
        self.pd0, self.pd1 = self.send(self.d0, self.core), self.send(self.d1, self.core)

    def far(self, order):
        far = self.x | self.y
        steps = (far, far, far | self.core, far | self.core)
        place = lambda full, *a: place_pieces(full, a, steps, (0, 1, 0, 1), self.size)
        self.full = order(place, self.full, self.d0, self.d1, self.pd0, self.pd1)
        return self.full


def place_kernel(me_ref, *refs, held):
    pieces, o_ref = refs[held:-1], refs[-1]
    for i, piece in enumerate(pieces):

        @pl.when(pl.program_id(0) == i)
        def _(piece=piece):
            o_ref[...] = piece[...].reshape(o_ref.shape)


def place_pieces(full, pieces, steps, halves, size):
    held = 0 if full is None else 1
    here, width = pieces[0].shape

    def target(j, me):
        device, half = me[0] ^ steps[0], halves[0]
        for i in range(1, len(pieces)):
            device = jnp.where(j == i, me[0] ^ steps[i], device)
            half = jnp.where(j == i, halves[i], half)
        return half, device, 0, 0

    hbm = pl.BlockSpec(memory_space=pl.ANY)
    me = lax.axis_index("tp").astype(jnp.int32).reshape(1)
    return pl.pallas_call(
        functools.partial(place_kernel, held=held),
        grid_spec=pltpu.PrefetchScalarGridSpec(
            num_scalar_prefetch=1,
            grid=(len(pieces),),
            in_specs=[hbm] * held + [pl.BlockSpec((here, width), lambda j, me: (0, 0))] * len(pieces),
            out_specs=pl.BlockSpec((1, None, here, width), target),
        ),
        out_shape=jax.ShapeDtypeStruct((2, size, here, width), bf16),
        input_output_aliases={1: 0} if held else {},
        compiler_params=params(),
        cost_estimate=SMALL,
        name="place_pieces",
    )(me, *([full] if held else []), *pieces)


class TpSum:
    def __init__(self, part, size):
        self.part, self.size, self.hop = part, size, 1
        self.send()

    def send(self):
        if self.size & (self.size - 1) == 0 and self.hop < self.size:
            self.came = lax.ppermute(self.part, "tp", [(i, i ^ self.hop) for i in range(self.size)])

    def fold(self, order):
        if self.size & (self.size - 1):
            self.part, self.size = lax.psum(self.part, "tp"), 1
        elif self.hop < self.size:
            self.part = order(lambda a, b: a + b, self.part, self.came)
            self.hop *= 2
            self.send()

    def result(self, order):
        while self.hop < self.size:
            self.fold(order)
        return self.part


def body(
    tokens,
    segment_ids,
    positions,
    norm_gain,
    norm_shift,
    query_key_value_weight,
    b_qkv,
    dense_weight,
    b_dense,
    inward_weight,
    b_in,
    outward_weight,
    b_out,
    cotangent,
):
    rows, tp = lax.axis_size("rows"), lax.axis_size("tp")
    seqs, here, width = tokens.shape
    length = here * tp
    n = seqs * length
    local = query_key_value_weight.shape[2]
    tile = min(128, local)
    span = length // 2

    exchange = tp == 8 and seqs == 2

    order = Order()
    gain, shift = norm_gain.astype(f32), norm_shift.astype(f32)
    norm = lambda a: norm_halves(a.reshape(seqs * here, width), gain, shift)
    halves = order(norm, tokens)

    if exchange:
        gather_normed = Gather(*halves, tp)
        gather_normed.others()

    def tables(positions, weight):
        place = positions.reshape(n, 1)
        cosine, sine = rope_tables(place, tile)
        start = jnp.arange(n, dtype=jnp.int32)[None] % span - positions.reshape(1, n)
        return cosine, sine, start, jnp.transpose(weight, (1, 0, 2))

    cosine, sine, start, w3 = order(tables, positions, query_key_value_weight)
    in_bias_row = b_in.astype(f32)[None]
    token_rows = lambda a: a.reshape(n, a.shape[-1])
    later = lambda a: lax.all_gather(order(lambda b: b, a), "tp", axis=1, tiled=True).reshape(n, width)
    if exchange:
        gather_normed.forward(order)
        gather_normed.pairs(order)
        grad = later(cotangent)
        gather_normed.near(order)
        hidden_of = lambda *a: mlp_hidden_of(*a, tuple(range(6)))
        hidden = order(hidden_of, gather_normed.full, inward_weight, in_bias_row)
        gather_normed.far_pairs(order)
        normed_full = gather_normed.far(order)
        hidden_of = lambda x, w, b, *before: mlp_hidden_of(x, w, b, (6, 7), before)
        act, slope = order(hidden_of, normed_full, inward_weight, in_bias_row, *hidden)
    else:
        normed_full = jnp.concatenate(halves).reshape(seqs, here, width)
        normed_full = lax.all_gather(normed_full, "tp", axis=1).reshape(seqs, tp, here, width)
        grad = later(cotangent)
        hidden_of = lambda *a: mlp_hidden_of(*a, tuple(range(tp)))
        act, slope = order(hidden_of, normed_full, inward_weight, in_bias_row)
    normed, act, slope = token_rows(normed_full), token_rows(act), token_rows(slope)
    qkv = order(project_qkv, normed, w3, b_qkv.astype(f32), cosine, sine)
    dense_ready, _ = lax.optimization_barrier((dense_weight, act))
    dense_full = lax.all_gather(dense_ready, "tp", axis=0, tiled=True)
    o0 = RowSum(order(lambda *a: weight_grad(*a, 0, 2), act, grad), rows)
    o1 = RowSum(order(lambda *a: weight_grad(*a, 1, 2), act, grad), rows)
    row_sum = lambda parts: [RowSum(part, rows) for part in parts]
    hidden_grad, attended_grad, in_bias = order(grad_in, grad, outward_weight, dense_weight, slope)
    o0.fold(order)
    i0, i1 = row_sum(order(lambda a, b: weight_grad_rows(a, b, (1, 1)), normed, hidden_grad))
    mlp_part = order(lambda *a: tokens_by_weight(*a, 0, 1), act, outward_weight).reshape(seqs, length, width)
    mlp_tok = lax.psum_scatter(mlp_part, "tp", scatter_dimension=1, tiled=True).reshape(seqs * here, width)
    o1.fold(order)
    o0.fold(order)
    both = lambda row: lambda s, q, g, c, t, *before: attention_both(s, q, g, c, t, span, tp, row, before)
    attended, by_owner, dqkv = order(both(0), start, qkv, attended_grad, cosine, sine)
    i0.fold(order)
    for row in range(1, seqs):
        kept = (attended, by_owner, dqkv)
        attended, by_owner, dqkv = order(both(row), start, qkv, attended_grad, cosine, sine, *kept)
    mine = lax.all_to_all(by_owner, "tp", split_axis=0, concat_axis=0, tiled=True)
    o1.fold(order)
    o0.settle(order)
    qs, vs = row_sum(order(lambda a, b: weight_grad_parts(a, b, weight=EARLY_WEIGHT), normed, dqkv))
    units = in_bias.shape[1]
    back = lambda share: lambda *a: normed_grad(*a[:5], shift[None], share, 2, a[5:])
    i1.fold(order)
    i0.fold(order)
    part, bias_a, norm_a = order(back(0), hidden_grad, dqkv, inward_weight, w3, normed)
    o1.settle(order)
    part, bias_b, norm_b = order(back(1), hidden_grad, dqkv, inward_weight, w3, normed, part)
    back_tok = lax.psum_scatter(part.reshape(seqs, length, width), "tp", scatter_dimension=1, tiled=True)
    i1.fold(order)
    qs.fold(order)
    (ds,) = row_sum([order(weight_grad, attended, grad)])
    vs.fold(order)
    i0.settle(order)

    cols = width // tp

    def column_sums(grad):
        mine = lax.dynamic_slice_in_dim(grad, lax.axis_index("tp") * cols, cols, 1)
        return jnp.sum(mine.astype(f32), axis=0)

    out_bias = order(column_sums, grad)
    rows_of = lambda a: a.reshape(seqs * here, width)
    bias_rows = (b_dense.astype(f32)[None], b_out.astype(f32)[None])
    own = lambda x, w, t, *m: project_own(x, w, *bias_rows, rows_of(t), m, weight=ORDER_WEIGHT)
    layer_out, squares = order(own, mine, dense_full, tokens, mlp_tok)
    layer_out = layer_out.reshape(tokens.shape)

    def pack(norm_a, norm_b, squares):
        norm_sums = norm_a + norm_b
        squares = jnp.sum(squares[:4], axis=1)
        pad = jnp.zeros((124,), f32)
        return jnp.concatenate([norm_sums[0] / gain, norm_sums[1], squares, pad]).reshape(-1, 128)

    packed = TpSum(order(pack, norm_a, norm_b, squares), tp)
    ds.fold(order)
    packed.fold(order)
    qs.fold(order)
    packed.fold(order)
    qkv_bias = bias_a + bias_b
    small = jnp.concatenate([in_bias[0], qkv_bias[:, 0].reshape(-1), out_bias]).reshape(-1, 128)
    small = RowSum(jnp.concatenate([packed.result(order), small]), rows)
    vs.fold(order)
    small.fold(order)
    out_grad = finish(o0, order, units)
    out_grad = finish(o1, order, units, units // 2, out_grad)
    in_grad = finish(i0, order, width)
    ds.fold(order)
    small.fold(order)
    in_grad = finish(i1, order, width, width // 2, in_grad)
    qkv_grad = finish(qs, order, 3 * width)

    def norm_back(back_tok, tokens, cotangent):
        values = tokens.astype(f32)
        center = values - jnp.mean(values, axis=-1, keepdims=True)
        inverse = lax.rsqrt(jnp.mean(center * center, axis=-1, keepdims=True) + epsilon)
        unit = center * inverse
        unit_grad = back_tok.astype(f32) * gain
        mean_grad = jnp.mean(unit_grad, axis=-1, keepdims=True)
        mean_both = jnp.mean(unit_grad * unit, axis=-1, keepdims=True)
        value_grad = (unit_grad - mean_grad - unit * mean_both) * inverse
        return (cotangent.astype(f32) + value_grad).astype(bf16)

    input_grad = order(norm_back, back_tok, tokens, cotangent)
    qkv_grad = finish(vs, order, 3 * width, 2 * width, qkv_grad)
    qkv_grad = jnp.transpose(qkv_grad.reshape(3, width, local), (1, 0, 2))
    dense_grad = finish(ds, order, local)
    small = small.result().reshape(-1)
    slice_at = lambda a: lax.dynamic_slice_in_dim(a, lax.axis_index("tp") * cols, cols, 0)
    gain_grad, shift_grad = slice_at(small[:width]), slice_at(small[width : 2 * width])
    rms_values = jnp.sqrt(small[2 * width : 2 * width + 4] / (seqs * rows * length * width))
    small = small[2 * width + 128 :]
    in_bias_grad = small[:units]
    qkv_bias_grad = small[units : units + 3 * local].reshape(3, local)
    out_bias_grad = small[units + 3 * local :]

    return (
        layer_out,
        input_grad,
        gain_grad,
        shift_grad,
        qkv_grad,
        qkv_bias_grad,
        dense_grad,
        out_bias_grad,
        in_grad,
        in_bias_grad,
        out_grad,
        out_bias_grad,
        rms_values,
    )


def solution(mesh):
    in_specs = (
        P("rows", "tp", None),
        P("rows", None),
        P("rows", None),
        P(),
        P(),
        P(None, None, "tp"),
        P(None, "tp"),
        P("tp", None),
        P(),
        P(None, "tp"),
        P("tp"),
        P("tp", None),
        P(),
        P("rows", "tp", None),
    )
    out_specs = (
        P("rows", "tp", None),
        P("rows", "tp", None),
        P("tp"),
        P("tp"),
        P(None, None, "tp"),
        P(None, "tp"),
        P("tp", None),
        P("tp"),
        P(None, "tp"),
        P("tp"),
        P("tp", None),
        P("tp"),
        P(),
    )
    return jax.shard_map(body, mesh=mesh, in_specs=in_specs, out_specs=out_specs, check_vma=False)
```

```python
import functools

import jax
import jax.numpy as jnp
from jax import lax
from jax.experimental import pallas as pl
from jax.experimental.pallas import tpu as pltpu
from jax.sharding import PartitionSpec as P

HD = 64
ROT = 32
epsilon = 1e-05
big_negative = -1e30
rope_base = 10000.0
f32 = jnp.float32
bf16 = jnp.bfloat16
VMEM_LIMIT = 56 << 20
ORDER_WEIGHT = int(2.15e11)
EARLY_WEIGHT = int(2.2e11)


def dot(a, b, ca, cb):
    return lax.dot_general(a, b, (((ca,), (cb,)), ((), ())), preferred_element_type=f32)


SMALL = pl.CostEstimate(flops=1, bytes_accessed=1, transcendentals=0)


def params():
    return pltpu.CompilerParams(vmem_limit_bytes=VMEM_LIMIT)


class Order:
    def __init__(self):
        self.last = ()

    def __call__(self, op, *operands):
        operands, _ = lax.optimization_barrier((operands, self.last))
        result = op(*operands)
        self.last = jax.tree.leaves(result)
        return result


def rope_swap(x):
    width = x.shape[-1]
    lane = lax.broadcasted_iota(jnp.int32, (1, width), 1) % HD
    up = pltpu.roll(x, width - ROT // 2, 1)
    down = pltpu.roll(x, ROT // 2, 1)
    return jnp.where(lane < ROT // 2, up, -down)


def norm_kernel(x_ref, gain_ref, shift_ref, first_ref, second_ref, *, per):
    x = x_ref[...].astype(f32)
    center = x - jnp.mean(x, axis=-1, keepdims=True)
    inverse = lax.rsqrt(jnp.mean(center * center, axis=-1, keepdims=True) + epsilon)
    out = (center * inverse * gain_ref[...] + shift_ref[...]).astype(bf16)

    @pl.when(pl.program_id(0) < per)
    def _():
        first_ref[...] = out

    @pl.when(pl.program_id(0) >= per)
    def _():
        second_ref[...] = out


def norm_halves(x, gain, shift, tm=128):
    n, width = x.shape
    per = n // 2 // tm
    vector = pl.BlockSpec((1, width), lambda i: (0, 0))
    return pl.pallas_call(
        functools.partial(norm_kernel, per=per),
        grid=(2 * per,),
        in_specs=[pl.BlockSpec((tm, width), lambda i: (i, 0)), vector, vector],
        out_specs=[
            pl.BlockSpec((tm, width), lambda i: (jnp.minimum(i, per - 1), 0)),
            pl.BlockSpec((tm, width), lambda i: (jnp.maximum(i - per, 0), 0)),
        ],
        out_shape=[jax.ShapeDtypeStruct((n // 2, width), bf16)] * 2,
        compiler_params=params(),
        cost_estimate=SMALL,
        name="norm_halves",
    )(x, gain[None], shift[None])


def table_kernel(place_ref, frequency_ref, c_ref, s_ref):
    angle = place_ref[...].astype(f32) * frequency_ref[...]
    lane = lax.broadcasted_iota(jnp.int32, angle.shape, 1) % HD
    turned = lane < ROT
    c_ref[...] = jnp.where(turned, jnp.cos(angle), 1.0)
    s_ref[...] = jnp.where(turned, jnp.sin(angle), 0.0)


def rope_tables(place, tile, tm=1024):
    n = place.shape[0]
    lane = jnp.arange(tile, dtype=jnp.int32) % (ROT // 2)
    frequency = (rope_base ** (-2.0 * lane.astype(f32) / ROT))[None]
    table = pl.BlockSpec((tm, tile), lambda i: (i, 0))
    return pl.pallas_call(
        table_kernel,
        grid=(n // tm,),
        in_specs=[pl.BlockSpec((tm, 1), lambda i: (i, 0)), pl.BlockSpec((1, tile), lambda i: (0, 0))],
        out_specs=[table, table],
        out_shape=[jax.ShapeDtypeStruct((n, tile), f32)] * 2,
        compiler_params=params(),
        cost_estimate=SMALL,
        name="rope_tables",
    )(place, frequency)


def qkv_kernel(x_ref, w_ref, b_ref, c_ref, s_ref, o_ref):
    x = x_ref[...]
    tile = c_ref.shape[-1]
    local = w_ref.shape[-1]
    cosine, sine = c_ref[...], s_ref[...]
    for part in range(3):
        full = dot(x, w_ref[part], 1, 0) + b_ref[part : part + 1, :]
        for at in range(0, local, tile):
            piece = full[:, at : at + tile]
            if part < 2:
                piece = piece * cosine - rope_swap(piece) * sine
            if part == 0:
                piece = piece * (HD**-0.5)
            o_ref[part, :, at : at + tile] = piece.astype(bf16)


def project_qkv(x, w3, bias, cosine, sine, tm=512):
    n, width = x.shape
    local = w3.shape[2]
    tile = cosine.shape[1]
    return pl.pallas_call(
        qkv_kernel,
        grid=(n // tm,),
        in_specs=[
            pl.BlockSpec((tm, width), lambda i: (i, 0)),
            pl.BlockSpec((3, width, local), lambda i: (0, 0, 0)),
            pl.BlockSpec((3, local), lambda i: (0, 0)),
            pl.BlockSpec((tm, tile), lambda i: (i, 0)),
            pl.BlockSpec((tm, tile), lambda i: (i, 0)),
        ],
        out_specs=pl.BlockSpec((3, tm, local), lambda i: (0, i, 0)),
        out_shape=jax.ShapeDtypeStruct((3, n, local), bf16),
        compiler_params=params(),
        cost_estimate=SMALL,
        name="qkv_rope",
    )(x, w3, bias, cosine, sine)


def chosen_kernel(me_ref, *refs, held):
    x_ref, w_ref, b_ref, act_ref, slope_ref = refs[held:]
    seqs, here, width = x_ref.shape
    x = x_ref[...].reshape(seqs * here, width)
    units = w_ref.shape[1]
    step = min(256, units)
    for at in range(0, units, step):
        cut = slice(at, at + step)
        h = dot(x, w_ref[:, cut], 1, 0) + b_ref[:, cut]
        square = h * h
        t = jnp.tanh(h * (0.7978845608028654 + 0.035677408136300125 * square))
        half = 0.5 + 0.5 * t
        act = h * half
        slope = half + (act - act * half) * (1.5957691216057308 + 0.21406444881780074 * square)
        act_ref[:, :, cut] = act.astype(bf16).reshape(seqs, here, step)
        slope_ref[:, :, cut] = slope.astype(bf16).reshape(seqs, here, step)


def mlp_hidden_of(x, w, bias, steps, before=(), weight=1):
    seqs, owners, here, width = x.shape
    units = w.shape[1]
    held = len(before)

    def device(j, me):
        chosen = me[0] ^ steps[0]
        for i in range(1, len(steps)):
            chosen = jnp.where(j == i, me[0] ^ steps[i], chosen)
        return 0, chosen, 0, 0

    out = pl.BlockSpec((seqs, None, here, units), device)
    me = lax.axis_index("tp").astype(jnp.int32).reshape(1)
    return pl.pallas_call(
        functools.partial(chosen_kernel, held=held),
        grid_spec=pltpu.PrefetchScalarGridSpec(
            num_scalar_prefetch=1,
            grid=(len(steps),),
            in_specs=[pl.BlockSpec(memory_space=pl.ANY)] * held
            + [
                pl.BlockSpec((seqs, None, here, width), device),
                pl.BlockSpec((width, units), lambda j, me: (0, 0)),
                pl.BlockSpec((1, units), lambda j, me: (0, 0)),
            ],
            out_specs=[out, out],
        ),
        out_shape=[jax.ShapeDtypeStruct((seqs, owners, here, units), bf16)] * 2,
        input_output_aliases={1 + i: i for i in range(held)},
        compiler_params=params(),
        cost_estimate=pl.CostEstimate(flops=int(weight), bytes_accessed=1, transcendentals=0),
        name="mlp_hidden_of",
    )(me, *before, x, w, bias)


def grad_in_kernel(g_ref, wo_ref, wd_ref, slope_ref, hg_ref, at_ref, sum_ref):
    g = g_ref[...]
    units = wo_ref.shape[0]
    step = min(256, units)

    @pl.when(pl.program_id(0) == 0)
    def _():
        sum_ref[...] = jnp.zeros_like(sum_ref)

    for at in range(0, units, step):
        slope = slope_ref[:, at : at + step].astype(f32)
        hg = (dot(g, wo_ref[at : at + step, :], 1, 1) * slope).astype(bf16)
        hg_ref[:, at : at + step] = hg
        sum_ref[0:1, at : at + step] += jnp.sum(hg.astype(f32), axis=0, keepdims=True)
    at_ref[...] = dot(g, wd_ref[...], 1, 1).astype(bf16)


def grad_in(g, wo, wd, slope, tm=512):
    n, width = g.shape
    units, local = wo.shape[0], wd.shape[0]
    return pl.pallas_call(
        grad_in_kernel,
        grid=(n // tm,),
        in_specs=[
            pl.BlockSpec((tm, width), lambda i: (i, 0)),
            pl.BlockSpec((units, width), lambda i: (0, 0)),
            pl.BlockSpec((local, width), lambda i: (0, 0)),
            pl.BlockSpec((tm, units), lambda i: (i, 0)),
        ],
        out_specs=[
            pl.BlockSpec((tm, units), lambda i: (i, 0)),
            pl.BlockSpec((tm, local), lambda i: (i, 0)),
            pl.BlockSpec((8, units), lambda i: (0, 0)),
        ],
        out_shape=[
            jax.ShapeDtypeStruct((n, units), bf16),
            jax.ShapeDtypeStruct((n, local), bf16),
            jax.ShapeDtypeStruct((8, units), f32),
        ],
        compiler_params=params(),
        cost_estimate=SMALL,
        name="grad_in",
    )(g, wo, wd, slope)


def tokens_kernel(x_ref, w_ref, o_ref):
    width = w_ref.shape[1]
    step = min(512, width)
    for at in range(0, width, step):
        o_ref[:, at : at + step] = dot(x_ref[...], w_ref[:, at : at + step], 1, 0).astype(o_ref.dtype)


def tokens_by_weight(x, w, share, shares, tm=512):
    n, depth = x.shape
    n //= shares
    width = w.shape[1]
    first = share * (n // tm)
    return pl.pallas_call(
        tokens_kernel,
        grid=(n // tm,),
        in_specs=[pl.BlockSpec((tm, depth), lambda i: (first + i, 0)), pl.BlockSpec((depth, width), lambda i: (0, 0))],
        out_specs=pl.BlockSpec((tm, width), lambda i: (i, 0)),
        out_shape=jax.ShapeDtypeStruct((n, width), bf16),
        compiler_params=params(),
        cost_estimate=SMALL,
        name="tokens_by_weight",
    )(x, w)


def weight_grad_kernel(a_ref, b_ref, o_ref):
    o_ref[...] = dot(a_ref[...], b_ref[...], 0, 0).astype(bf16)


def weight_grad(a, b, share=0, shares=1, tile=512, weight=1):
    n, rows = a.shape
    rows //= shares
    cols = b.shape[1]
    tile = min(tile, cols)
    return pl.pallas_call(
        weight_grad_kernel,
        grid=(cols // tile,),
        in_specs=[
            pl.BlockSpec((n, rows), lambda j: (0, share), pipeline_mode=pl.Buffered(1)),
            pl.BlockSpec((n, tile), lambda j: (0, j)),
        ],
        out_specs=pl.BlockSpec((rows, tile), lambda j: (0, j)),
        out_shape=jax.ShapeDtypeStruct((rows, cols), bf16),
        compiler_params=params(),
        cost_estimate=pl.CostEstimate(flops=int(weight), bytes_accessed=1, transcendentals=0),
        name="weight_grad",
    )(a, b)


def weight_grad_rows_kernel(a_ref, b_ref, *o_refs, counts):
    full = dot(a_ref[...], b_ref[...], 0, 0).astype(bf16)
    step = pl.program_id(0)
    first = 0
    for o_ref, count in zip(o_refs, counts):

        @pl.when((step >= first) & (step < first + count))
        def _(o_ref=o_ref):
            o_ref[...] = full

        first += count


def weight_grad_rows(a, b, shares, tile=512):
    n, rows = a.shape
    cols = b.shape[1]
    counts = [rows * share // sum(shares) // tile for share in shares]
    firsts = [sum(counts[:i]) for i in range(len(counts))]
    out = lambda i: pl.BlockSpec((tile, cols), lambda j: (jnp.clip(j - firsts[i], 0, counts[i] - 1), 0))
    return pl.pallas_call(
        functools.partial(weight_grad_rows_kernel, counts=counts),
        grid=(rows // tile,),
        in_specs=[
            pl.BlockSpec((n, tile), lambda j: (0, j)),
            pl.BlockSpec((n, cols), lambda j: (0, 0), pipeline_mode=pl.Buffered(1)),
        ],
        out_specs=[out(i) for i in range(len(counts))],
        out_shape=[jax.ShapeDtypeStruct((count * tile, cols), bf16) for count in counts],
        compiler_params=params(),
        cost_estimate=SMALL,
        name="weight_grad_rows",
    )(a, b)


def weight_grad_parts_kernel(a_ref, b_ref, first_ref, last_ref):
    for part in range(2):
        first_ref[part] = dot(a_ref[...], b_ref[part], 0, 0).astype(bf16)
    last_ref[...] = dot(a_ref[...], b_ref[2], 0, 0).astype(bf16)


def weight_grad_parts(a, b, tile=512, weight=1):
    n, rows = a.shape
    parts, _, cols = b.shape
    return pl.pallas_call(
        weight_grad_parts_kernel,
        grid=(rows // tile,),
        in_specs=[
            pl.BlockSpec((n, tile), lambda j: (0, j)),
            pl.BlockSpec((parts, n, cols), lambda j: (0, 0, 0), pipeline_mode=pl.Buffered(1)),
        ],
        out_specs=[pl.BlockSpec((2, tile, cols), lambda j: (0, j, 0)), pl.BlockSpec((tile, cols), lambda j: (j, 0))],
        out_shape=[jax.ShapeDtypeStruct((2, rows, cols), bf16), jax.ShapeDtypeStruct((rows, cols), bf16)],
        compiler_params=params(),
        cost_estimate=pl.CostEstimate(flops=int(weight), bytes_accessed=1, transcendentals=0),
        name="weight_grad_parts",
    )(a, b)


def normed_grad_kernel(*refs, held):
    hg_ref, dq_ref, wi_ref, w3_ref, x_ref, shift_ref, o_ref, sum_ref, norm_ref = refs[held:]

    @pl.when(pl.program_id(0) == 0)
    def _():
        sum_ref[...] = jnp.zeros_like(sum_ref)
        norm_ref[...] = jnp.zeros_like(norm_ref)

    for part in range(3):
        sum_ref[part, 0:1] += jnp.sum(dq_ref[part].astype(f32), axis=0, keepdims=True)
    width = o_ref.shape[1]
    step = min(512, width)
    for at in range(0, width, step):
        cut = slice(at, at + step)
        total = dot(hg_ref[...], wi_ref[cut, :], 1, 1)
        for part in range(3):
            total += dot(dq_ref[part], w3_ref[part, cut, :], 1, 1)
        o_ref[:, cut] = total.astype(bf16)
        scaled = x_ref[:, cut].astype(f32) - shift_ref[:, cut]
        norm_ref[0:1, cut] += jnp.sum(total * scaled, axis=0, keepdims=True)
        norm_ref[1:2, cut] += jnp.sum(total, axis=0, keepdims=True)


def normed_grad(hg, dqkv, wi, w3, x, shift, share, shares, before=(), tm=512):
    n, units = hg.shape
    held = len(before)
    steps = n // shares // tm
    first = share * steps
    width, local = w3.shape[1:]
    return pl.pallas_call(
        functools.partial(normed_grad_kernel, held=held),
        grid=(steps,),
        in_specs=[pl.BlockSpec(memory_space=pl.ANY)] * held
        + [
            pl.BlockSpec((tm, units), lambda i: (first + i, 0)),
            pl.BlockSpec((3, tm, local), lambda i: (0, first + i, 0)),
            pl.BlockSpec((width, units), lambda i: (0, 0)),
            pl.BlockSpec((3, width, local), lambda i: (0, 0, 0)),
            pl.BlockSpec((tm, width), lambda i: (first + i, 0)),
            pl.BlockSpec((1, width), lambda i: (0, 0)),
        ],
        out_specs=[
            pl.BlockSpec((tm, width), lambda i: (first + i, 0)),
            pl.BlockSpec((3, 8, local), lambda i: (0, 0, 0)),
            pl.BlockSpec((8, width), lambda i: (0, 0)),
        ],
        out_shape=[
            jax.ShapeDtypeStruct((n, width), bf16),
            jax.ShapeDtypeStruct((3, 8, local), f32),
            jax.ShapeDtypeStruct((8, width), f32),
        ],
        input_output_aliases={i: i for i in range(held)},
        compiler_params=params(),
        cost_estimate=SMALL,
        name="normed_grad",
    )(*before, hg, dqkv, wi, w3, x, shift)


def attention_kernel(*refs, bq, held):
    start_ref, q_ref, k_ref, v_ref, do_ref, c_ref, s_ref, o_ref, by_owner_ref, g_ref, dk_acc, dv_acc = refs[held:]
    span, width = q_ref.shape
    here = by_owner_ref.shape[1]
    lane = lax.broadcasted_iota(jnp.int32, (1, width), 1) // HD
    zero = jnp.zeros((), bf16)
    heads = range(width // HD)
    cuts = [slice(head * HD, (head + 1) * HD) for head in heads]
    blocks = span // bq
    keys_across, vals_across = k_ref[...].T, v_ref[...].T

    def turn_back(x, at, n):
        return x * c_ref[at : at + n, :] + rope_swap(x) * s_ref[at : at + n, :]

    def products(block):
        at, n = block * bq, (block + 1) * bq
        keys, vals = k_ref[0:n, :], v_ref[0:n, :]
        queries = [jnp.where(lane == head, q_ref[at:n, :], zero) for head in heads]
        grads = [jnp.where(lane == head, do_ref[at:n, :], zero) for head in heads]
        return queries, grads, [dot(keys, q, 1, 1) for q in queries], [dot(vals, g, 1, 1) for g in grads]

    ahead = products(0)
    for block in range(blocks):
        at, n = block * bq, (block + 1) * bq
        queries, grads, scores, prob_grads = ahead
        key = lax.broadcasted_iota(jnp.int32, (n, bq), 0)
        place = lax.broadcasted_iota(jnp.int32, (1, bq), 1) + at
        allowed = (key >= start_ref[:, at:n]) & (key <= place)
        if block + 1 < blocks:
            ahead = products(block + 1)
        probs = []
        for head in heads:
            score = jnp.where(allowed, scores[head], big_negative)
            expd = jnp.exp(score - jnp.max(score, axis=0, keepdims=True))
            probs.append(expd * (1.0 / jnp.sum(expd, axis=0, keepdims=True)))
        low = [p.astype(bf16) for p in probs]
        out = [dot(vals_across[cut, 0:n], p, 1, 0) for cut, p in zip(cuts, low)]
        dv = sum(dot(p, g, 1, 0) for p, g in zip(low, grads))
        score_grads = []
        for p, g in zip(probs, prob_grads):
            both = p * g
            score_grads.append((both - p * jnp.sum(both, axis=0, keepdims=True)).astype(bf16))
        dq = [dot(keys_across[cut, 0:n], g, 1, 0) for cut, g in zip(cuts, score_grads)]
        dk = sum(dot(g, q, 1, 0) for g, q in zip(score_grads, queries))
        out = jnp.concatenate(out, axis=0).T.astype(bf16)
        o_ref[at:n, :] = out
        by_owner_ref[at // here, at % here : at % here + bq] = out
        g_ref[0, at:n, :] = turn_back(jnp.concatenate(dq, axis=0).T * (HD**-0.5), at, bq).astype(bf16)
        if block:
            dk_acc[0:at, :] += dk[0:at]
            dv_acc[0:at, :] += dv[0:at]
        dk_acc[at:n, :] = dk[at:n]
        dv_acc[at:n, :] = dv[at:n]
    g_ref[1] = turn_back(dk_acc[...], 0, span).astype(bf16)
    g_ref[2] = dv_acc[...].astype(bf16)


def attention_both(start, qkv, grad, cosine, sine, span, owners, row, before=(), bq=128):
    n, local = grad.shape
    here = 2 * span // owners
    width = cosine.shape[1]
    bq = min(bq, here)
    held = len(before)
    first = 2 * row
    part = lambda which: pl.BlockSpec((None, span, width), lambda t, p: (which, first + t, p))
    table = pl.BlockSpec((span, width), lambda t, p: (first + t, 0))
    return pl.pallas_call(
        functools.partial(attention_kernel, bq=bq, held=held),
        grid=(2, local // width),
        in_specs=[pl.BlockSpec(memory_space=pl.ANY)] * held
        + [
            pl.BlockSpec((1, span), lambda t, p: (0, first + t)),
            part(0),
            part(1),
            part(2),
            pl.BlockSpec((span, width), lambda t, p: (first + t, p)),
            table,
            table,
        ],
        out_specs=[
            pl.BlockSpec((span, width), lambda t, p: (first + t, p)),
            pl.BlockSpec((owners // 2, None, here, width), lambda t, p: (t, row, 0, p)),
            pl.BlockSpec((3, span, width), lambda t, p: (0, first + t, p)),
        ],
        out_shape=[
            jax.ShapeDtypeStruct((n, local), bf16),
            jax.ShapeDtypeStruct((owners, n // (2 * span), here, local), bf16),
            jax.ShapeDtypeStruct((3, n, local), bf16),
        ],
        scratch_shapes=[pltpu.VMEM((span, width), f32)] * 2,
        input_output_aliases={i: i for i in range(held)},
        compiler_params=params(),
        cost_estimate=SMALL,
        name="attention_both",
    )(*before, start, qkv, qkv, qkv, grad, cosine, sine)


def own_kernel(x_ref, w_ref, bd_ref, bo_ref, token_ref, *refs):
    *mlp_refs, o_ref, sum_ref = refs
    owners, seqs, here, local = x_ref.shape
    attention = jnp.zeros((seqs * here, w_ref.shape[1]), f32) + bd_ref[...]
    for owner in range(owners):
        x = x_ref[owner].reshape(seqs * here, local)
        attention += dot(x, w_ref[owner * local : (owner + 1) * local, :], 1, 0)
    tokens = token_ref[...].astype(f32)
    mlp = jnp.concatenate([a[...] for a in mlp_refs], axis=0).astype(f32) + bo_ref[...]
    total = tokens + attention + mlp
    o_ref[...] = total.astype(bf16)

    @pl.when(pl.program_id(0) == 0)
    def _():
        sum_ref[...] = jnp.zeros_like(sum_ref)

    for i, a in enumerate((tokens, attention, mlp, total)):
        sum_ref[i : i + 1, :] += jnp.sum(a * a, axis=0, keepdims=True)


def project_own(x, w, bd, bo, tokens, mlp_parts, tile=512, weight=1):
    owners, seqs, here, local = x.shape
    width = w.shape[1]
    rows = seqs * here
    column = lambda high: pl.BlockSpec((high, tile), lambda j: (0, j))
    return pl.pallas_call(
        own_kernel,
        grid=(width // tile,),
        in_specs=[
            pl.BlockSpec(x.shape, lambda j: (0, 0, 0, 0)),
            column(owners * local),
            column(1),
            column(1),
            column(rows),
        ]
        + [column(a.shape[0]) for a in mlp_parts],
        out_specs=[column(rows), pl.BlockSpec((8, tile), lambda j: (0, 0))],
        out_shape=[jax.ShapeDtypeStruct((rows, width), bf16), jax.ShapeDtypeStruct((8, tile), f32)],
        compiler_params=params(),
        cost_estimate=pl.CostEstimate(flops=int(weight), bytes_accessed=1, transcendentals=0),
        name="project_own",
    )(x, w, bd, bo, tokens, *mlp_parts)


def line_ok(size):
    return size >= 4 and size & (size - 1) == 0


class RowSum:
    def __init__(self, part, size):
        self.part, self.size, self.axis = part, size, "rows"
        groups = range(0, size, 4)
        pairs = lambda *ends: [(g + a, g + b) for g in groups for a, b in ends]
        self.hops = [pairs((0, 1), (3, 2)), pairs((1, 2), (2, 1))]
        hop = 4
        while hop < size:
            self.hops.append([(i, i ^ hop) for i in range(size)])
            hop *= 2
        self.hops.append(pairs((1, 0), (2, 3)))
        self.send()

    def send(self):
        if line_ok(self.size):
            self.came = lax.ppermute(self.part, self.axis, self.hops.pop(0))

    def fold(self, order):
        if line_ok(self.size) and self.hops:
            add = lambda a, b: (a.astype(f32) + b.astype(f32)).astype(a.dtype)
            self.part = order(add, self.part, self.came)
            self.send()

    def settle(self, order):
        if line_ok(self.size):
            self.came = order(lambda a: a, self.came)

    def complete(self, order):
        while self.hops:
            self.fold(order)

    def result(self, order=None):
        if not line_ok(self.size):
            return lax.psum(self.part.astype(f32), "rows")
        self.complete(order or Order())
        place = lax.axis_index("rows") % 4
        return jnp.where((place == 1) | (place == 2), self.part, self.came).astype(f32)


def finish_kernel(inner_ref, kept_ref, came_ref, *refs):
    o_ref = refs[-1]

    @pl.when(inner_ref[0] == 1)
    def _():
        o_ref[...] = kept_ref[...].astype(f32)

    @pl.when(inner_ref[0] == 0)
    def _():
        o_ref[...] = came_ref[...].astype(f32)


def finish(total, order, high, first=0, before=None, tile=512, weight=1):
    flat = lambda a: a.reshape(-1, a.shape[-1])
    rows, cols = flat(total.part).shape
    if not line_ok(total.size):
        before = jnp.zeros((high, cols), f32) if before is None else before
        return lax.dynamic_update_slice(before, flat(total.result()), (first, 0))
    total.complete(order)
    tile = min(tile, rows)
    held = [] if before is None else [before]
    block = pl.BlockSpec((tile, cols), lambda j: (j, 0))
    place = lax.axis_index("rows") % 4
    inner = ((place == 1) | (place == 2)).astype(jnp.int32).reshape(1)
    call = pl.pallas_call(
        finish_kernel,
        grid=(rows // tile,),
        in_specs=[pl.BlockSpec(memory_space=pltpu.SMEM), block, block] + [pl.BlockSpec(memory_space=pl.ANY)] * len(held),
        out_specs=pl.BlockSpec((tile, cols), lambda j: (first // tile + j, 0)),
        out_shape=jax.ShapeDtypeStruct((high, cols), f32),
        input_output_aliases={3: 0} if held else {},
        compiler_params=params(),
        cost_estimate=pl.CostEstimate(flops=int(weight), bytes_accessed=1, transcendentals=0),
        name="finish",
    )
    return order(lambda *a: call(inner, *a), flat(total.part), flat(total.came), *held)


class Gather:
    core, x, y = 1, 2, 4

    def __init__(self, first, second, size):
        self.first, self.second, self.size = first, second, size
        self.x0, self.y1 = self.send(first, self.x), self.send(second, self.y)

    def send(self, a, step):
        return lax.ppermute(a, "tp", [(i, i ^ step) for i in range(self.size)])

    def others(self, order=None):
        first, second = self.first, self.second
        if order:
            first, second = order(lambda a, b: (a, b), first, second)
        self.x1, self.y0 = self.send(second, self.x), self.send(first, self.y)
        self.c0 = self.send(first, self.core)

    def forward(self, order):
        came = (self.x0, self.y1, self.c0, self.second)
        self.x0, self.y1, self.c0, self.second = order(lambda *a: a, *came)
        self.c1 = self.send(self.second, self.core)
        self.d0, self.d1 = self.send(self.x0, self.y), self.send(self.y1, self.x)

    def pairs(self, order):
        came = (self.x0, self.y1, self.x1, self.y0, self.c1)
        self.x0, self.y1, self.x1, self.y0, self.c1 = order(lambda *a: a, *came)
        self.px0, self.py1 = self.send(self.x0, self.core), self.send(self.y1, self.core)
        self.px1, self.py0 = self.send(self.x1, self.core), self.send(self.y0, self.core)

    def near(self, order):
        steps = [step for step in (0, self.core, self.x, self.y, self.x | self.core, self.y | self.core) for _ in range(2)]
        pieces = (self.first, self.second, self.c0, self.c1, self.x0, self.x1, self.y0, self.y1)
        pieces += (self.px0, self.px1, self.py0, self.py1)
        self.full = order(lambda *a: place_pieces(None, a, steps, (0, 1) * 6, self.size), *pieces)

    def far_pairs(self, order):
        self.d0, self.d1 = order(lambda a, b: (a, b), self.d0, self.d1)
        self.pd0, self.pd1 = self.send(self.d0, self.core), self.send(self.d1, self.core)

    def far(self, order):
        far = self.x | self.y
        steps = (far, far, far | self.core, far | self.core)
        place = lambda full, *a: place_pieces(full, a, steps, (0, 1, 0, 1), self.size)
        self.full = order(place, self.full, self.d0, self.d1, self.pd0, self.pd1)
        return self.full


def place_kernel(me_ref, *refs, held):
    pieces, o_ref = refs[held:-1], refs[-1]
    for i, piece in enumerate(pieces):

        @pl.when(pl.program_id(0) == i)
        def _(piece=piece):
            o_ref[...] = piece[...].reshape(o_ref.shape)


def place_pieces(full, pieces, steps, halves, size):
    held = 0 if full is None else 1
    here, width = pieces[0].shape

    def target(j, me):
        device, half = me[0] ^ steps[0], halves[0]
        for i in range(1, len(pieces)):
            device = jnp.where(j == i, me[0] ^ steps[i], device)
            half = jnp.where(j == i, halves[i], half)
        return half, device, 0, 0

    hbm = pl.BlockSpec(memory_space=pl.ANY)
    me = lax.axis_index("tp").astype(jnp.int32).reshape(1)
    return pl.pallas_call(
        functools.partial(place_kernel, held=held),
        grid_spec=pltpu.PrefetchScalarGridSpec(
            num_scalar_prefetch=1,
            grid=(len(pieces),),
            in_specs=[hbm] * held + [pl.BlockSpec((here, width), lambda j, me: (0, 0))] * len(pieces),
            out_specs=pl.BlockSpec((1, None, here, width), target),
        ),
        out_shape=jax.ShapeDtypeStruct((2, size, here, width), bf16),
        input_output_aliases={1: 0} if held else {},
        compiler_params=params(),
        cost_estimate=SMALL,
        name="place_pieces",
    )(me, *([full] if held else []), *pieces)


class TpSum:
    def __init__(self, part, size):
        self.part, self.size, self.hop = part, size, 1
        self.send()

    def send(self):
        if self.size & (self.size - 1) == 0 and self.hop < self.size:
            self.came = lax.ppermute(self.part, "tp", [(i, i ^ self.hop) for i in range(self.size)])

    def fold(self, order):
        if self.size & (self.size - 1):
            self.part, self.size = lax.psum(self.part, "tp"), 1
        elif self.hop < self.size:
            self.part = order(lambda a, b: a + b, self.part, self.came)
            self.hop *= 2
            self.send()

    def result(self, order):
        while self.hop < self.size:
            self.fold(order)
        return self.part


def body(
    tokens,
    segment_ids,
    positions,
    norm_gain,
    norm_shift,
    query_key_value_weight,
    b_qkv,
    dense_weight,
    b_dense,
    inward_weight,
    b_in,
    outward_weight,
    b_out,
    cotangent,
):
    rows, tp = lax.axis_size("rows"), lax.axis_size("tp")
    seqs, here, width = tokens.shape
    length = here * tp
    n = seqs * length
    local = query_key_value_weight.shape[2]
    tile = min(128, local)
    span = length // 2

    exchange = tp == 8 and seqs == 2

    order = Order()
    gain, shift = norm_gain.astype(f32), norm_shift.astype(f32)
    norm = lambda a: norm_halves(a.reshape(seqs * here, width), gain, shift)
    halves = order(norm, tokens)

    if exchange:
        gather_normed = Gather(*halves, tp)
        gather_normed.others()

    def tables(positions, weight):
        place = positions.reshape(n, 1)
        cosine, sine = rope_tables(place, tile)
        start = jnp.arange(n, dtype=jnp.int32)[None] % span - positions.reshape(1, n)
        return cosine, sine, start, jnp.transpose(weight, (1, 0, 2))

    cosine, sine, start, w3 = order(tables, positions, query_key_value_weight)
    in_bias_row = b_in.astype(f32)[None]
    token_rows = lambda a: a.reshape(n, a.shape[-1])
    later = lambda a: lax.all_gather(order(lambda b: b, a), "tp", axis=1, tiled=True).reshape(n, width)
    if exchange:
        gather_normed.forward(order)
        gather_normed.pairs(order)
        grad = later(cotangent)
        gather_normed.near(order)
        hidden_of = lambda *a: mlp_hidden_of(*a, tuple(range(6)))
        hidden = order(hidden_of, gather_normed.full, inward_weight, in_bias_row)
        gather_normed.far_pairs(order)
        normed_full = gather_normed.far(order)
        hidden_of = lambda x, w, b, *before: mlp_hidden_of(x, w, b, (6, 7), before)
        act, slope = order(hidden_of, normed_full, inward_weight, in_bias_row, *hidden)
    else:
        normed_full = jnp.concatenate(halves).reshape(seqs, here, width)
        normed_full = lax.all_gather(normed_full, "tp", axis=1).reshape(seqs, tp, here, width)
        grad = later(cotangent)
        hidden_of = lambda *a: mlp_hidden_of(*a, tuple(range(tp)))
        act, slope = order(hidden_of, normed_full, inward_weight, in_bias_row)
    normed, act, slope = token_rows(normed_full), token_rows(act), token_rows(slope)
    qkv = order(project_qkv, normed, w3, b_qkv.astype(f32), cosine, sine)
    dense_ready, _ = lax.optimization_barrier((dense_weight, act))
    dense_full = lax.all_gather(dense_ready, "tp", axis=0, tiled=True)
    o0 = RowSum(order(lambda *a: weight_grad(*a, 0, 2), act, grad), rows)
    o1 = RowSum(order(lambda *a: weight_grad(*a, 1, 2), act, grad), rows)
    row_sum = lambda parts: [RowSum(part, rows) for part in parts]
    hidden_grad, attended_grad, in_bias = order(grad_in, grad, outward_weight, dense_weight, slope)
    o0.fold(order)
    i0, i1 = row_sum(order(lambda a, b: weight_grad_rows(a, b, (1, 1)), normed, hidden_grad))
    mlp_part = order(lambda *a: tokens_by_weight(*a, 0, 1), act, outward_weight).reshape(seqs, length, width)
    mlp_tok = lax.psum_scatter(mlp_part, "tp", scatter_dimension=1, tiled=True).reshape(seqs * here, width)
    o1.fold(order)
    o0.fold(order)
    both = lambda row: lambda s, q, g, c, t, *before: attention_both(s, q, g, c, t, span, tp, row, before)
    attended, by_owner, dqkv = order(both(0), start, qkv, attended_grad, cosine, sine)
    i0.fold(order)
    for row in range(1, seqs):
        kept = (attended, by_owner, dqkv)
        attended, by_owner, dqkv = order(both(row), start, qkv, attended_grad, cosine, sine, *kept)
    mine = lax.all_to_all(by_owner, "tp", split_axis=0, concat_axis=0, tiled=True)
    o1.fold(order)
    o0.settle(order)
    qs, vs = row_sum(order(lambda a, b: weight_grad_parts(a, b, weight=EARLY_WEIGHT), normed, dqkv))
    units = in_bias.shape[1]
    back = lambda share: lambda *a: normed_grad(*a[:5], shift[None], share, 2, a[5:])
    i1.fold(order)
    i0.fold(order)
    part, bias_a, norm_a = order(back(0), hidden_grad, dqkv, inward_weight, w3, normed)
    o1.settle(order)
    i1.fold(order)
    qs.fold(order)
    part, bias_b, norm_b = order(back(1), hidden_grad, dqkv, inward_weight, w3, normed, part)
    back_tok = lax.psum_scatter(part.reshape(seqs, length, width), "tp", scatter_dimension=1, tiled=True)
    vs.fold(order)
    (ds,) = row_sum([order(weight_grad, attended, grad)])
    i0.settle(order)

    cols = width // tp

    def column_sums(grad):
        mine = lax.dynamic_slice_in_dim(grad, lax.axis_index("tp") * cols, cols, 1)
        return jnp.sum(mine.astype(f32), axis=0)

    out_bias = order(column_sums, grad)
    rows_of = lambda a: a.reshape(seqs * here, width)
    bias_rows = (b_dense.astype(f32)[None], b_out.astype(f32)[None])
    own = lambda x, w, t, *m: project_own(x, w, *bias_rows, rows_of(t), m)
    layer_out, squares = order(own, mine, dense_full, tokens, mlp_tok)
    layer_out = layer_out.reshape(tokens.shape)

    def pack(norm_a, norm_b, squares):
        norm_sums = norm_a + norm_b
        squares = jnp.sum(squares[:4], axis=1)
        pad = jnp.zeros((124,), f32)
        return jnp.concatenate([norm_sums[0] / gain, norm_sums[1], squares, pad]).reshape(-1, 128)

    i1.settle(order)
    packed = TpSum(order(pack, norm_a, norm_b, squares), tp)
    ds.fold(order)
    packed.fold(order)
    qs.fold(order)
    packed.fold(order)
    qkv_bias = bias_a + bias_b
    small = jnp.concatenate([in_bias[0], qkv_bias[:, 0].reshape(-1), out_bias]).reshape(-1, 128)
    small = RowSum(jnp.concatenate([packed.result(order), small]), rows)
    vs.fold(order)
    small.fold(order)
    ds.fold(order)
    out_grad = finish(o0, order, units, weight=ORDER_WEIGHT)
    out_grad = finish(o1, order, units, units // 2, out_grad)
    in_grad = finish(i0, order, width)
    small.fold(order)
    in_grad = finish(i1, order, width, width // 2, in_grad)
    qkv_grad = finish(qs, order, 3 * width)

    def norm_back(back_tok, tokens, cotangent):
        values = tokens.astype(f32)
        center = values - jnp.mean(values, axis=-1, keepdims=True)
        inverse = lax.rsqrt(jnp.mean(center * center, axis=-1, keepdims=True) + epsilon)
        unit = center * inverse
        unit_grad = back_tok.astype(f32) * gain
        mean_grad = jnp.mean(unit_grad, axis=-1, keepdims=True)
        mean_both = jnp.mean(unit_grad * unit, axis=-1, keepdims=True)
        value_grad = (unit_grad - mean_grad - unit * mean_both) * inverse
        return (cotangent.astype(f32) + value_grad).astype(bf16)

    input_grad = order(norm_back, back_tok, tokens, cotangent)
    qkv_grad = finish(vs, order, 3 * width, 2 * width, qkv_grad)
    qkv_grad = jnp.transpose(qkv_grad.reshape(3, width, local), (1, 0, 2))
    dense_grad = finish(ds, order, local)
    small = small.result().reshape(-1)
    slice_at = lambda a: lax.dynamic_slice_in_dim(a, lax.axis_index("tp") * cols, cols, 0)
    gain_grad, shift_grad = slice_at(small[:width]), slice_at(small[width : 2 * width])
    rms_values = jnp.sqrt(small[2 * width : 2 * width + 4] / (seqs * rows * length * width))
    small = small[2 * width + 128 :]
    in_bias_grad = small[:units]
    qkv_bias_grad = small[units : units + 3 * local].reshape(3, local)
    out_bias_grad = small[units + 3 * local :]

    return (
        layer_out,
        input_grad,
        gain_grad,
        shift_grad,
        qkv_grad,
        qkv_bias_grad,
        dense_grad,
        out_bias_grad,
        in_grad,
        in_bias_grad,
        out_grad,
        out_bias_grad,
        rms_values,
    )


def solution(mesh):
    in_specs = (
        P("rows", "tp", None),
        P("rows", None),
        P("rows", None),
        P(),
        P(),
        P(None, None, "tp"),
        P(None, "tp"),
        P("tp", None),
        P(),
        P(None, "tp"),
        P("tp"),
        P("tp", None),
        P(),
        P("rows", "tp", None),
    )
    out_specs = (
        P("rows", "tp", None),
        P("rows", "tp", None),
        P("tp"),
        P("tp"),
        P(None, None, "tp"),
        P(None, "tp"),
        P("tp", None),
        P("tp"),
        P(None, "tp"),
        P("tp"),
        P("tp", None),
        P("tp"),
        P(),
    )
    return jax.shard_map(body, mesh=mesh, in_specs=in_specs, out_specs=out_specs, check_vma=False)
```

```python
import functools

import jax
import jax.numpy as jnp
from jax import lax
from jax.experimental import pallas as pl
from jax.experimental.pallas import tpu as pltpu
from jax.sharding import PartitionSpec as P

HD = 64
ROT = 32
epsilon = 1e-05
big_negative = -1e30
rope_base = 10000.0
f32 = jnp.float32
bf16 = jnp.bfloat16
VMEM_LIMIT = 56 << 20
ORDER_WEIGHT = int(2.15e11)
EARLY_WEIGHT = int(2.2e11)


def dot(a, b, ca, cb):
    return lax.dot_general(a, b, (((ca,), (cb,)), ((), ())), preferred_element_type=f32)


SMALL = pl.CostEstimate(flops=1, bytes_accessed=1, transcendentals=0)


def params():
    return pltpu.CompilerParams(vmem_limit_bytes=VMEM_LIMIT)


class Order:
    def __init__(self):
        self.last = ()

    def __call__(self, op, *operands):
        operands, _ = lax.optimization_barrier((operands, self.last))
        result = op(*operands)
        self.last = jax.tree.leaves(result)
        return result


def rope_swap(x):
    width = x.shape[-1]
    lane = lax.broadcasted_iota(jnp.int32, (1, width), 1) % HD
    up = pltpu.roll(x, width - ROT // 2, 1)
    down = pltpu.roll(x, ROT // 2, 1)
    return jnp.where(lane < ROT // 2, up, -down)


def norm_kernel(x_ref, gain_ref, shift_ref, first_ref, second_ref, *, per):
    x = x_ref[...].astype(f32)
    center = x - jnp.mean(x, axis=-1, keepdims=True)
    inverse = lax.rsqrt(jnp.mean(center * center, axis=-1, keepdims=True) + epsilon)
    out = (center * inverse * gain_ref[...] + shift_ref[...]).astype(bf16)

    @pl.when(pl.program_id(0) < per)
    def _():
        first_ref[...] = out

    @pl.when(pl.program_id(0) >= per)
    def _():
        second_ref[...] = out


def norm_halves(x, gain, shift, tm=128):
    n, width = x.shape
    per = n // 2 // tm
    vector = pl.BlockSpec((1, width), lambda i: (0, 0))
    return pl.pallas_call(
        functools.partial(norm_kernel, per=per),
        grid=(2 * per,),
        in_specs=[pl.BlockSpec((tm, width), lambda i: (i, 0)), vector, vector],
        out_specs=[
            pl.BlockSpec((tm, width), lambda i: (jnp.minimum(i, per - 1), 0)),
            pl.BlockSpec((tm, width), lambda i: (jnp.maximum(i - per, 0), 0)),
        ],
        out_shape=[jax.ShapeDtypeStruct((n // 2, width), bf16)] * 2,
        compiler_params=params(),
        cost_estimate=SMALL,
        name="norm_halves",
    )(x, gain[None], shift[None])


def table_kernel(place_ref, frequency_ref, c_ref, s_ref):
    angle = place_ref[...].astype(f32) * frequency_ref[...]
    lane = lax.broadcasted_iota(jnp.int32, angle.shape, 1) % HD
    turned = lane < ROT
    c_ref[...] = jnp.where(turned, jnp.cos(angle), 1.0)
    s_ref[...] = jnp.where(turned, jnp.sin(angle), 0.0)


def rope_tables(place, tile, tm=1024):
    n = place.shape[0]
    lane = jnp.arange(tile, dtype=jnp.int32) % (ROT // 2)
    frequency = (rope_base ** (-2.0 * lane.astype(f32) / ROT))[None]
    table = pl.BlockSpec((tm, tile), lambda i: (i, 0))
    return pl.pallas_call(
        table_kernel,
        grid=(n // tm,),
        in_specs=[pl.BlockSpec((tm, 1), lambda i: (i, 0)), pl.BlockSpec((1, tile), lambda i: (0, 0))],
        out_specs=[table, table],
        out_shape=[jax.ShapeDtypeStruct((n, tile), f32)] * 2,
        compiler_params=params(),
        cost_estimate=SMALL,
        name="rope_tables",
    )(place, frequency)


def qkv_kernel(x_ref, w_ref, b_ref, c_ref, s_ref, o_ref):
    x = x_ref[...]
    tile = c_ref.shape[-1]
    local = w_ref.shape[-1]
    cosine, sine = c_ref[...], s_ref[...]
    for part in range(3):
        full = dot(x, w_ref[part], 1, 0) + b_ref[part : part + 1, :]
        for at in range(0, local, tile):
            piece = full[:, at : at + tile]
            if part < 2:
                piece = piece * cosine - rope_swap(piece) * sine
            if part == 0:
                piece = piece * (HD**-0.5)
            o_ref[part, :, at : at + tile] = piece.astype(bf16)


def project_qkv(x, w3, bias, cosine, sine, tm=512):
    n, width = x.shape
    local = w3.shape[2]
    tile = cosine.shape[1]
    return pl.pallas_call(
        qkv_kernel,
        grid=(n // tm,),
        in_specs=[
            pl.BlockSpec((tm, width), lambda i: (i, 0)),
            pl.BlockSpec((3, width, local), lambda i: (0, 0, 0)),
            pl.BlockSpec((3, local), lambda i: (0, 0)),
            pl.BlockSpec((tm, tile), lambda i: (i, 0)),
            pl.BlockSpec((tm, tile), lambda i: (i, 0)),
        ],
        out_specs=pl.BlockSpec((3, tm, local), lambda i: (0, i, 0)),
        out_shape=jax.ShapeDtypeStruct((3, n, local), bf16),
        compiler_params=params(),
        cost_estimate=SMALL,
        name="qkv_rope",
    )(x, w3, bias, cosine, sine)


def chosen_kernel(me_ref, *refs, held):
    x_ref, w_ref, b_ref, act_ref, slope_ref = refs[held:]
    seqs, here, width = x_ref.shape
    x = x_ref[...].reshape(seqs * here, width)
    units = w_ref.shape[1]
    step = min(256, units)
    for at in range(0, units, step):
        cut = slice(at, at + step)
        h = dot(x, w_ref[:, cut], 1, 0) + b_ref[:, cut]
        square = h * h
        t = jnp.tanh(h * (0.7978845608028654 + 0.035677408136300125 * square))
        half = 0.5 + 0.5 * t
        act = h * half
        slope = half + (act - act * half) * (1.5957691216057308 + 0.21406444881780074 * square)
        act_ref[:, :, cut] = act.astype(bf16).reshape(seqs, here, step)
        slope_ref[:, :, cut] = slope.astype(bf16).reshape(seqs, here, step)


def mlp_hidden_of(x, w, bias, steps, before=(), weight=1):
    seqs, owners, here, width = x.shape
    units = w.shape[1]
    held = len(before)

    def device(j, me):
        chosen = me[0] ^ steps[0]
        for i in range(1, len(steps)):
            chosen = jnp.where(j == i, me[0] ^ steps[i], chosen)
        return 0, chosen, 0, 0

    out = pl.BlockSpec((seqs, None, here, units), device)
    me = lax.axis_index("tp").astype(jnp.int32).reshape(1)
    return pl.pallas_call(
        functools.partial(chosen_kernel, held=held),
        grid_spec=pltpu.PrefetchScalarGridSpec(
            num_scalar_prefetch=1,
            grid=(len(steps),),
            in_specs=[pl.BlockSpec(memory_space=pl.ANY)] * held
            + [
                pl.BlockSpec((seqs, None, here, width), device),
                pl.BlockSpec((width, units), lambda j, me: (0, 0)),
                pl.BlockSpec((1, units), lambda j, me: (0, 0)),
            ],
            out_specs=[out, out],
        ),
        out_shape=[jax.ShapeDtypeStruct((seqs, owners, here, units), bf16)] * 2,
        input_output_aliases={1 + i: i for i in range(held)},
        compiler_params=params(),
        cost_estimate=pl.CostEstimate(flops=int(weight), bytes_accessed=1, transcendentals=0),
        name="mlp_hidden_of",
    )(me, *before, x, w, bias)


def grad_in_kernel(g_ref, wo_ref, wd_ref, slope_ref, hg_ref, at_ref, sum_ref):
    g = g_ref[...]
    units = wo_ref.shape[0]
    step = min(256, units)

    @pl.when(pl.program_id(0) == 0)
    def _():
        sum_ref[...] = jnp.zeros_like(sum_ref)

    for at in range(0, units, step):
        slope = slope_ref[:, at : at + step].astype(f32)
        hg = (dot(g, wo_ref[at : at + step, :], 1, 1) * slope).astype(bf16)
        hg_ref[:, at : at + step] = hg
        sum_ref[0:1, at : at + step] += jnp.sum(hg.astype(f32), axis=0, keepdims=True)
    at_ref[...] = dot(g, wd_ref[...], 1, 1).astype(bf16)


def grad_in(g, wo, wd, slope, tm=512):
    n, width = g.shape
    units, local = wo.shape[0], wd.shape[0]
    return pl.pallas_call(
        grad_in_kernel,
        grid=(n // tm,),
        in_specs=[
            pl.BlockSpec((tm, width), lambda i: (i, 0)),
            pl.BlockSpec((units, width), lambda i: (0, 0)),
            pl.BlockSpec((local, width), lambda i: (0, 0)),
            pl.BlockSpec((tm, units), lambda i: (i, 0)),
        ],
        out_specs=[
            pl.BlockSpec((tm, units), lambda i: (i, 0)),
            pl.BlockSpec((tm, local), lambda i: (i, 0)),
            pl.BlockSpec((8, units), lambda i: (0, 0)),
        ],
        out_shape=[
            jax.ShapeDtypeStruct((n, units), bf16),
            jax.ShapeDtypeStruct((n, local), bf16),
            jax.ShapeDtypeStruct((8, units), f32),
        ],
        compiler_params=params(),
        cost_estimate=SMALL,
        name="grad_in",
    )(g, wo, wd, slope)


def tokens_kernel(*refs, held):
    x_ref, w_ref, o_ref = refs[held:]
    width = w_ref.shape[1]
    step = min(512, width)
    for at in range(0, width, step):
        o_ref[:, at : at + step] = dot(x_ref[...], w_ref[:, at : at + step], 1, 0).astype(o_ref.dtype)


def tokens_by_weight(x, w, share, shares, before=(), tm=512):
    n, depth = x.shape
    held = len(before)
    steps = n // shares // tm
    width = w.shape[1]
    first = share * steps
    return pl.pallas_call(
        functools.partial(tokens_kernel, held=held),
        grid=(steps,),
        in_specs=[pl.BlockSpec(memory_space=pl.ANY)] * held
        + [pl.BlockSpec((tm, depth), lambda i: (first + i, 0)), pl.BlockSpec((depth, width), lambda i: (0, 0))],
        out_specs=pl.BlockSpec((tm, width), lambda i: (first + i, 0)),
        out_shape=jax.ShapeDtypeStruct((n, width), bf16),
        input_output_aliases={i: i for i in range(held)},
        compiler_params=params(),
        cost_estimate=SMALL,
        name="tokens_by_weight",
    )(*before, x, w)


def weight_grad_kernel(a_ref, b_ref, o_ref):
    o_ref[...] = dot(a_ref[...], b_ref[...], 0, 0).astype(bf16)


def weight_grad(a, b, share=0, shares=1, tile=512, weight=1):
    n, rows = a.shape
    rows //= shares
    cols = b.shape[1]
    tile = min(tile, cols)
    return pl.pallas_call(
        weight_grad_kernel,
        grid=(cols // tile,),
        in_specs=[
            pl.BlockSpec((n, rows), lambda j: (0, share), pipeline_mode=pl.Buffered(1)),
            pl.BlockSpec((n, tile), lambda j: (0, j)),
        ],
        out_specs=pl.BlockSpec((rows, tile), lambda j: (0, j)),
        out_shape=jax.ShapeDtypeStruct((rows, cols), bf16),
        compiler_params=params(),
        cost_estimate=pl.CostEstimate(flops=int(weight), bytes_accessed=1, transcendentals=0),
        name="weight_grad",
    )(a, b)


def weight_grad_rows_kernel(a_ref, b_ref, *o_refs, counts):
    full = dot(a_ref[...], b_ref[...], 0, 0).astype(bf16)
    step = pl.program_id(0)
    first = 0
    for o_ref, count in zip(o_refs, counts):

        @pl.when((step >= first) & (step < first + count))
        def _(o_ref=o_ref):
            o_ref[...] = full

        first += count


def weight_grad_rows(a, b, shares, tile=512):
    n, rows = a.shape
    cols = b.shape[1]
    counts = [rows * share // sum(shares) // tile for share in shares]
    firsts = [sum(counts[:i]) for i in range(len(counts))]
    out = lambda i: pl.BlockSpec((tile, cols), lambda j: (jnp.clip(j - firsts[i], 0, counts[i] - 1), 0))
    return pl.pallas_call(
        functools.partial(weight_grad_rows_kernel, counts=counts),
        grid=(rows // tile,),
        in_specs=[
            pl.BlockSpec((n, tile), lambda j: (0, j)),
            pl.BlockSpec((n, cols), lambda j: (0, 0), pipeline_mode=pl.Buffered(1)),
        ],
        out_specs=[out(i) for i in range(len(counts))],
        out_shape=[jax.ShapeDtypeStruct((count * tile, cols), bf16) for count in counts],
        compiler_params=params(),
        cost_estimate=SMALL,
        name="weight_grad_rows",
    )(a, b)


def weight_grad_parts_kernel(a_ref, b_ref, first_ref, last_ref):
    for part in range(2):
        first_ref[part] = dot(a_ref[...], b_ref[part], 0, 0).astype(bf16)
    last_ref[...] = dot(a_ref[...], b_ref[2], 0, 0).astype(bf16)


def weight_grad_parts(a, b, tile=512, weight=1):
    n, rows = a.shape
    parts, _, cols = b.shape
    return pl.pallas_call(
        weight_grad_parts_kernel,
        grid=(rows // tile,),
        in_specs=[
            pl.BlockSpec((n, tile), lambda j: (0, j)),
            pl.BlockSpec((parts, n, cols), lambda j: (0, 0, 0), pipeline_mode=pl.Buffered(1)),
        ],
        out_specs=[pl.BlockSpec((2, tile, cols), lambda j: (0, j, 0)), pl.BlockSpec((tile, cols), lambda j: (j, 0))],
        out_shape=[jax.ShapeDtypeStruct((2, rows, cols), bf16), jax.ShapeDtypeStruct((rows, cols), bf16)],
        compiler_params=params(),
        cost_estimate=pl.CostEstimate(flops=int(weight), bytes_accessed=1, transcendentals=0),
        name="weight_grad_parts",
    )(a, b)


def normed_grad_kernel(*refs, held):
    hg_ref, dq_ref, wi_ref, w3_ref, x_ref, shift_ref, o_ref, sum_ref, norm_ref = refs[held:]

    @pl.when(pl.program_id(0) == 0)
    def _():
        sum_ref[...] = jnp.zeros_like(sum_ref)
        norm_ref[...] = jnp.zeros_like(norm_ref)

    for part in range(3):
        sum_ref[part, 0:1] += jnp.sum(dq_ref[part].astype(f32), axis=0, keepdims=True)
    width = o_ref.shape[1]
    step = min(512, width)
    for at in range(0, width, step):
        cut = slice(at, at + step)
        total = dot(hg_ref[...], wi_ref[cut, :], 1, 1)
        for part in range(3):
            total += dot(dq_ref[part], w3_ref[part, cut, :], 1, 1)
        o_ref[:, cut] = total.astype(bf16)
        scaled = x_ref[:, cut].astype(f32) - shift_ref[:, cut]
        norm_ref[0:1, cut] += jnp.sum(total * scaled, axis=0, keepdims=True)
        norm_ref[1:2, cut] += jnp.sum(total, axis=0, keepdims=True)


def normed_grad(hg, dqkv, wi, w3, x, shift, share, shares, before=(), tm=512):
    n, units = hg.shape
    held = len(before)
    steps = n // shares // tm
    first = share * steps
    width, local = w3.shape[1:]
    return pl.pallas_call(
        functools.partial(normed_grad_kernel, held=held),
        grid=(steps,),
        in_specs=[pl.BlockSpec(memory_space=pl.ANY)] * held
        + [
            pl.BlockSpec((tm, units), lambda i: (first + i, 0)),
            pl.BlockSpec((3, tm, local), lambda i: (0, first + i, 0)),
            pl.BlockSpec((width, units), lambda i: (0, 0)),
            pl.BlockSpec((3, width, local), lambda i: (0, 0, 0)),
            pl.BlockSpec((tm, width), lambda i: (first + i, 0)),
            pl.BlockSpec((1, width), lambda i: (0, 0)),
        ],
        out_specs=[
            pl.BlockSpec((tm, width), lambda i: (first + i, 0)),
            pl.BlockSpec((3, 8, local), lambda i: (0, 0, 0)),
            pl.BlockSpec((8, width), lambda i: (0, 0)),
        ],
        out_shape=[
            jax.ShapeDtypeStruct((n, width), bf16),
            jax.ShapeDtypeStruct((3, 8, local), f32),
            jax.ShapeDtypeStruct((8, width), f32),
        ],
        input_output_aliases={i: i for i in range(held)},
        compiler_params=params(),
        cost_estimate=SMALL,
        name="normed_grad",
    )(*before, hg, dqkv, wi, w3, x, shift)


def attention_kernel(*refs, bq, held):
    start_ref, q_ref, k_ref, v_ref, do_ref, c_ref, s_ref, o_ref, by_owner_ref, g_ref, dk_acc, dv_acc = refs[held:]
    span, width = q_ref.shape
    here = by_owner_ref.shape[1]
    lane = lax.broadcasted_iota(jnp.int32, (1, width), 1) // HD
    zero = jnp.zeros((), bf16)
    heads = range(width // HD)
    cuts = [slice(head * HD, (head + 1) * HD) for head in heads]
    blocks = span // bq
    keys_across, vals_across = k_ref[...].T, v_ref[...].T

    def turn_back(x, at, n):
        return x * c_ref[at : at + n, :] + rope_swap(x) * s_ref[at : at + n, :]

    def products(block):
        at, n = block * bq, (block + 1) * bq
        keys, vals = k_ref[0:n, :], v_ref[0:n, :]
        queries = [jnp.where(lane == head, q_ref[at:n, :], zero) for head in heads]
        grads = [jnp.where(lane == head, do_ref[at:n, :], zero) for head in heads]
        return queries, grads, [dot(keys, q, 1, 1) for q in queries], [dot(vals, g, 1, 1) for g in grads]

    ahead = products(0)
    for block in range(blocks):
        at, n = block * bq, (block + 1) * bq
        queries, grads, scores, prob_grads = ahead
        key = lax.broadcasted_iota(jnp.int32, (n, bq), 0)
        place = lax.broadcasted_iota(jnp.int32, (1, bq), 1) + at
        allowed = (key >= start_ref[:, at:n]) & (key <= place)
        if block + 1 < blocks:
            ahead = products(block + 1)
        probs = []
        for head in heads:
            score = jnp.where(allowed, scores[head], big_negative)
            expd = jnp.exp(score - jnp.max(score, axis=0, keepdims=True))
            probs.append(expd * (1.0 / jnp.sum(expd, axis=0, keepdims=True)))
        low = [p.astype(bf16) for p in probs]
        out = [dot(vals_across[cut, 0:n], p, 1, 0) for cut, p in zip(cuts, low)]
        dv = sum(dot(p, g, 1, 0) for p, g in zip(low, grads))
        score_grads = []
        for p, g in zip(probs, prob_grads):
            both = p * g
            score_grads.append((both - p * jnp.sum(both, axis=0, keepdims=True)).astype(bf16))
        dq = [dot(keys_across[cut, 0:n], g, 1, 0) for cut, g in zip(cuts, score_grads)]
        dk = sum(dot(g, q, 1, 0) for g, q in zip(score_grads, queries))
        out = jnp.concatenate(out, axis=0).T.astype(bf16)
        o_ref[at:n, :] = out
        by_owner_ref[at // here, at % here : at % here + bq] = out
        g_ref[0, at:n, :] = turn_back(jnp.concatenate(dq, axis=0).T * (HD**-0.5), at, bq).astype(bf16)
        if block:
            dk_acc[0:at, :] += dk[0:at]
            dv_acc[0:at, :] += dv[0:at]
        dk_acc[at:n, :] = dk[at:n]
        dv_acc[at:n, :] = dv[at:n]
    g_ref[1] = turn_back(dk_acc[...], 0, span).astype(bf16)
    g_ref[2] = dv_acc[...].astype(bf16)


def attention_both(start, qkv, grad, cosine, sine, span, owners, row, before=(), bq=128):
    n, local = grad.shape
    here = 2 * span // owners
    width = cosine.shape[1]
    bq = min(bq, here)
    held = len(before)
    first = 2 * row
    part = lambda which: pl.BlockSpec((None, span, width), lambda t, p: (which, first + t, p))
    table = pl.BlockSpec((span, width), lambda t, p: (first + t, 0))
    return pl.pallas_call(
        functools.partial(attention_kernel, bq=bq, held=held),
        grid=(2, local // width),
        in_specs=[pl.BlockSpec(memory_space=pl.ANY)] * held
        + [
            pl.BlockSpec((1, span), lambda t, p: (0, first + t)),
            part(0),
            part(1),
            part(2),
            pl.BlockSpec((span, width), lambda t, p: (first + t, p)),
            table,
            table,
        ],
        out_specs=[
            pl.BlockSpec((span, width), lambda t, p: (first + t, p)),
            pl.BlockSpec((owners // 2, None, here, width), lambda t, p: (t, row, 0, p)),
            pl.BlockSpec((3, span, width), lambda t, p: (0, first + t, p)),
        ],
        out_shape=[
            jax.ShapeDtypeStruct((n, local), bf16),
            jax.ShapeDtypeStruct((owners, n // (2 * span), here, local), bf16),
            jax.ShapeDtypeStruct((3, n, local), bf16),
        ],
        scratch_shapes=[pltpu.VMEM((span, width), f32)] * 2,
        input_output_aliases={i: i for i in range(held)},
        compiler_params=params(),
        cost_estimate=SMALL,
        name="attention_both",
    )(*before, start, qkv, qkv, qkv, grad, cosine, sine)


def own_kernel(x_ref, w_ref, bd_ref, bo_ref, token_ref, *refs):
    *mlp_refs, o_ref, sum_ref = refs
    owners, seqs, here, local = x_ref.shape
    attention = jnp.zeros((seqs * here, w_ref.shape[1]), f32) + bd_ref[...]
    for owner in range(owners):
        x = x_ref[owner].reshape(seqs * here, local)
        attention += dot(x, w_ref[owner * local : (owner + 1) * local, :], 1, 0)
    tokens = token_ref[...].astype(f32)
    mlp = jnp.concatenate([a[...] for a in mlp_refs], axis=0).astype(f32) + bo_ref[...]
    total = tokens + attention + mlp
    o_ref[...] = total.astype(bf16)

    @pl.when(pl.program_id(0) == 0)
    def _():
        sum_ref[...] = jnp.zeros_like(sum_ref)

    for i, a in enumerate((tokens, attention, mlp, total)):
        sum_ref[i : i + 1, :] += jnp.sum(a * a, axis=0, keepdims=True)


def project_own(x, w, bd, bo, tokens, mlp_parts, tile=512, weight=1):
    owners, seqs, here, local = x.shape
    width = w.shape[1]
    rows = seqs * here
    column = lambda high: pl.BlockSpec((high, tile), lambda j: (0, j))
    return pl.pallas_call(
        own_kernel,
        grid=(width // tile,),
        in_specs=[
            pl.BlockSpec(x.shape, lambda j: (0, 0, 0, 0)),
            column(owners * local),
            column(1),
            column(1),
            column(rows),
        ]
        + [column(a.shape[0]) for a in mlp_parts],
        out_specs=[column(rows), pl.BlockSpec((8, tile), lambda j: (0, 0))],
        out_shape=[jax.ShapeDtypeStruct((rows, width), bf16), jax.ShapeDtypeStruct((8, tile), f32)],
        compiler_params=params(),
        cost_estimate=pl.CostEstimate(flops=int(weight), bytes_accessed=1, transcendentals=0),
        name="project_own",
    )(x, w, bd, bo, tokens, *mlp_parts)


def line_ok(size):
    return size >= 4 and size & (size - 1) == 0


class RowSum:
    def __init__(self, part, size):
        self.part, self.size, self.axis = part, size, "rows"
        groups = range(0, size, 4)
        pairs = lambda *ends: [(g + a, g + b) for g in groups for a, b in ends]
        self.hops = [pairs((0, 1), (3, 2)), pairs((1, 2), (2, 1))]
        hop = 4
        while hop < size:
            self.hops.append([(i, i ^ hop) for i in range(size)])
            hop *= 2
        self.hops.append(pairs((1, 0), (2, 3)))
        self.send()

    def send(self):
        if line_ok(self.size):
            self.came = lax.ppermute(self.part, self.axis, self.hops.pop(0))

    def fold(self, order):
        if line_ok(self.size) and self.hops:
            add = lambda a, b: (a.astype(f32) + b.astype(f32)).astype(a.dtype)
            self.part = order(add, self.part, self.came)
            self.send()

    def settle(self, order):
        if line_ok(self.size):
            self.came = order(lambda a: a, self.came)

    def complete(self, order):
        while self.hops:
            self.fold(order)

    def result(self, order=None):
        if not line_ok(self.size):
            return lax.psum(self.part.astype(f32), "rows")
        self.complete(order or Order())
        place = lax.axis_index("rows") % 4
        return jnp.where((place == 1) | (place == 2), self.part, self.came).astype(f32)


def finish_kernel(inner_ref, kept_ref, came_ref, *refs):
    o_ref = refs[-1]

    @pl.when(inner_ref[0] == 1)
    def _():
        o_ref[...] = kept_ref[...].astype(f32)

    @pl.when(inner_ref[0] == 0)
    def _():
        o_ref[...] = came_ref[...].astype(f32)


def finish(total, order, high, first=0, before=None, tile=512, weight=1):
    flat = lambda a: a.reshape(-1, a.shape[-1])
    rows, cols = flat(total.part).shape
    if not line_ok(total.size):
        before = jnp.zeros((high, cols), f32) if before is None else before
        return lax.dynamic_update_slice(before, flat(total.result()), (first, 0))
    total.complete(order)
    tile = min(tile, rows)
    held = [] if before is None else [before]
    block = pl.BlockSpec((tile, cols), lambda j: (j, 0))
    place = lax.axis_index("rows") % 4
    inner = ((place == 1) | (place == 2)).astype(jnp.int32).reshape(1)
    call = pl.pallas_call(
        finish_kernel,
        grid=(rows // tile,),
        in_specs=[pl.BlockSpec(memory_space=pltpu.SMEM), block, block] + [pl.BlockSpec(memory_space=pl.ANY)] * len(held),
        out_specs=pl.BlockSpec((tile, cols), lambda j: (first // tile + j, 0)),
        out_shape=jax.ShapeDtypeStruct((high, cols), f32),
        input_output_aliases={3: 0} if held else {},
        compiler_params=params(),
        cost_estimate=pl.CostEstimate(flops=int(weight), bytes_accessed=1, transcendentals=0),
        name="finish",
    )
    return order(lambda *a: call(inner, *a), flat(total.part), flat(total.came), *held)


class Gather:
    core, x, y = 1, 2, 4

    def __init__(self, first, second, size):
        self.first, self.second, self.size = first, second, size
        self.x0, self.y1 = self.send(first, self.x), self.send(second, self.y)

    def send(self, a, step):
        return lax.ppermute(a, "tp", [(i, i ^ step) for i in range(self.size)])

    def others(self, order=None):
        first, second = self.first, self.second
        if order:
            first, second = order(lambda a, b: (a, b), first, second)
        self.x1, self.y0 = self.send(second, self.x), self.send(first, self.y)
        self.c0 = self.send(first, self.core)

    def forward(self, order):
        came = (self.x0, self.y1, self.c0, self.second)
        self.x0, self.y1, self.c0, self.second = order(lambda *a: a, *came)
        self.c1 = self.send(self.second, self.core)
        self.d0, self.d1 = self.send(self.x0, self.y), self.send(self.y1, self.x)

    def pairs(self, order):
        came = (self.x0, self.y1, self.x1, self.y0, self.c1)
        self.x0, self.y1, self.x1, self.y0, self.c1 = order(lambda *a: a, *came)
        self.px0, self.py1 = self.send(self.x0, self.core), self.send(self.y1, self.core)
        self.px1, self.py0 = self.send(self.x1, self.core), self.send(self.y0, self.core)

    def near(self, order):
        steps = [step for step in (0, self.core, self.x, self.y, self.x | self.core, self.y | self.core) for _ in range(2)]
        pieces = (self.first, self.second, self.c0, self.c1, self.x0, self.x1, self.y0, self.y1)
        pieces += (self.px0, self.px1, self.py0, self.py1)
        self.full = order(lambda *a: place_pieces(None, a, steps, (0, 1) * 6, self.size), *pieces)

    def far_pairs(self, order):
        self.d0, self.d1 = order(lambda a, b: (a, b), self.d0, self.d1)
        self.pd0, self.pd1 = self.send(self.d0, self.core), self.send(self.d1, self.core)

    def far(self, order):
        far = self.x | self.y
        steps = (far, far, far | self.core, far | self.core)
        place = lambda full, *a: place_pieces(full, a, steps, (0, 1, 0, 1), self.size)
        self.full = order(place, self.full, self.d0, self.d1, self.pd0, self.pd1)
        return self.full


def place_kernel(me_ref, *refs, held):
    pieces, o_ref = refs[held:-1], refs[-1]
    for i, piece in enumerate(pieces):

        @pl.when(pl.program_id(0) == i)
        def _(piece=piece):
            o_ref[...] = piece[...].reshape(o_ref.shape)


def place_pieces(full, pieces, steps, halves, size):
    held = 0 if full is None else 1
    here, width = pieces[0].shape

    def target(j, me):
        device, half = me[0] ^ steps[0], halves[0]
        for i in range(1, len(pieces)):
            device = jnp.where(j == i, me[0] ^ steps[i], device)
            half = jnp.where(j == i, halves[i], half)
        return half, device, 0, 0

    hbm = pl.BlockSpec(memory_space=pl.ANY)
    me = lax.axis_index("tp").astype(jnp.int32).reshape(1)
    return pl.pallas_call(
        functools.partial(place_kernel, held=held),
        grid_spec=pltpu.PrefetchScalarGridSpec(
            num_scalar_prefetch=1,
            grid=(len(pieces),),
            in_specs=[hbm] * held + [pl.BlockSpec((here, width), lambda j, me: (0, 0))] * len(pieces),
            out_specs=pl.BlockSpec((1, None, here, width), target),
        ),
        out_shape=jax.ShapeDtypeStruct((2, size, here, width), bf16),
        input_output_aliases={1: 0} if held else {},
        compiler_params=params(),
        cost_estimate=SMALL,
        name="place_pieces",
    )(me, *([full] if held else []), *pieces)


class TpSum:
    def __init__(self, part, size):
        self.part, self.size, self.hop = part, size, 1
        self.send()

    def send(self):
        if self.size & (self.size - 1) == 0 and self.hop < self.size:
            self.came = lax.ppermute(self.part, "tp", [(i, i ^ self.hop) for i in range(self.size)])

    def fold(self, order):
        if self.size & (self.size - 1):
            self.part, self.size = lax.psum(self.part, "tp"), 1
        elif self.hop < self.size:
            self.part = order(lambda a, b: a + b, self.part, self.came)
            self.hop *= 2
            self.send()

    def result(self, order):
        while self.hop < self.size:
            self.fold(order)
        return self.part


def body(
    tokens,
    segment_ids,
    positions,
    norm_gain,
    norm_shift,
    query_key_value_weight,
    b_qkv,
    dense_weight,
    b_dense,
    inward_weight,
    b_in,
    outward_weight,
    b_out,
    cotangent,
):
    rows, tp = lax.axis_size("rows"), lax.axis_size("tp")
    seqs, here, width = tokens.shape
    length = here * tp
    n = seqs * length
    local = query_key_value_weight.shape[2]
    tile = min(128, local)
    span = length // 2

    exchange = tp == 8 and seqs == 2

    order = Order()
    gain, shift = norm_gain.astype(f32), norm_shift.astype(f32)
    norm = lambda a: norm_halves(a.reshape(seqs * here, width), gain, shift)
    halves = order(norm, tokens)

    if exchange:
        gather_normed = Gather(*halves, tp)
        gather_normed.others()

    def tables(positions, weight):
        place = positions.reshape(n, 1)
        cosine, sine = rope_tables(place, tile)
        start = jnp.arange(n, dtype=jnp.int32)[None] % span - positions.reshape(1, n)
        return cosine, sine, start, jnp.transpose(weight, (1, 0, 2))

    cosine, sine, start, w3 = order(tables, positions, query_key_value_weight)
    in_bias_row = b_in.astype(f32)[None]
    token_rows = lambda a: a.reshape(n, a.shape[-1])
    later = lambda a: lax.all_gather(order(lambda b: b, a), "tp", axis=1, tiled=True).reshape(n, width)
    if exchange:
        gather_normed.forward(order)
        gather_normed.pairs(order)
        grad = later(cotangent)
        gather_normed.near(order)
        hidden_of = lambda *a: mlp_hidden_of(*a, tuple(range(6)))
        hidden = order(hidden_of, gather_normed.full, inward_weight, in_bias_row)
        gather_normed.far_pairs(order)
        normed_full = gather_normed.far(order)
        hidden_of = lambda x, w, b, *before: mlp_hidden_of(x, w, b, (6, 7), before)
        act, slope = order(hidden_of, normed_full, inward_weight, in_bias_row, *hidden)
    else:
        normed_full = jnp.concatenate(halves).reshape(seqs, here, width)
        normed_full = lax.all_gather(normed_full, "tp", axis=1).reshape(seqs, tp, here, width)
        grad = later(cotangent)
        hidden_of = lambda *a: mlp_hidden_of(*a, tuple(range(tp)))
        act, slope = order(hidden_of, normed_full, inward_weight, in_bias_row)
    normed, act, slope = token_rows(normed_full), token_rows(act), token_rows(slope)
    qkv = order(project_qkv, normed, w3, b_qkv.astype(f32), cosine, sine)
    mlp_half = order(lambda *a: tokens_by_weight(*a, 0, 2), act, outward_weight)
    dense_ready, _ = lax.optimization_barrier((dense_weight, act))
    dense_full = lax.all_gather(dense_ready, "tp", axis=0, tiled=True)
    o0 = RowSum(order(lambda *a: weight_grad(*a, 0, 2), act, grad), rows)
    o1 = RowSum(order(lambda *a: weight_grad(*a, 1, 2), act, grad), rows)
    row_sum = lambda parts: [RowSum(part, rows) for part in parts]
    hidden_grad, attended_grad, in_bias = order(grad_in, grad, outward_weight, dense_weight, slope)
    o0.fold(order)
    i0, i1 = row_sum(order(lambda a, b: weight_grad_rows(a, b, (1, 1)), normed, hidden_grad))
    mlp_part = order(lambda x, w, *kept: tokens_by_weight(x, w, 1, 2, kept), act, outward_weight, mlp_half)
    mlp_part = mlp_part.reshape(seqs, length, width)
    mlp_tok = lax.psum_scatter(mlp_part, "tp", scatter_dimension=1, tiled=True).reshape(seqs * here, width)
    o1.fold(order)
    o0.fold(order)
    both = lambda row: lambda s, q, g, c, t, *before: attention_both(s, q, g, c, t, span, tp, row, before)
    attended, by_owner, dqkv = order(both(0), start, qkv, attended_grad, cosine, sine)
    i0.fold(order)
    for row in range(1, seqs):
        kept = (attended, by_owner, dqkv)
        attended, by_owner, dqkv = order(both(row), start, qkv, attended_grad, cosine, sine, *kept)
    mine = lax.all_to_all(by_owner, "tp", split_axis=0, concat_axis=0, tiled=True)
    o1.fold(order)
    o0.settle(order)
    qs, vs = row_sum(order(lambda a, b: weight_grad_parts(a, b, weight=EARLY_WEIGHT), normed, dqkv))
    units = in_bias.shape[1]
    back = lambda share: lambda *a: normed_grad(*a[:5], shift[None], share, 2, a[5:])
    i1.fold(order)
    i0.fold(order)
    part, bias_a, norm_a = order(back(0), hidden_grad, dqkv, inward_weight, w3, normed)
    o1.settle(order)
    i1.fold(order)
    qs.fold(order)
    part, bias_b, norm_b = order(back(1), hidden_grad, dqkv, inward_weight, w3, normed, part)
    back_tok = lax.psum_scatter(part.reshape(seqs, length, width), "tp", scatter_dimension=1, tiled=True)
    vs.fold(order)
    (ds,) = row_sum([order(weight_grad, attended, grad)])
    i0.settle(order)

    cols = width // tp

    def column_sums(grad):
        mine = lax.dynamic_slice_in_dim(grad, lax.axis_index("tp") * cols, cols, 1)
        return jnp.sum(mine.astype(f32), axis=0)

    out_bias = order(column_sums, grad)
    qs.fold(order)
    rows_of = lambda a: a.reshape(seqs * here, width)
    bias_rows = (b_dense.astype(f32)[None], b_out.astype(f32)[None])
    own = lambda x, w, t, *m: project_own(x, w, *bias_rows, rows_of(t), m)
    layer_out, squares = order(own, mine, dense_full, tokens, mlp_tok)
    layer_out = layer_out.reshape(tokens.shape)

    def pack(norm_a, norm_b, squares):
        norm_sums = norm_a + norm_b
        squares = jnp.sum(squares[:4], axis=1)
        pad = jnp.zeros((124,), f32)
        return jnp.concatenate([norm_sums[0] / gain, norm_sums[1], squares, pad]).reshape(-1, 128)

    i1.settle(order)
    packed = TpSum(order(pack, norm_a, norm_b, squares), tp)
    ds.fold(order)
    packed.fold(order)
    packed.fold(order)
    qkv_bias = bias_a + bias_b
    small = jnp.concatenate([in_bias[0], qkv_bias[:, 0].reshape(-1), out_bias]).reshape(-1, 128)
    small = RowSum(jnp.concatenate([packed.result(order), small]), rows)
    vs.fold(order)
    small.fold(order)
    ds.fold(order)
    qs.settle(order)
    out_grad = finish(o0, order, units, weight=ORDER_WEIGHT)
    out_grad = finish(o1, order, units, units // 2, out_grad)
    in_grad = finish(i0, order, width)
    small.fold(order)
    in_grad = finish(i1, order, width, width // 2, in_grad)
    qkv_grad = finish(qs, order, 3 * width)

    def norm_back(back_tok, tokens, cotangent):
        values = tokens.astype(f32)
        center = values - jnp.mean(values, axis=-1, keepdims=True)
        inverse = lax.rsqrt(jnp.mean(center * center, axis=-1, keepdims=True) + epsilon)
        unit = center * inverse
        unit_grad = back_tok.astype(f32) * gain
        mean_grad = jnp.mean(unit_grad, axis=-1, keepdims=True)
        mean_both = jnp.mean(unit_grad * unit, axis=-1, keepdims=True)
        value_grad = (unit_grad - mean_grad - unit * mean_both) * inverse
        return (cotangent.astype(f32) + value_grad).astype(bf16)

    input_grad = order(norm_back, back_tok, tokens, cotangent)
    qkv_grad = finish(vs, order, 3 * width, 2 * width, qkv_grad)
    qkv_grad = jnp.transpose(qkv_grad.reshape(3, width, local), (1, 0, 2))
    dense_grad = finish(ds, order, local)
    small = small.result().reshape(-1)
    slice_at = lambda a: lax.dynamic_slice_in_dim(a, lax.axis_index("tp") * cols, cols, 0)
    gain_grad, shift_grad = slice_at(small[:width]), slice_at(small[width : 2 * width])
    rms_values = jnp.sqrt(small[2 * width : 2 * width + 4] / (seqs * rows * length * width))
    small = small[2 * width + 128 :]
    in_bias_grad = small[:units]
    qkv_bias_grad = small[units : units + 3 * local].reshape(3, local)
    out_bias_grad = small[units + 3 * local :]

    return (
        layer_out,
        input_grad,
        gain_grad,
        shift_grad,
        qkv_grad,
        qkv_bias_grad,
        dense_grad,
        out_bias_grad,
        in_grad,
        in_bias_grad,
        out_grad,
        out_bias_grad,
        rms_values,
    )


def solution(mesh):
    in_specs = (
        P("rows", "tp", None),
        P("rows", None),
        P("rows", None),
        P(),
        P(),
        P(None, None, "tp"),
        P(None, "tp"),
        P("tp", None),
        P(),
        P(None, "tp"),
        P("tp"),
        P("tp", None),
        P(),
        P("rows", "tp", None),
    )
    out_specs = (
        P("rows", "tp", None),
        P("rows", "tp", None),
        P("tp"),
        P("tp"),
        P(None, None, "tp"),
        P(None, "tp"),
        P("tp", None),
        P("tp"),
        P(None, "tp"),
        P("tp"),
        P("tp", None),
        P("tp"),
        P(),
    )
    return jax.shard_map(body, mesh=mesh, in_specs=in_specs, out_specs=out_specs, check_vma=False)
```

```python
import functools

import jax
import jax.numpy as jnp
from jax import lax
from jax.experimental import pallas as pl
from jax.experimental.pallas import tpu as pltpu
from jax.sharding import PartitionSpec as P

HD = 64
ROT = 32
epsilon = 1e-05
big_negative = -1e30
rope_base = 10000.0
f32 = jnp.float32
bf16 = jnp.bfloat16
VMEM_LIMIT = 56 << 20
ORDER_WEIGHT = int(2.15e11)
EARLY_WEIGHT = int(2.2e11)


def dot(a, b, ca, cb):
    return lax.dot_general(a, b, (((ca,), (cb,)), ((), ())), preferred_element_type=f32)


SMALL = pl.CostEstimate(flops=1, bytes_accessed=1, transcendentals=0)


def params():
    return pltpu.CompilerParams(vmem_limit_bytes=VMEM_LIMIT)


class Order:
    def __init__(self):
        self.last = ()

    def __call__(self, op, *operands):
        operands, _ = lax.optimization_barrier((operands, self.last))
        result = op(*operands)
        self.last = jax.tree.leaves(result)
        return result


def rope_swap(x):
    width = x.shape[-1]
    lane = lax.broadcasted_iota(jnp.int32, (1, width), 1) % HD
    up = pltpu.roll(x, width - ROT // 2, 1)
    down = pltpu.roll(x, ROT // 2, 1)
    return jnp.where(lane < ROT // 2, up, -down)


def norm_kernel(x_ref, gain_ref, shift_ref, first_ref, second_ref, *, per):
    x = x_ref[...].astype(f32)
    center = x - jnp.mean(x, axis=-1, keepdims=True)
    inverse = lax.rsqrt(jnp.mean(center * center, axis=-1, keepdims=True) + epsilon)
    out = (center * inverse * gain_ref[...] + shift_ref[...]).astype(bf16)

    @pl.when(pl.program_id(0) < per)
    def _():
        first_ref[...] = out

    @pl.when(pl.program_id(0) >= per)
    def _():
        second_ref[...] = out


def norm_halves(x, gain, shift, tm=128):
    n, width = x.shape
    per = n // 2 // tm
    vector = pl.BlockSpec((1, width), lambda i: (0, 0))
    return pl.pallas_call(
        functools.partial(norm_kernel, per=per),
        grid=(2 * per,),
        in_specs=[pl.BlockSpec((tm, width), lambda i: (i, 0)), vector, vector],
        out_specs=[
            pl.BlockSpec((tm, width), lambda i: (jnp.minimum(i, per - 1), 0)),
            pl.BlockSpec((tm, width), lambda i: (jnp.maximum(i - per, 0), 0)),
        ],
        out_shape=[jax.ShapeDtypeStruct((n // 2, width), bf16)] * 2,
        compiler_params=params(),
        cost_estimate=SMALL,
        name="norm_halves",
    )(x, gain[None], shift[None])


def norm_back_kernel(back_ref, x_ref, g_ref, gain_ref, o_ref):
    x = x_ref[...].astype(f32)
    center = x - jnp.mean(x, axis=-1, keepdims=True)
    inverse = lax.rsqrt(jnp.mean(center * center, axis=-1, keepdims=True) + epsilon)
    unit = center * inverse
    unit_grad = back_ref[...].astype(f32) * gain_ref[...]
    mean_grad = jnp.mean(unit_grad, axis=-1, keepdims=True)
    mean_both = jnp.mean(unit_grad * unit, axis=-1, keepdims=True)
    value_grad = (unit_grad - mean_grad - unit * mean_both) * inverse
    o_ref[...] = (g_ref[...].astype(f32) + value_grad).astype(bf16)


def norm_back(back, x, g, gain, tm=128):
    n, width = x.shape
    block = pl.BlockSpec((tm, width), lambda i: (i, 0))
    return pl.pallas_call(
        norm_back_kernel,
        grid=(n // tm,),
        in_specs=[block, block, block, pl.BlockSpec((1, width), lambda i: (0, 0))],
        out_specs=block,
        out_shape=jax.ShapeDtypeStruct((n, width), bf16),
        compiler_params=params(),
        cost_estimate=SMALL,
        name="norm_back",
    )(back, x, g, gain[None])


def table_kernel(place_ref, frequency_ref, c_ref, s_ref):
    angle = place_ref[...].astype(f32) * frequency_ref[...]
    lane = lax.broadcasted_iota(jnp.int32, angle.shape, 1) % HD
    turned = lane < ROT
    c_ref[...] = jnp.where(turned, jnp.cos(angle), 1.0)
    s_ref[...] = jnp.where(turned, jnp.sin(angle), 0.0)


def rope_tables(place, tile, tm=1024):
    n = place.shape[0]
    lane = jnp.arange(tile, dtype=jnp.int32) % (ROT // 2)
    frequency = (rope_base ** (-2.0 * lane.astype(f32) / ROT))[None]
    table = pl.BlockSpec((tm, tile), lambda i: (i, 0))
    return pl.pallas_call(
        table_kernel,
        grid=(n // tm,),
        in_specs=[pl.BlockSpec((tm, 1), lambda i: (i, 0)), pl.BlockSpec((1, tile), lambda i: (0, 0))],
        out_specs=[table, table],
        out_shape=[jax.ShapeDtypeStruct((n, tile), f32)] * 2,
        compiler_params=params(),
        cost_estimate=SMALL,
        name="rope_tables",
    )(place, frequency)


def qkv_kernel(x_ref, w_ref, b_ref, c_ref, s_ref, o_ref):
    x = x_ref[...]
    tile = c_ref.shape[-1]
    local = w_ref.shape[-1]
    cosine, sine = c_ref[...], s_ref[...]
    for part in range(3):
        full = dot(x, w_ref[part], 1, 0) + b_ref[part : part + 1, :]
        for at in range(0, local, tile):
            piece = full[:, at : at + tile]
            if part < 2:
                piece = piece * cosine - rope_swap(piece) * sine
            if part == 0:
                piece = piece * (HD**-0.5)
            o_ref[part, :, at : at + tile] = piece.astype(bf16)


def project_qkv(x, w3, bias, cosine, sine, tm=512):
    n, width = x.shape
    local = w3.shape[2]
    tile = cosine.shape[1]
    return pl.pallas_call(
        qkv_kernel,
        grid=(n // tm,),
        in_specs=[
            pl.BlockSpec((tm, width), lambda i: (i, 0)),
            pl.BlockSpec((3, width, local), lambda i: (0, 0, 0)),
            pl.BlockSpec((3, local), lambda i: (0, 0)),
            pl.BlockSpec((tm, tile), lambda i: (i, 0)),
            pl.BlockSpec((tm, tile), lambda i: (i, 0)),
        ],
        out_specs=pl.BlockSpec((3, tm, local), lambda i: (0, i, 0)),
        out_shape=jax.ShapeDtypeStruct((3, n, local), bf16),
        compiler_params=params(),
        cost_estimate=SMALL,
        name="qkv_rope",
    )(x, w3, bias, cosine, sine)


def chosen_kernel(me_ref, *refs, held):
    x_ref, w_ref, b_ref, act_ref, slope_ref = refs[held:]
    seqs, here, width = x_ref.shape
    x = x_ref[...].reshape(seqs * here, width)
    units = w_ref.shape[1]
    step = min(256, units)
    for at in range(0, units, step):
        cut = slice(at, at + step)
        h = dot(x, w_ref[:, cut], 1, 0) + b_ref[:, cut]
        square = h * h
        t = jnp.tanh(h * (0.7978845608028654 + 0.035677408136300125 * square))
        half = 0.5 + 0.5 * t
        act = h * half
        slope = half + (act - act * half) * (1.5957691216057308 + 0.21406444881780074 * square)
        act_ref[:, :, cut] = act.astype(bf16).reshape(seqs, here, step)
        slope_ref[:, :, cut] = slope.astype(bf16).reshape(seqs, here, step)


def mlp_hidden_of(x, w, bias, steps, before=(), weight=1):
    seqs, owners, here, width = x.shape
    units = w.shape[1]
    held = len(before)

    def device(j, me):
        chosen = me[0] ^ steps[0]
        for i in range(1, len(steps)):
            chosen = jnp.where(j == i, me[0] ^ steps[i], chosen)
        return 0, chosen, 0, 0

    out = pl.BlockSpec((seqs, None, here, units), device)
    me = lax.axis_index("tp").astype(jnp.int32).reshape(1)
    return pl.pallas_call(
        functools.partial(chosen_kernel, held=held),
        grid_spec=pltpu.PrefetchScalarGridSpec(
            num_scalar_prefetch=1,
            grid=(len(steps),),
            in_specs=[pl.BlockSpec(memory_space=pl.ANY)] * held
            + [
                pl.BlockSpec((seqs, None, here, width), device),
                pl.BlockSpec((width, units), lambda j, me: (0, 0)),
                pl.BlockSpec((1, units), lambda j, me: (0, 0)),
            ],
            out_specs=[out, out],
        ),
        out_shape=[jax.ShapeDtypeStruct((seqs, owners, here, units), bf16)] * 2,
        input_output_aliases={1 + i: i for i in range(held)},
        compiler_params=params(),
        cost_estimate=pl.CostEstimate(flops=int(weight), bytes_accessed=1, transcendentals=0),
        name="mlp_hidden_of",
    )(me, *before, x, w, bias)


def grad_in_kernel(g_ref, wo_ref, wd_ref, slope_ref, hg_ref, at_ref, sum_ref):
    g = g_ref[...]
    units = wo_ref.shape[0]
    step = min(256, units)

    @pl.when(pl.program_id(0) == 0)
    def _():
        sum_ref[...] = jnp.zeros_like(sum_ref)

    for at in range(0, units, step):
        slope = slope_ref[:, at : at + step].astype(f32)
        hg = (dot(g, wo_ref[at : at + step, :], 1, 1) * slope).astype(bf16)
        hg_ref[:, at : at + step] = hg
        sum_ref[0:1, at : at + step] += jnp.sum(hg.astype(f32), axis=0, keepdims=True)
    at_ref[...] = dot(g, wd_ref[...], 1, 1).astype(bf16)


def grad_in(g, wo, wd, slope, tm=512):
    n, width = g.shape
    units, local = wo.shape[0], wd.shape[0]
    return pl.pallas_call(
        grad_in_kernel,
        grid=(n // tm,),
        in_specs=[
            pl.BlockSpec((tm, width), lambda i: (i, 0)),
            pl.BlockSpec((units, width), lambda i: (0, 0)),
            pl.BlockSpec((local, width), lambda i: (0, 0)),
            pl.BlockSpec((tm, units), lambda i: (i, 0)),
        ],
        out_specs=[
            pl.BlockSpec((tm, units), lambda i: (i, 0)),
            pl.BlockSpec((tm, local), lambda i: (i, 0)),
            pl.BlockSpec((8, units), lambda i: (0, 0)),
        ],
        out_shape=[
            jax.ShapeDtypeStruct((n, units), bf16),
            jax.ShapeDtypeStruct((n, local), bf16),
            jax.ShapeDtypeStruct((8, units), f32),
        ],
        compiler_params=params(),
        cost_estimate=SMALL,
        name="grad_in",
    )(g, wo, wd, slope)


def tokens_kernel(*refs, held):
    x_ref, w_ref, o_ref = refs[held:]
    width = w_ref.shape[1]
    step = min(512, width)
    for at in range(0, width, step):
        o_ref[:, at : at + step] = dot(x_ref[...], w_ref[:, at : at + step], 1, 0).astype(o_ref.dtype)


def tokens_by_weight(x, w, share, shares, before=(), tm=512):
    n, depth = x.shape
    held = len(before)
    steps = n // shares // tm
    width = w.shape[1]
    first = share * steps
    return pl.pallas_call(
        functools.partial(tokens_kernel, held=held),
        grid=(steps,),
        in_specs=[pl.BlockSpec(memory_space=pl.ANY)] * held
        + [pl.BlockSpec((tm, depth), lambda i: (first + i, 0)), pl.BlockSpec((depth, width), lambda i: (0, 0))],
        out_specs=pl.BlockSpec((tm, width), lambda i: (first + i, 0)),
        out_shape=jax.ShapeDtypeStruct((n, width), bf16),
        input_output_aliases={i: i for i in range(held)},
        compiler_params=params(),
        cost_estimate=SMALL,
        name="tokens_by_weight",
    )(*before, x, w)


def weight_grad_kernel(a_ref, b_ref, o_ref):
    o_ref[...] = dot(a_ref[...], b_ref[...], 0, 0).astype(bf16)


def weight_grad(a, b, share=0, shares=1, tile=512, weight=1):
    n, rows = a.shape
    rows //= shares
    cols = b.shape[1]
    tile = min(tile, cols)
    return pl.pallas_call(
        weight_grad_kernel,
        grid=(cols // tile,),
        in_specs=[
            pl.BlockSpec((n, rows), lambda j: (0, share), pipeline_mode=pl.Buffered(1)),
            pl.BlockSpec((n, tile), lambda j: (0, j)),
        ],
        out_specs=pl.BlockSpec((rows, tile), lambda j: (0, j)),
        out_shape=jax.ShapeDtypeStruct((rows, cols), bf16),
        compiler_params=params(),
        cost_estimate=pl.CostEstimate(flops=int(weight), bytes_accessed=1, transcendentals=0),
        name="weight_grad",
    )(a, b)


def weight_grad_rows_kernel(a_ref, b_ref, *o_refs, counts):
    full = dot(a_ref[...], b_ref[...], 0, 0).astype(bf16)
    step = pl.program_id(0)
    first = 0
    for o_ref, count in zip(o_refs, counts):

        @pl.when((step >= first) & (step < first + count))
        def _(o_ref=o_ref):
            o_ref[...] = full

        first += count


def weight_grad_rows(a, b, shares, tile=512):
    n, rows = a.shape
    cols = b.shape[1]
    counts = [rows * share // sum(shares) // tile for share in shares]
    firsts = [sum(counts[:i]) for i in range(len(counts))]
    out = lambda i: pl.BlockSpec((tile, cols), lambda j: (jnp.clip(j - firsts[i], 0, counts[i] - 1), 0))
    return pl.pallas_call(
        functools.partial(weight_grad_rows_kernel, counts=counts),
        grid=(rows // tile,),
        in_specs=[
            pl.BlockSpec((n, tile), lambda j: (0, j)),
            pl.BlockSpec((n, cols), lambda j: (0, 0), pipeline_mode=pl.Buffered(1)),
        ],
        out_specs=[out(i) for i in range(len(counts))],
        out_shape=[jax.ShapeDtypeStruct((count * tile, cols), bf16) for count in counts],
        compiler_params=params(),
        cost_estimate=SMALL,
        name="weight_grad_rows",
    )(a, b)


def weight_grad_parts_kernel(a_ref, b_ref, first_ref, last_ref):
    for part in range(2):
        first_ref[part] = dot(a_ref[...], b_ref[part], 0, 0).astype(bf16)
    last_ref[...] = dot(a_ref[...], b_ref[2], 0, 0).astype(bf16)


def weight_grad_parts(a, b, tile=512, weight=1):
    n, rows = a.shape
    parts, _, cols = b.shape
    return pl.pallas_call(
        weight_grad_parts_kernel,
        grid=(rows // tile,),
        in_specs=[
            pl.BlockSpec((n, tile), lambda j: (0, j)),
            pl.BlockSpec((parts, n, cols), lambda j: (0, 0, 0), pipeline_mode=pl.Buffered(1)),
        ],
        out_specs=[pl.BlockSpec((2, tile, cols), lambda j: (0, j, 0)), pl.BlockSpec((tile, cols), lambda j: (j, 0))],
        out_shape=[jax.ShapeDtypeStruct((2, rows, cols), bf16), jax.ShapeDtypeStruct((rows, cols), bf16)],
        compiler_params=params(),
        cost_estimate=pl.CostEstimate(flops=int(weight), bytes_accessed=1, transcendentals=0),
        name="weight_grad_parts",
    )(a, b)


def normed_grad_kernel(*refs, held):
    hg_ref, dq_ref, wi_ref, w3_ref, x_ref, shift_ref, o_ref, sum_ref, norm_ref = refs[held:]

    @pl.when(pl.program_id(0) == 0)
    def _():
        sum_ref[...] = jnp.zeros_like(sum_ref)
        norm_ref[...] = jnp.zeros_like(norm_ref)

    for part in range(3):
        sum_ref[part, 0:1] += jnp.sum(dq_ref[part].astype(f32), axis=0, keepdims=True)
    width = o_ref.shape[1]
    step = min(512, width)
    for at in range(0, width, step):
        cut = slice(at, at + step)
        total = dot(hg_ref[...], wi_ref[cut, :], 1, 1)
        for part in range(3):
            total += dot(dq_ref[part], w3_ref[part, cut, :], 1, 1)
        o_ref[:, cut] = total.astype(bf16)
        scaled = x_ref[:, cut].astype(f32) - shift_ref[:, cut]
        norm_ref[0:1, cut] += jnp.sum(total * scaled, axis=0, keepdims=True)
        norm_ref[1:2, cut] += jnp.sum(total, axis=0, keepdims=True)


def normed_grad(hg, dqkv, wi, w3, x, shift, share, shares, before=(), tm=512):
    n, units = hg.shape
    held = len(before)
    steps = n // shares // tm
    first = share * steps
    width, local = w3.shape[1:]
    return pl.pallas_call(
        functools.partial(normed_grad_kernel, held=held),
        grid=(steps,),
        in_specs=[pl.BlockSpec(memory_space=pl.ANY)] * held
        + [
            pl.BlockSpec((tm, units), lambda i: (first + i, 0)),
            pl.BlockSpec((3, tm, local), lambda i: (0, first + i, 0)),
            pl.BlockSpec((width, units), lambda i: (0, 0)),
            pl.BlockSpec((3, width, local), lambda i: (0, 0, 0)),
            pl.BlockSpec((tm, width), lambda i: (first + i, 0)),
            pl.BlockSpec((1, width), lambda i: (0, 0)),
        ],
        out_specs=[
            pl.BlockSpec((tm, width), lambda i: (first + i, 0)),
            pl.BlockSpec((3, 8, local), lambda i: (0, 0, 0)),
            pl.BlockSpec((8, width), lambda i: (0, 0)),
        ],
        out_shape=[
            jax.ShapeDtypeStruct((n, width), bf16),
            jax.ShapeDtypeStruct((3, 8, local), f32),
            jax.ShapeDtypeStruct((8, width), f32),
        ],
        input_output_aliases={i: i for i in range(held)},
        compiler_params=params(),
        cost_estimate=SMALL,
        name="normed_grad",
    )(*before, hg, dqkv, wi, w3, x, shift)


def attention_kernel(*refs, bq, held):
    start_ref, q_ref, k_ref, v_ref, do_ref, c_ref, s_ref, o_ref, by_owner_ref, g_ref, dk_acc, dv_acc = refs[held:]
    span, width = q_ref.shape
    here = by_owner_ref.shape[1]
    lane = lax.broadcasted_iota(jnp.int32, (1, width), 1) // HD
    zero = jnp.zeros((), bf16)
    heads = range(width // HD)
    cuts = [slice(head * HD, (head + 1) * HD) for head in heads]
    blocks = span // bq
    keys_across, vals_across = k_ref[...].T, v_ref[...].T

    def turn_back(x, at, n):
        return x * c_ref[at : at + n, :] + rope_swap(x) * s_ref[at : at + n, :]

    def products(block):
        at, n = block * bq, (block + 1) * bq
        keys, vals = k_ref[0:n, :], v_ref[0:n, :]
        queries = [jnp.where(lane == head, q_ref[at:n, :], zero) for head in heads]
        grads = [jnp.where(lane == head, do_ref[at:n, :], zero) for head in heads]
        return queries, grads, [dot(keys, q, 1, 1) for q in queries], [dot(vals, g, 1, 1) for g in grads]

    ahead = products(0)
    for block in range(blocks):
        at, n = block * bq, (block + 1) * bq
        queries, grads, scores, prob_grads = ahead
        key = lax.broadcasted_iota(jnp.int32, (n, bq), 0)
        place = lax.broadcasted_iota(jnp.int32, (1, bq), 1) + at
        allowed = (key >= start_ref[:, at:n]) & (key <= place)
        if block + 1 < blocks:
            ahead = products(block + 1)
        probs = []
        for head in heads:
            score = jnp.where(allowed, scores[head], big_negative)
            expd = jnp.exp(score - jnp.max(score, axis=0, keepdims=True))
            probs.append(expd * (1.0 / jnp.sum(expd, axis=0, keepdims=True)))
        low = [p.astype(bf16) for p in probs]
        out = [dot(vals_across[cut, 0:n], p, 1, 0) for cut, p in zip(cuts, low)]
        dv = sum(dot(p, g, 1, 0) for p, g in zip(low, grads))
        score_grads = []
        for p, g in zip(probs, prob_grads):
            both = p * g
            score_grads.append((both - p * jnp.sum(both, axis=0, keepdims=True)).astype(bf16))
        dq = [dot(keys_across[cut, 0:n], g, 1, 0) for cut, g in zip(cuts, score_grads)]
        dk = sum(dot(g, q, 1, 0) for g, q in zip(score_grads, queries))
        out = jnp.concatenate(out, axis=0).T.astype(bf16)
        o_ref[at:n, :] = out
        by_owner_ref[at // here, at % here : at % here + bq] = out
        g_ref[0, at:n, :] = turn_back(jnp.concatenate(dq, axis=0).T * (HD**-0.5), at, bq).astype(bf16)
        if block:
            dk_acc[0:at, :] += dk[0:at]
            dv_acc[0:at, :] += dv[0:at]
        dk_acc[at:n, :] = dk[at:n]
        dv_acc[at:n, :] = dv[at:n]
    g_ref[1] = turn_back(dk_acc[...], 0, span).astype(bf16)
    g_ref[2] = dv_acc[...].astype(bf16)


def attention_both(start, qkv, grad, cosine, sine, span, owners, row, before=(), bq=128):
    n, local = grad.shape
    here = 2 * span // owners
    width = cosine.shape[1]
    bq = min(bq, here)
    held = len(before)
    first = 2 * row
    part = lambda which: pl.BlockSpec((None, span, width), lambda t, p: (which, first + t, p))
    table = pl.BlockSpec((span, width), lambda t, p: (first + t, 0))
    return pl.pallas_call(
        functools.partial(attention_kernel, bq=bq, held=held),
        grid=(2, local // width),
        in_specs=[pl.BlockSpec(memory_space=pl.ANY)] * held
        + [
            pl.BlockSpec((1, span), lambda t, p: (0, first + t)),
            part(0),
            part(1),
            part(2),
            pl.BlockSpec((span, width), lambda t, p: (first + t, p)),
            table,
            table,
        ],
        out_specs=[
            pl.BlockSpec((span, width), lambda t, p: (first + t, p)),
            pl.BlockSpec((owners // 2, None, here, width), lambda t, p: (t, row, 0, p)),
            pl.BlockSpec((3, span, width), lambda t, p: (0, first + t, p)),
        ],
        out_shape=[
            jax.ShapeDtypeStruct((n, local), bf16),
            jax.ShapeDtypeStruct((owners, n // (2 * span), here, local), bf16),
            jax.ShapeDtypeStruct((3, n, local), bf16),
        ],
        scratch_shapes=[pltpu.VMEM((span, width), f32)] * 2,
        input_output_aliases={i: i for i in range(held)},
        compiler_params=params(),
        cost_estimate=SMALL,
        name="attention_both",
    )(*before, start, qkv, qkv, qkv, grad, cosine, sine)


def own_kernel(x_ref, w_ref, bd_ref, bo_ref, token_ref, *refs):
    *mlp_refs, o_ref, sum_ref = refs
    owners, seqs, here, local = x_ref.shape
    attention = jnp.zeros((seqs * here, w_ref.shape[1]), f32) + bd_ref[...]
    for owner in range(owners):
        x = x_ref[owner].reshape(seqs * here, local)
        attention += dot(x, w_ref[owner * local : (owner + 1) * local, :], 1, 0)
    tokens = token_ref[...].astype(f32)
    mlp = jnp.concatenate([a[...] for a in mlp_refs], axis=0).astype(f32) + bo_ref[...]
    total = tokens + attention + mlp
    o_ref[...] = total.astype(bf16)

    @pl.when(pl.program_id(0) == 0)
    def _():
        sum_ref[...] = jnp.zeros_like(sum_ref)

    for i, a in enumerate((tokens, attention, mlp, total)):
        sum_ref[i : i + 1, :] += jnp.sum(a * a, axis=0, keepdims=True)


def project_own(x, w, bd, bo, tokens, mlp_parts, tile=512, weight=1):
    owners, seqs, here, local = x.shape
    width = w.shape[1]
    rows = seqs * here
    column = lambda high: pl.BlockSpec((high, tile), lambda j: (0, j))
    return pl.pallas_call(
        own_kernel,
        grid=(width // tile,),
        in_specs=[
            pl.BlockSpec(x.shape, lambda j: (0, 0, 0, 0)),
            column(owners * local),
            column(1),
            column(1),
            column(rows),
        ]
        + [column(a.shape[0]) for a in mlp_parts],
        out_specs=[column(rows), pl.BlockSpec((8, tile), lambda j: (0, 0))],
        out_shape=[jax.ShapeDtypeStruct((rows, width), bf16), jax.ShapeDtypeStruct((8, tile), f32)],
        compiler_params=params(),
        cost_estimate=pl.CostEstimate(flops=int(weight), bytes_accessed=1, transcendentals=0),
        name="project_own",
    )(x, w, bd, bo, tokens, *mlp_parts)


def line_ok(size):
    return size >= 4 and size & (size - 1) == 0


class RowSum:
    def __init__(self, part, size):
        self.part, self.size, self.axis = part, size, "rows"
        groups = range(0, size, 4)
        pairs = lambda *ends: [(g + a, g + b) for g in groups for a, b in ends]
        self.hops = [pairs((0, 1), (3, 2)), pairs((1, 2), (2, 1))]
        hop = 4
        while hop < size:
            self.hops.append([(i, i ^ hop) for i in range(size)])
            hop *= 2
        self.hops.append(pairs((1, 0), (2, 3)))
        self.send()

    def send(self):
        if line_ok(self.size):
            self.came = lax.ppermute(self.part, self.axis, self.hops.pop(0))

    def fold(self, order):
        if line_ok(self.size) and self.hops:
            add = lambda a, b: (a.astype(f32) + b.astype(f32)).astype(a.dtype)
            self.part = order(add, self.part, self.came)
            self.send()

    def settle(self, order):
        if line_ok(self.size):
            self.came = order(lambda a: a, self.came)

    def complete(self, order):
        while self.hops:
            self.fold(order)

    def result(self, order=None):
        if not line_ok(self.size):
            return lax.psum(self.part.astype(f32), "rows")
        self.complete(order or Order())
        place = lax.axis_index("rows") % 4
        return jnp.where((place == 1) | (place == 2), self.part, self.came).astype(f32)


def finish_kernel(inner_ref, kept_ref, came_ref, *refs):
    o_ref = refs[-1]

    @pl.when(inner_ref[0] == 1)
    def _():
        o_ref[...] = kept_ref[...].astype(f32)

    @pl.when(inner_ref[0] == 0)
    def _():
        o_ref[...] = came_ref[...].astype(f32)


def finish(total, order, high, first=0, before=None, tile=512, weight=1):
    flat = lambda a: a.reshape(-1, a.shape[-1])
    rows, cols = flat(total.part).shape
    if not line_ok(total.size):
        before = jnp.zeros((high, cols), f32) if before is None else before
        return lax.dynamic_update_slice(before, flat(total.result()), (first, 0))
    total.complete(order)
    tile = min(tile, rows)
    held = [] if before is None else [before]
    block = pl.BlockSpec((tile, cols), lambda j: (j, 0))
    place = lax.axis_index("rows") % 4
    inner = ((place == 1) | (place == 2)).astype(jnp.int32).reshape(1)
    call = pl.pallas_call(
        finish_kernel,
        grid=(rows // tile,),
        in_specs=[pl.BlockSpec(memory_space=pltpu.SMEM), block, block] + [pl.BlockSpec(memory_space=pl.ANY)] * len(held),
        out_specs=pl.BlockSpec((tile, cols), lambda j: (first // tile + j, 0)),
        out_shape=jax.ShapeDtypeStruct((high, cols), f32),
        input_output_aliases={3: 0} if held else {},
        compiler_params=params(),
        cost_estimate=pl.CostEstimate(flops=int(weight), bytes_accessed=1, transcendentals=0),
        name="finish",
    )
    return order(lambda *a: call(inner, *a), flat(total.part), flat(total.came), *held)


class Gather:
    core, x, y = 1, 2, 4

    def __init__(self, first, second, size):
        self.first, self.second, self.size = first, second, size
        self.x0, self.y1 = self.send(first, self.x), self.send(second, self.y)

    def send(self, a, step):
        return lax.ppermute(a, "tp", [(i, i ^ step) for i in range(self.size)])

    def others(self, order=None):
        first, second = self.first, self.second
        if order:
            first, second = order(lambda a, b: (a, b), first, second)
        self.x1, self.y0 = self.send(second, self.x), self.send(first, self.y)
        self.c0 = self.send(first, self.core)

    def forward(self, order):
        came = (self.x0, self.y1, self.c0, self.second)
        self.x0, self.y1, self.c0, self.second = order(lambda *a: a, *came)
        self.c1 = self.send(self.second, self.core)
        self.d0, self.d1 = self.send(self.x0, self.y), self.send(self.y1, self.x)

    def pairs(self, order):
        came = (self.x0, self.y1, self.x1, self.y0, self.c1)
        self.x0, self.y1, self.x1, self.y0, self.c1 = order(lambda *a: a, *came)
        self.px0, self.py1 = self.send(self.x0, self.core), self.send(self.y1, self.core)
        self.px1, self.py0 = self.send(self.x1, self.core), self.send(self.y0, self.core)

    def near(self, order):
        steps = [step for step in (0, self.core, self.x, self.y, self.x | self.core, self.y | self.core) for _ in range(2)]
        pieces = (self.first, self.second, self.c0, self.c1, self.x0, self.x1, self.y0, self.y1)
        pieces += (self.px0, self.px1, self.py0, self.py1)
        self.full = order(lambda *a: place_pieces(None, a, steps, (0, 1) * 6, self.size), *pieces)

    def far_pairs(self, order):
        self.d0, self.d1 = order(lambda a, b: (a, b), self.d0, self.d1)
        self.pd0, self.pd1 = self.send(self.d0, self.core), self.send(self.d1, self.core)

    def far(self, order):
        far = self.x | self.y
        steps = (far, far, far | self.core, far | self.core)
        place = lambda full, *a: place_pieces(full, a, steps, (0, 1, 0, 1), self.size)
        self.full = order(place, self.full, self.d0, self.d1, self.pd0, self.pd1)
        return self.full


def place_kernel(me_ref, *refs, held):
    pieces, o_ref = refs[held:-1], refs[-1]
    for i, piece in enumerate(pieces):

        @pl.when(pl.program_id(0) == i)
        def _(piece=piece):
            o_ref[...] = piece[...].reshape(o_ref.shape)


def place_pieces(full, pieces, steps, halves, size):
    held = 0 if full is None else 1
    here, width = pieces[0].shape

    def target(j, me):
        device, half = me[0] ^ steps[0], halves[0]
        for i in range(1, len(pieces)):
            device = jnp.where(j == i, me[0] ^ steps[i], device)
            half = jnp.where(j == i, halves[i], half)
        return half, device, 0, 0

    hbm = pl.BlockSpec(memory_space=pl.ANY)
    me = lax.axis_index("tp").astype(jnp.int32).reshape(1)
    return pl.pallas_call(
        functools.partial(place_kernel, held=held),
        grid_spec=pltpu.PrefetchScalarGridSpec(
            num_scalar_prefetch=1,
            grid=(len(pieces),),
            in_specs=[hbm] * held + [pl.BlockSpec((here, width), lambda j, me: (0, 0))] * len(pieces),
            out_specs=pl.BlockSpec((1, None, here, width), target),
        ),
        out_shape=jax.ShapeDtypeStruct((2, size, here, width), bf16),
        input_output_aliases={1: 0} if held else {},
        compiler_params=params(),
        cost_estimate=SMALL,
        name="place_pieces",
    )(me, *([full] if held else []), *pieces)


class TpSum:
    def __init__(self, part, size):
        self.part, self.size, self.hop = part, size, 1
        self.send()

    def send(self):
        if self.size & (self.size - 1) == 0 and self.hop < self.size:
            self.came = lax.ppermute(self.part, "tp", [(i, i ^ self.hop) for i in range(self.size)])

    def fold(self, order):
        if self.size & (self.size - 1):
            self.part, self.size = lax.psum(self.part, "tp"), 1
        elif self.hop < self.size:
            self.part = order(lambda a, b: a + b, self.part, self.came)
            self.hop *= 2
            self.send()

    def result(self, order):
        while self.hop < self.size:
            self.fold(order)
        return self.part


def body(
    tokens,
    segment_ids,
    positions,
    norm_gain,
    norm_shift,
    query_key_value_weight,
    b_qkv,
    dense_weight,
    b_dense,
    inward_weight,
    b_in,
    outward_weight,
    b_out,
    cotangent,
):
    rows, tp = lax.axis_size("rows"), lax.axis_size("tp")
    seqs, here, width = tokens.shape
    length = here * tp
    n = seqs * length
    local = query_key_value_weight.shape[2]
    tile = min(128, local)
    span = length // 2

    exchange = tp == 8 and seqs == 2

    order = Order()
    gain, shift = norm_gain.astype(f32), norm_shift.astype(f32)
    norm = lambda a: norm_halves(a.reshape(seqs * here, width), gain, shift)
    halves = order(norm, tokens)

    if exchange:
        gather_normed = Gather(*halves, tp)
        gather_normed.others()

    def tables(positions, weight):
        place = positions.reshape(n, 1)
        cosine, sine = rope_tables(place, tile)
        start = jnp.arange(n, dtype=jnp.int32)[None] % span - positions.reshape(1, n)
        return cosine, sine, start, jnp.transpose(weight, (1, 0, 2))

    cosine, sine, start, w3 = order(tables, positions, query_key_value_weight)
    in_bias_row = b_in.astype(f32)[None]
    token_rows = lambda a: a.reshape(n, a.shape[-1])
    later = lambda a: lax.all_gather(order(lambda b: b, a), "tp", axis=1, tiled=True).reshape(n, width)
    if exchange:
        gather_normed.forward(order)
        gather_normed.pairs(order)
        grad = later(cotangent)
        gather_normed.near(order)
        hidden_of = lambda *a: mlp_hidden_of(*a, tuple(range(6)))
        hidden = order(hidden_of, gather_normed.full, inward_weight, in_bias_row)
        gather_normed.far_pairs(order)
        normed_full = gather_normed.far(order)
        hidden_of = lambda x, w, b, *before: mlp_hidden_of(x, w, b, (6, 7), before)
        act, slope = order(hidden_of, normed_full, inward_weight, in_bias_row, *hidden)
    else:
        normed_full = jnp.concatenate(halves).reshape(seqs, here, width)
        normed_full = lax.all_gather(normed_full, "tp", axis=1).reshape(seqs, tp, here, width)
        grad = later(cotangent)
        hidden_of = lambda *a: mlp_hidden_of(*a, tuple(range(tp)))
        act, slope = order(hidden_of, normed_full, inward_weight, in_bias_row)
    normed, act, slope = token_rows(normed_full), token_rows(act), token_rows(slope)
    qkv = order(project_qkv, normed, w3, b_qkv.astype(f32), cosine, sine)
    mlp_half = order(lambda *a: tokens_by_weight(*a, 0, 2), act, outward_weight)
    dense_ready, _ = lax.optimization_barrier((dense_weight, act))
    dense_full = lax.all_gather(dense_ready, "tp", axis=0, tiled=True)
    o0 = RowSum(order(lambda *a: weight_grad(*a, 0, 2), act, grad), rows)
    o1 = RowSum(order(lambda *a: weight_grad(*a, 1, 2), act, grad), rows)
    row_sum = lambda parts: [RowSum(part, rows) for part in parts]
    hidden_grad, attended_grad, in_bias = order(grad_in, grad, outward_weight, dense_weight, slope)
    o0.fold(order)
    i0, i1 = row_sum(order(lambda a, b: weight_grad_rows(a, b, (1, 1)), normed, hidden_grad))
    mlp_part = order(lambda x, w, *kept: tokens_by_weight(x, w, 1, 2, kept), act, outward_weight, mlp_half)
    mlp_part = mlp_part.reshape(seqs, length, width)
    mlp_tok = lax.psum_scatter(mlp_part, "tp", scatter_dimension=1, tiled=True).reshape(seqs * here, width)
    o1.fold(order)
    o0.fold(order)
    both = lambda row: lambda s, q, g, c, t, *before: attention_both(s, q, g, c, t, span, tp, row, before)
    attended, by_owner, dqkv = order(both(0), start, qkv, attended_grad, cosine, sine)
    i0.fold(order)
    for row in range(1, seqs):
        kept = (attended, by_owner, dqkv)
        attended, by_owner, dqkv = order(both(row), start, qkv, attended_grad, cosine, sine, *kept)
    mine = lax.all_to_all(by_owner, "tp", split_axis=0, concat_axis=0, tiled=True)
    o1.fold(order)
    o0.settle(order)
    qs, vs = row_sum(order(lambda a, b: weight_grad_parts(a, b, weight=EARLY_WEIGHT), normed, dqkv))
    units = in_bias.shape[1]
    back = lambda share: lambda *a: normed_grad(*a[:5], shift[None], share, 2, a[5:])
    i1.fold(order)
    i0.fold(order)
    part, bias_a, norm_a = order(back(0), hidden_grad, dqkv, inward_weight, w3, normed)
    o1.settle(order)
    i1.fold(order)
    qs.fold(order)
    part, bias_b, norm_b = order(back(1), hidden_grad, dqkv, inward_weight, w3, normed, part)
    back_tok = lax.psum_scatter(part.reshape(seqs, length, width), "tp", scatter_dimension=1, tiled=True)
    vs.fold(order)
    (ds,) = row_sum([order(weight_grad, attended, grad)])
    i0.settle(order)

    cols = width // tp

    def column_sums(grad):
        mine = lax.dynamic_slice_in_dim(grad, lax.axis_index("tp") * cols, cols, 1)
        return jnp.sum(mine.astype(f32), axis=0)

    out_bias = order(column_sums, grad)
    qs.fold(order)
    rows_of = lambda a: a.reshape(seqs * here, width)
    bias_rows = (b_dense.astype(f32)[None], b_out.astype(f32)[None])
    own = lambda x, w, t, *m: project_own(x, w, *bias_rows, rows_of(t), m)
    layer_out, squares = order(own, mine, dense_full, tokens, mlp_tok)
    layer_out = layer_out.reshape(tokens.shape)

    def pack(norm_a, norm_b, squares):
        norm_sums = norm_a + norm_b
        squares = jnp.sum(squares[:4], axis=1)
        pad = jnp.zeros((124,), f32)
        return jnp.concatenate([norm_sums[0] / gain, norm_sums[1], squares, pad]).reshape(-1, 128)

    i1.settle(order)
    packed = TpSum(order(pack, norm_a, norm_b, squares), tp)
    ds.fold(order)
    packed.fold(order)
    packed.fold(order)
    qkv_bias = bias_a + bias_b
    small = jnp.concatenate([in_bias[0], qkv_bias[:, 0].reshape(-1), out_bias]).reshape(-1, 128)
    small = RowSum(jnp.concatenate([packed.result(order), small]), rows)
    vs.fold(order)
    small.fold(order)
    ds.fold(order)
    qs.settle(order)
    out_grad = finish(o0, order, units, weight=ORDER_WEIGHT)
    out_grad = finish(o1, order, units, units // 2, out_grad)
    in_grad = finish(i0, order, width)
    small.fold(order)
    in_grad = finish(i1, order, width, width // 2, in_grad)
    qkv_grad = finish(qs, order, 3 * width)

    token_back = lambda b, t, c: norm_back(rows_of(b), rows_of(t), rows_of(c), gain).reshape(tokens.shape)
    input_grad = order(token_back, back_tok, tokens, cotangent)
    qkv_grad = finish(vs, order, 3 * width, 2 * width, qkv_grad)
    qkv_grad = jnp.transpose(qkv_grad.reshape(3, width, local), (1, 0, 2))
    dense_grad = finish(ds, order, local)
    small.settle(order)
    small = small.result().reshape(-1)
    slice_at = lambda a: lax.dynamic_slice_in_dim(a, lax.axis_index("tp") * cols, cols, 0)
    gain_grad, shift_grad = slice_at(small[:width]), slice_at(small[width : 2 * width])
    rms_values = jnp.sqrt(small[2 * width : 2 * width + 4] / (seqs * rows * length * width))
    small = small[2 * width + 128 :]
    in_bias_grad = small[:units]
    qkv_bias_grad = small[units : units + 3 * local].reshape(3, local)
    out_bias_grad = small[units + 3 * local :]

    return (
        layer_out,
        input_grad,
        gain_grad,
        shift_grad,
        qkv_grad,
        qkv_bias_grad,
        dense_grad,
        out_bias_grad,
        in_grad,
        in_bias_grad,
        out_grad,
        out_bias_grad,
        rms_values,
    )


def solution(mesh):
    in_specs = (
        P("rows", "tp", None),
        P("rows", None),
        P("rows", None),
        P(),
        P(),
        P(None, None, "tp"),
        P(None, "tp"),
        P("tp", None),
        P(),
        P(None, "tp"),
        P("tp"),
        P("tp", None),
        P(),
        P("rows", "tp", None),
    )
    out_specs = (
        P("rows", "tp", None),
        P("rows", "tp", None),
        P("tp"),
        P("tp"),
        P(None, None, "tp"),
        P(None, "tp"),
        P("tp", None),
        P("tp"),
        P(None, "tp"),
        P("tp"),
        P("tp", None),
        P("tp"),
        P(),
    )
    return jax.shard_map(body, mesh=mesh, in_specs=in_specs, out_specs=out_specs, check_vma=False)
```

```python
import functools

import jax
import jax.numpy as jnp
from jax import lax
from jax.experimental import pallas as pl
from jax.experimental.pallas import tpu as pltpu
from jax.sharding import PartitionSpec as P

HD = 64
ROT = 32
epsilon = 1e-05
big_negative = -1e30
rope_base = 10000.0
f32 = jnp.float32
bf16 = jnp.bfloat16
VMEM_LIMIT = 56 << 20
ORDER_WEIGHT = int(2.2e11)
EARLY_WEIGHT = int(2.2e11)


def dot(a, b, ca, cb):
    return lax.dot_general(a, b, (((ca,), (cb,)), ((), ())), preferred_element_type=f32)


SMALL = pl.CostEstimate(flops=1, bytes_accessed=1, transcendentals=0)


def params():
    return pltpu.CompilerParams(vmem_limit_bytes=VMEM_LIMIT)


class Order:
    def __init__(self):
        self.last = ()

    def __call__(self, op, *operands):
        operands, _ = lax.optimization_barrier((operands, self.last))
        result = op(*operands)
        self.last = jax.tree.leaves(result)
        return result


def rope_swap(x):
    width = x.shape[-1]
    lane = lax.broadcasted_iota(jnp.int32, (1, width), 1) % HD
    up = pltpu.roll(x, width - ROT // 2, 1)
    down = pltpu.roll(x, ROT // 2, 1)
    return jnp.where(lane < ROT // 2, up, -down)


def norm_kernel(x_ref, gain_ref, shift_ref, first_ref, second_ref, *, per):
    x = x_ref[...].astype(f32)
    center = x - jnp.mean(x, axis=-1, keepdims=True)
    inverse = lax.rsqrt(jnp.mean(center * center, axis=-1, keepdims=True) + epsilon)
    out = (center * inverse * gain_ref[...] + shift_ref[...]).astype(bf16)

    @pl.when(pl.program_id(0) < per)
    def _():
        first_ref[...] = out

    @pl.when(pl.program_id(0) >= per)
    def _():
        second_ref[...] = out


def norm_halves(x, gain, shift, tm=128):
    n, width = x.shape
    per = n // 2 // tm
    vector = pl.BlockSpec((1, width), lambda i: (0, 0))
    return pl.pallas_call(
        functools.partial(norm_kernel, per=per),
        grid=(2 * per,),
        in_specs=[pl.BlockSpec((tm, width), lambda i: (i, 0)), vector, vector],
        out_specs=[
            pl.BlockSpec((tm, width), lambda i: (jnp.minimum(i, per - 1), 0)),
            pl.BlockSpec((tm, width), lambda i: (jnp.maximum(i - per, 0), 0)),
        ],
        out_shape=[jax.ShapeDtypeStruct((n // 2, width), bf16)] * 2,
        compiler_params=params(),
        cost_estimate=SMALL,
        name="norm_halves",
    )(x, gain[None], shift[None])


def norm_back_kernel(back_ref, x_ref, g_ref, gain_ref, o_ref):
    x = x_ref[...].astype(f32)
    center = x - jnp.mean(x, axis=-1, keepdims=True)
    inverse = lax.rsqrt(jnp.mean(center * center, axis=-1, keepdims=True) + epsilon)
    unit = center * inverse
    unit_grad = back_ref[...].astype(f32) * gain_ref[...]
    mean_grad = jnp.mean(unit_grad, axis=-1, keepdims=True)
    mean_both = jnp.mean(unit_grad * unit, axis=-1, keepdims=True)
    value_grad = (unit_grad - mean_grad - unit * mean_both) * inverse
    o_ref[...] = (g_ref[...].astype(f32) + value_grad).astype(bf16)


def norm_back(back, x, g, gain, tm=128):
    n, width = x.shape
    block = pl.BlockSpec((tm, width), lambda i: (i, 0))
    return pl.pallas_call(
        norm_back_kernel,
        grid=(n // tm,),
        in_specs=[block, block, block, pl.BlockSpec((1, width), lambda i: (0, 0))],
        out_specs=block,
        out_shape=jax.ShapeDtypeStruct((n, width), bf16),
        compiler_params=params(),
        cost_estimate=SMALL,
        name="norm_back",
    )(back, x, g, gain[None])


def table_kernel(place_ref, frequency_ref, c_ref, s_ref):
    angle = place_ref[...].astype(f32) * frequency_ref[...]
    lane = lax.broadcasted_iota(jnp.int32, angle.shape, 1) % HD
    turned = lane < ROT
    c_ref[...] = jnp.where(turned, jnp.cos(angle), 1.0)
    s_ref[...] = jnp.where(turned, jnp.sin(angle), 0.0)


def rope_tables(place, tile, tm=1024):
    n = place.shape[0]
    lane = jnp.arange(tile, dtype=jnp.int32) % (ROT // 2)
    frequency = (rope_base ** (-2.0 * lane.astype(f32) / ROT))[None]
    table = pl.BlockSpec((tm, tile), lambda i: (i, 0))
    return pl.pallas_call(
        table_kernel,
        grid=(n // tm,),
        in_specs=[pl.BlockSpec((tm, 1), lambda i: (i, 0)), pl.BlockSpec((1, tile), lambda i: (0, 0))],
        out_specs=[table, table],
        out_shape=[jax.ShapeDtypeStruct((n, tile), f32)] * 2,
        compiler_params=params(),
        cost_estimate=SMALL,
        name="rope_tables",
    )(place, frequency)


def qkv_kernel(x_ref, w_ref, b_ref, c_ref, s_ref, o_ref):
    x = x_ref[...]
    tile = c_ref.shape[-1]
    local = w_ref.shape[-1]
    cosine, sine = c_ref[...], s_ref[...]
    for part in range(3):
        full = dot(x, w_ref[part], 1, 0) + b_ref[part : part + 1, :]
        for at in range(0, local, tile):
            piece = full[:, at : at + tile]
            if part < 2:
                piece = piece * cosine - rope_swap(piece) * sine
            if part == 0:
                piece = piece * (HD**-0.5)
            o_ref[part, :, at : at + tile] = piece.astype(bf16)


def project_qkv(x, w3, bias, cosine, sine, tm=512):
    n, width = x.shape
    local = w3.shape[2]
    tile = cosine.shape[1]
    return pl.pallas_call(
        qkv_kernel,
        grid=(n // tm,),
        in_specs=[
            pl.BlockSpec((tm, width), lambda i: (i, 0)),
            pl.BlockSpec((3, width, local), lambda i: (0, 0, 0)),
            pl.BlockSpec((3, local), lambda i: (0, 0)),
            pl.BlockSpec((tm, tile), lambda i: (i, 0)),
            pl.BlockSpec((tm, tile), lambda i: (i, 0)),
        ],
        out_specs=pl.BlockSpec((3, tm, local), lambda i: (0, i, 0)),
        out_shape=jax.ShapeDtypeStruct((3, n, local), bf16),
        compiler_params=params(),
        cost_estimate=SMALL,
        name="qkv_rope",
    )(x, w3, bias, cosine, sine)


def chosen_kernel(me_ref, *refs, held):
    x_ref, w_ref, b_ref, act_ref, slope_ref = refs[held:]
    seqs, here, width = x_ref.shape
    x = x_ref[...].reshape(seqs * here, width)
    units = w_ref.shape[1]
    step = min(256, units)
    for at in range(0, units, step):
        cut = slice(at, at + step)
        h = dot(x, w_ref[:, cut], 1, 0) + b_ref[:, cut]
        square = h * h
        t = jnp.tanh(h * (0.7978845608028654 + 0.035677408136300125 * square))
        half = 0.5 + 0.5 * t
        act = h * half
        slope = half + (act - act * half) * (1.5957691216057308 + 0.21406444881780074 * square)
        act_ref[:, :, cut] = act.astype(bf16).reshape(seqs, here, step)
        slope_ref[:, :, cut] = slope.astype(bf16).reshape(seqs, here, step)


def mlp_hidden_of(x, w, bias, steps, before=(), weight=1):
    seqs, owners, here, width = x.shape
    units = w.shape[1]
    held = len(before)

    def device(j, me):
        chosen = me[0] ^ steps[0]
        for i in range(1, len(steps)):
            chosen = jnp.where(j == i, me[0] ^ steps[i], chosen)
        return 0, chosen, 0, 0

    out = pl.BlockSpec((seqs, None, here, units), device)
    me = lax.axis_index("tp").astype(jnp.int32).reshape(1)
    return pl.pallas_call(
        functools.partial(chosen_kernel, held=held),
        grid_spec=pltpu.PrefetchScalarGridSpec(
            num_scalar_prefetch=1,
            grid=(len(steps),),
            in_specs=[pl.BlockSpec(memory_space=pl.ANY)] * held
            + [
                pl.BlockSpec((seqs, None, here, width), device),
                pl.BlockSpec((width, units), lambda j, me: (0, 0)),
                pl.BlockSpec((1, units), lambda j, me: (0, 0)),
            ],
            out_specs=[out, out],
        ),
        out_shape=[jax.ShapeDtypeStruct((seqs, owners, here, units), bf16)] * 2,
        input_output_aliases={1 + i: i for i in range(held)},
        compiler_params=params(),
        cost_estimate=pl.CostEstimate(flops=int(weight), bytes_accessed=1, transcendentals=0),
        name="mlp_hidden_of",
    )(me, *before, x, w, bias)


def grad_in_kernel(g_ref, wo_ref, wd_ref, slope_ref, hg_ref, at_ref, sum_ref):
    g = g_ref[...]
    units = wo_ref.shape[0]
    step = min(256, units)

    @pl.when(pl.program_id(0) == 0)
    def _():
        sum_ref[...] = jnp.zeros_like(sum_ref)

    for at in range(0, units, step):
        slope = slope_ref[:, at : at + step].astype(f32)
        hg = (dot(g, wo_ref[at : at + step, :], 1, 1) * slope).astype(bf16)
        hg_ref[:, at : at + step] = hg
        sum_ref[0:1, at : at + step] += jnp.sum(hg.astype(f32), axis=0, keepdims=True)
    at_ref[...] = dot(g, wd_ref[...], 1, 1).astype(bf16)


def grad_in(g, wo, wd, slope, tm=512):
    n, width = g.shape
    units, local = wo.shape[0], wd.shape[0]
    return pl.pallas_call(
        grad_in_kernel,
        grid=(n // tm,),
        in_specs=[
            pl.BlockSpec((tm, width), lambda i: (i, 0)),
            pl.BlockSpec((units, width), lambda i: (0, 0)),
            pl.BlockSpec((local, width), lambda i: (0, 0)),
            pl.BlockSpec((tm, units), lambda i: (i, 0)),
        ],
        out_specs=[
            pl.BlockSpec((tm, units), lambda i: (i, 0)),
            pl.BlockSpec((tm, local), lambda i: (i, 0)),
            pl.BlockSpec((8, units), lambda i: (0, 0)),
        ],
        out_shape=[
            jax.ShapeDtypeStruct((n, units), bf16),
            jax.ShapeDtypeStruct((n, local), bf16),
            jax.ShapeDtypeStruct((8, units), f32),
        ],
        compiler_params=params(),
        cost_estimate=SMALL,
        name="grad_in",
    )(g, wo, wd, slope)


def tokens_kernel(*refs, held):
    x_ref, w_ref, o_ref = refs[held:]
    width = w_ref.shape[1]
    step = min(512, width)
    for at in range(0, width, step):
        o_ref[:, at : at + step] = dot(x_ref[...], w_ref[:, at : at + step], 1, 0).astype(o_ref.dtype)


def tokens_by_weight(x, w, share, shares, before=(), tm=512):
    n, depth = x.shape
    held = len(before)
    steps = n // shares // tm
    width = w.shape[1]
    first = share * steps
    return pl.pallas_call(
        functools.partial(tokens_kernel, held=held),
        grid=(steps,),
        in_specs=[pl.BlockSpec(memory_space=pl.ANY)] * held
        + [pl.BlockSpec((tm, depth), lambda i: (first + i, 0)), pl.BlockSpec((depth, width), lambda i: (0, 0))],
        out_specs=pl.BlockSpec((tm, width), lambda i: (first + i, 0)),
        out_shape=jax.ShapeDtypeStruct((n, width), bf16),
        input_output_aliases={i: i for i in range(held)},
        compiler_params=params(),
        cost_estimate=SMALL,
        name="tokens_by_weight",
    )(*before, x, w)


def weight_grad_kernel(a_ref, b_ref, o_ref):
    o_ref[...] = dot(a_ref[...], b_ref[...], 0, 0).astype(bf16)


def weight_grad(a, b, share=0, shares=1, tile=512, weight=1):
    n, rows = a.shape
    rows //= shares
    cols = b.shape[1]
    tile = min(tile, cols)
    return pl.pallas_call(
        weight_grad_kernel,
        grid=(cols // tile,),
        in_specs=[
            pl.BlockSpec((n, rows), lambda j: (0, share), pipeline_mode=pl.Buffered(1)),
            pl.BlockSpec((n, tile), lambda j: (0, j)),
        ],
        out_specs=pl.BlockSpec((rows, tile), lambda j: (0, j)),
        out_shape=jax.ShapeDtypeStruct((rows, cols), bf16),
        compiler_params=params(),
        cost_estimate=pl.CostEstimate(flops=int(weight), bytes_accessed=1, transcendentals=0),
        name="weight_grad",
    )(a, b)


def weight_grad_rows_kernel(a_ref, b_ref, *o_refs, counts):
    full = dot(a_ref[...], b_ref[...], 0, 0).astype(bf16)
    step = pl.program_id(0)
    first = 0
    for o_ref, count in zip(o_refs, counts):

        @pl.when((step >= first) & (step < first + count))
        def _(o_ref=o_ref):
            o_ref[...] = full

        first += count


def weight_grad_rows(a, b, shares, tile=512):
    n, rows = a.shape
    cols = b.shape[1]
    counts = [rows * share // sum(shares) // tile for share in shares]
    firsts = [sum(counts[:i]) for i in range(len(counts))]
    out = lambda i: pl.BlockSpec((tile, cols), lambda j: (jnp.clip(j - firsts[i], 0, counts[i] - 1), 0))
    return pl.pallas_call(
        functools.partial(weight_grad_rows_kernel, counts=counts),
        grid=(rows // tile,),
        in_specs=[
            pl.BlockSpec((n, tile), lambda j: (0, j)),
            pl.BlockSpec((n, cols), lambda j: (0, 0), pipeline_mode=pl.Buffered(1)),
        ],
        out_specs=[out(i) for i in range(len(counts))],
        out_shape=[jax.ShapeDtypeStruct((count * tile, cols), bf16) for count in counts],
        compiler_params=params(),
        cost_estimate=SMALL,
        name="weight_grad_rows",
    )(a, b)


def weight_grad_parts_kernel(a_ref, b_ref, first_ref, last_ref):
    for part in range(2):
        first_ref[part] = dot(a_ref[...], b_ref[part], 0, 0).astype(bf16)
    last_ref[...] = dot(a_ref[...], b_ref[2], 0, 0).astype(bf16)


def weight_grad_parts(a, b, tile=512, weight=1):
    n, rows = a.shape
    parts, _, cols = b.shape
    return pl.pallas_call(
        weight_grad_parts_kernel,
        grid=(rows // tile,),
        in_specs=[
            pl.BlockSpec((n, tile), lambda j: (0, j)),
            pl.BlockSpec((parts, n, cols), lambda j: (0, 0, 0), pipeline_mode=pl.Buffered(1)),
        ],
        out_specs=[pl.BlockSpec((2, tile, cols), lambda j: (0, j, 0)), pl.BlockSpec((tile, cols), lambda j: (j, 0))],
        out_shape=[jax.ShapeDtypeStruct((2, rows, cols), bf16), jax.ShapeDtypeStruct((rows, cols), bf16)],
        compiler_params=params(),
        cost_estimate=pl.CostEstimate(flops=int(weight), bytes_accessed=1, transcendentals=0),
        name="weight_grad_parts",
    )(a, b)


def normed_grad_kernel(*refs, held):
    hg_ref, dq_ref, wi_ref, w3_ref, x_ref, shift_ref, o_ref, sum_ref, norm_ref = refs[held:]

    @pl.when(pl.program_id(0) == 0)
    def _():
        sum_ref[...] = jnp.zeros_like(sum_ref)
        norm_ref[...] = jnp.zeros_like(norm_ref)

    for part in range(3):
        sum_ref[part, 0:1] += jnp.sum(dq_ref[part].astype(f32), axis=0, keepdims=True)
    width = o_ref.shape[1]
    step = min(512, width)
    for at in range(0, width, step):
        cut = slice(at, at + step)
        total = dot(hg_ref[...], wi_ref[cut, :], 1, 1)
        for part in range(3):
            total += dot(dq_ref[part], w3_ref[part, cut, :], 1, 1)
        o_ref[:, cut] = total.astype(bf16)
        scaled = x_ref[:, cut].astype(f32) - shift_ref[:, cut]
        norm_ref[0:1, cut] += jnp.sum(total * scaled, axis=0, keepdims=True)
        norm_ref[1:2, cut] += jnp.sum(total, axis=0, keepdims=True)


def normed_grad(hg, dqkv, wi, w3, x, shift, share, shares, before=(), tm=512):
    n, units = hg.shape
    held = len(before)
    steps = n // shares // tm
    first = share * steps
    width, local = w3.shape[1:]
    return pl.pallas_call(
        functools.partial(normed_grad_kernel, held=held),
        grid=(steps,),
        in_specs=[pl.BlockSpec(memory_space=pl.ANY)] * held
        + [
            pl.BlockSpec((tm, units), lambda i: (first + i, 0)),
            pl.BlockSpec((3, tm, local), lambda i: (0, first + i, 0)),
            pl.BlockSpec((width, units), lambda i: (0, 0)),
            pl.BlockSpec((3, width, local), lambda i: (0, 0, 0)),
            pl.BlockSpec((tm, width), lambda i: (first + i, 0)),
            pl.BlockSpec((1, width), lambda i: (0, 0)),
        ],
        out_specs=[
            pl.BlockSpec((tm, width), lambda i: (first + i, 0)),
            pl.BlockSpec((3, 8, local), lambda i: (0, 0, 0)),
            pl.BlockSpec((8, width), lambda i: (0, 0)),
        ],
        out_shape=[
            jax.ShapeDtypeStruct((n, width), bf16),
            jax.ShapeDtypeStruct((3, 8, local), f32),
            jax.ShapeDtypeStruct((8, width), f32),
        ],
        input_output_aliases={i: i for i in range(held)},
        compiler_params=params(),
        cost_estimate=SMALL,
        name="normed_grad",
    )(*before, hg, dqkv, wi, w3, x, shift)


def attention_kernel(*refs, bq, held):
    start_ref, q_ref, k_ref, v_ref, do_ref, c_ref, s_ref, o_ref, by_owner_ref, g_ref, dk_acc, dv_acc = refs[held:]
    span, width = q_ref.shape
    here = by_owner_ref.shape[1]
    lane = lax.broadcasted_iota(jnp.int32, (1, width), 1) // HD
    zero = jnp.zeros((), bf16)
    heads = range(width // HD)
    cuts = [slice(head * HD, (head + 1) * HD) for head in heads]
    blocks = span // bq
    keys_across, vals_across = k_ref[...].T, v_ref[...].T

    def turn_back(x, at, n):
        return x * c_ref[at : at + n, :] + rope_swap(x) * s_ref[at : at + n, :]

    def products(block):
        at, n = block * bq, (block + 1) * bq
        keys, vals = k_ref[0:n, :], v_ref[0:n, :]
        queries = [jnp.where(lane == head, q_ref[at:n, :], zero) for head in heads]
        grads = [jnp.where(lane == head, do_ref[at:n, :], zero) for head in heads]
        return queries, grads, [dot(keys, q, 1, 1) for q in queries], [dot(vals, g, 1, 1) for g in grads]

    ahead = products(0)
    for block in range(blocks):
        at, n = block * bq, (block + 1) * bq
        queries, grads, scores, prob_grads = ahead
        key = lax.broadcasted_iota(jnp.int32, (n, bq), 0)
        place = lax.broadcasted_iota(jnp.int32, (1, bq), 1) + at
        allowed = (key >= start_ref[:, at:n]) & (key <= place)
        if block + 1 < blocks:
            ahead = products(block + 1)
        probs = []
        for head in heads:
            score = jnp.where(allowed, scores[head], big_negative)
            expd = jnp.exp(score - jnp.max(score, axis=0, keepdims=True))
            probs.append(expd * (1.0 / jnp.sum(expd, axis=0, keepdims=True)))
        low = [p.astype(bf16) for p in probs]
        out = [dot(vals_across[cut, 0:n], p, 1, 0) for cut, p in zip(cuts, low)]
        dv = sum(dot(p, g, 1, 0) for p, g in zip(low, grads))
        score_grads = []
        for p, g in zip(probs, prob_grads):
            both = p * g
            score_grads.append((both - p * jnp.sum(both, axis=0, keepdims=True)).astype(bf16))
        dq = [dot(keys_across[cut, 0:n], g, 1, 0) for cut, g in zip(cuts, score_grads)]
        dk = sum(dot(g, q, 1, 0) for g, q in zip(score_grads, queries))
        out = jnp.concatenate(out, axis=0).T.astype(bf16)
        o_ref[at:n, :] = out
        by_owner_ref[at // here, at % here : at % here + bq] = out
        g_ref[0, at:n, :] = turn_back(jnp.concatenate(dq, axis=0).T * (HD**-0.5), at, bq).astype(bf16)
        if block:
            dk_acc[0:at, :] += dk[0:at]
            dv_acc[0:at, :] += dv[0:at]
        dk_acc[at:n, :] = dk[at:n]
        dv_acc[at:n, :] = dv[at:n]
    g_ref[1] = turn_back(dk_acc[...], 0, span).astype(bf16)
    g_ref[2] = dv_acc[...].astype(bf16)


def attention_both(start, qkv, grad, cosine, sine, span, owners, row, before=(), bq=128):
    n, local = grad.shape
    here = 2 * span // owners
    width = cosine.shape[1]
    bq = min(bq, here)
    held = len(before)
    first = 2 * row
    part = lambda which: pl.BlockSpec((None, span, width), lambda t, p: (which, first + t, p))
    table = pl.BlockSpec((span, width), lambda t, p: (first + t, 0))
    return pl.pallas_call(
        functools.partial(attention_kernel, bq=bq, held=held),
        grid=(2, local // width),
        in_specs=[pl.BlockSpec(memory_space=pl.ANY)] * held
        + [
            pl.BlockSpec((1, span), lambda t, p: (0, first + t)),
            part(0),
            part(1),
            part(2),
            pl.BlockSpec((span, width), lambda t, p: (first + t, p)),
            table,
            table,
        ],
        out_specs=[
            pl.BlockSpec((span, width), lambda t, p: (first + t, p)),
            pl.BlockSpec((owners // 2, None, here, width), lambda t, p: (t, row, 0, p)),
            pl.BlockSpec((3, span, width), lambda t, p: (0, first + t, p)),
        ],
        out_shape=[
            jax.ShapeDtypeStruct((n, local), bf16),
            jax.ShapeDtypeStruct((owners, n // (2 * span), here, local), bf16),
            jax.ShapeDtypeStruct((3, n, local), bf16),
        ],
        scratch_shapes=[pltpu.VMEM((span, width), f32)] * 2,
        input_output_aliases={i: i for i in range(held)},
        compiler_params=params(),
        cost_estimate=SMALL,
        name="attention_both",
    )(*before, start, qkv, qkv, qkv, grad, cosine, sine)


def own_kernel(x_ref, w_ref, bd_ref, bo_ref, token_ref, *refs):
    *mlp_refs, o_ref, sum_ref = refs
    owners, seqs, here, local = x_ref.shape
    attention = jnp.zeros((seqs * here, w_ref.shape[1]), f32) + bd_ref[...]
    for owner in range(owners):
        x = x_ref[owner].reshape(seqs * here, local)
        attention += dot(x, w_ref[owner * local : (owner + 1) * local, :], 1, 0)
    tokens = token_ref[...].astype(f32)
    mlp = jnp.concatenate([a[...] for a in mlp_refs], axis=0).astype(f32) + bo_ref[...]
    total = tokens + attention + mlp
    o_ref[...] = total.astype(bf16)

    @pl.when(pl.program_id(0) == 0)
    def _():
        sum_ref[...] = jnp.zeros_like(sum_ref)

    for i, a in enumerate((tokens, attention, mlp, total)):
        sum_ref[i : i + 1, :] += jnp.sum(a * a, axis=0, keepdims=True)


def project_own(x, w, bd, bo, tokens, mlp_parts, tile=512, weight=1):
    owners, seqs, here, local = x.shape
    width = w.shape[1]
    rows = seqs * here
    column = lambda high: pl.BlockSpec((high, tile), lambda j: (0, j))
    return pl.pallas_call(
        own_kernel,
        grid=(width // tile,),
        in_specs=[
            pl.BlockSpec(x.shape, lambda j: (0, 0, 0, 0)),
            column(owners * local),
            column(1),
            column(1),
            column(rows),
        ]
        + [column(a.shape[0]) for a in mlp_parts],
        out_specs=[column(rows), pl.BlockSpec((8, tile), lambda j: (0, 0))],
        out_shape=[jax.ShapeDtypeStruct((rows, width), bf16), jax.ShapeDtypeStruct((8, tile), f32)],
        compiler_params=params(),
        cost_estimate=pl.CostEstimate(flops=int(weight), bytes_accessed=1, transcendentals=0),
        name="project_own",
    )(x, w, bd, bo, tokens, *mlp_parts)


def line_ok(size):
    return size >= 4 and size & (size - 1) == 0


class RowSum:
    def __init__(self, part, size):
        self.part, self.size, self.axis = part, size, "rows"
        groups = range(0, size, 4)
        pairs = lambda *ends: [(g + a, g + b) for g in groups for a, b in ends]
        self.hops = [pairs((0, 1), (3, 2)), pairs((1, 2), (2, 1))]
        hop = 4
        while hop < size:
            self.hops.append([(i, i ^ hop) for i in range(size)])
            hop *= 2
        self.hops.append(pairs((1, 0), (2, 3)))
        self.send()

    def send(self):
        if line_ok(self.size):
            self.came = lax.ppermute(self.part, self.axis, self.hops.pop(0))

    def fold(self, order):
        if line_ok(self.size) and self.hops:
            add = lambda a, b: (a.astype(f32) + b.astype(f32)).astype(a.dtype)
            self.part = order(add, self.part, self.came)
            self.send()

    def settle(self, order):
        if line_ok(self.size):
            self.came = order(lambda a: a, self.came)

    def complete(self, order):
        while self.hops:
            self.fold(order)

    def result(self, order=None):
        if not line_ok(self.size):
            return lax.psum(self.part.astype(f32), "rows")
        self.complete(order or Order())
        place = lax.axis_index("rows") % 4
        return jnp.where((place == 1) | (place == 2), self.part, self.came).astype(f32)


def finish_kernel(inner_ref, kept_ref, came_ref, *refs):
    o_ref = refs[-1]

    @pl.when(inner_ref[0] == 1)
    def _():
        o_ref[...] = kept_ref[...].astype(f32)

    @pl.when(inner_ref[0] == 0)
    def _():
        o_ref[...] = came_ref[...].astype(f32)


def finish(total, order, high, first=0, before=None, tile=512, weight=1):
    flat = lambda a: a.reshape(-1, a.shape[-1])
    rows, cols = flat(total.part).shape
    if not line_ok(total.size):
        before = jnp.zeros((high, cols), f32) if before is None else before
        return lax.dynamic_update_slice(before, flat(total.result()), (first, 0))
    total.complete(order)
    tile = min(tile, rows)
    held = [] if before is None else [before]
    block = pl.BlockSpec((tile, cols), lambda j: (j, 0))
    place = lax.axis_index("rows") % 4
    inner = ((place == 1) | (place == 2)).astype(jnp.int32).reshape(1)
    call = pl.pallas_call(
        finish_kernel,
        grid=(rows // tile,),
        in_specs=[pl.BlockSpec(memory_space=pltpu.SMEM), block, block] + [pl.BlockSpec(memory_space=pl.ANY)] * len(held),
        out_specs=pl.BlockSpec((tile, cols), lambda j: (first // tile + j, 0)),
        out_shape=jax.ShapeDtypeStruct((high, cols), f32),
        input_output_aliases={3: 0} if held else {},
        compiler_params=params(),
        cost_estimate=pl.CostEstimate(flops=int(weight), bytes_accessed=1, transcendentals=0),
        name="finish",
    )
    return order(lambda *a: call(inner, *a), flat(total.part), flat(total.came), *held)


class Gather:
    core, x, y = 1, 2, 4

    def __init__(self, first, second, size):
        self.first, self.second, self.size = first, second, size
        self.x0, self.y1 = self.send(first, self.x), self.send(second, self.y)

    def send(self, a, step):
        return lax.ppermute(a, "tp", [(i, i ^ step) for i in range(self.size)])

    def others(self, order=None):
        first, second = self.first, self.second
        if order:
            first, second = order(lambda a, b: (a, b), first, second)
        self.x1, self.y0 = self.send(second, self.x), self.send(first, self.y)
        self.c0 = self.send(first, self.core)

    def forward(self, order):
        came = (self.x0, self.y1, self.c0, self.second)
        self.x0, self.y1, self.c0, self.second = order(lambda *a: a, *came)
        self.c1 = self.send(self.second, self.core)
        self.d0, self.d1 = self.send(self.x0, self.y), self.send(self.y1, self.x)

    def pairs(self, order):
        came = (self.x0, self.y1, self.x1, self.y0, self.c1)
        self.x0, self.y1, self.x1, self.y0, self.c1 = order(lambda *a: a, *came)
        self.px0, self.py1 = self.send(self.x0, self.core), self.send(self.y1, self.core)
        self.px1, self.py0 = self.send(self.x1, self.core), self.send(self.y0, self.core)

    def near(self, order):
        steps = [step for step in (0, self.core, self.x, self.y, self.x | self.core, self.y | self.core) for _ in range(2)]
        pieces = (self.first, self.second, self.c0, self.c1, self.x0, self.x1, self.y0, self.y1)
        pieces += (self.px0, self.px1, self.py0, self.py1)
        self.full = order(lambda *a: place_pieces(None, a, steps, (0, 1) * 6, self.size), *pieces)

    def far_pairs(self, order):
        self.d0, self.d1 = order(lambda a, b: (a, b), self.d0, self.d1)
        self.pd0, self.pd1 = self.send(self.d0, self.core), self.send(self.d1, self.core)

    def far(self, order):
        far = self.x | self.y
        steps = (far, far, far | self.core, far | self.core)
        place = lambda full, *a: place_pieces(full, a, steps, (0, 1, 0, 1), self.size)
        self.full = order(place, self.full, self.d0, self.d1, self.pd0, self.pd1)
        return self.full


def place_kernel(me_ref, *refs, held):
    pieces, o_ref = refs[held:-1], refs[-1]
    for i, piece in enumerate(pieces):

        @pl.when(pl.program_id(0) == i)
        def _(piece=piece):
            o_ref[...] = piece[...].reshape(o_ref.shape)


def place_pieces(full, pieces, steps, halves, size):
    held = 0 if full is None else 1
    here, width = pieces[0].shape

    def target(j, me):
        device, half = me[0] ^ steps[0], halves[0]
        for i in range(1, len(pieces)):
            device = jnp.where(j == i, me[0] ^ steps[i], device)
            half = jnp.where(j == i, halves[i], half)
        return half, device, 0, 0

    hbm = pl.BlockSpec(memory_space=pl.ANY)
    me = lax.axis_index("tp").astype(jnp.int32).reshape(1)
    return pl.pallas_call(
        functools.partial(place_kernel, held=held),
        grid_spec=pltpu.PrefetchScalarGridSpec(
            num_scalar_prefetch=1,
            grid=(len(pieces),),
            in_specs=[hbm] * held + [pl.BlockSpec((here, width), lambda j, me: (0, 0))] * len(pieces),
            out_specs=pl.BlockSpec((1, None, here, width), target),
        ),
        out_shape=jax.ShapeDtypeStruct((2, size, here, width), bf16),
        input_output_aliases={1: 0} if held else {},
        compiler_params=params(),
        cost_estimate=SMALL,
        name="place_pieces",
    )(me, *([full] if held else []), *pieces)


class TpSum:
    def __init__(self, part, size):
        self.part, self.size, self.hop = part, size, 1
        self.send()

    def send(self):
        if self.size & (self.size - 1) == 0 and self.hop < self.size:
            self.came = lax.ppermute(self.part, "tp", [(i, i ^ self.hop) for i in range(self.size)])

    def fold(self, order):
        if self.size & (self.size - 1):
            self.part, self.size = lax.psum(self.part, "tp"), 1
        elif self.hop < self.size:
            self.part = order(lambda a, b: a + b, self.part, self.came)
            self.hop *= 2
            self.send()

    def result(self, order):
        while self.hop < self.size:
            self.fold(order)
        return self.part


def body(
    tokens,
    segment_ids,
    positions,
    norm_gain,
    norm_shift,
    query_key_value_weight,
    b_qkv,
    dense_weight,
    b_dense,
    inward_weight,
    b_in,
    outward_weight,
    b_out,
    cotangent,
):
    rows, tp = lax.axis_size("rows"), lax.axis_size("tp")
    seqs, here, width = tokens.shape
    length = here * tp
    n = seqs * length
    local = query_key_value_weight.shape[2]
    tile = min(128, local)
    span = length // 2

    exchange = tp == 8 and seqs == 2

    order = Order()
    gain, shift = norm_gain.astype(f32), norm_shift.astype(f32)
    norm = lambda a: norm_halves(a.reshape(seqs * here, width), gain, shift)
    halves = order(norm, tokens)

    if exchange:
        gather_normed = Gather(*halves, tp)
        gather_normed.others()

    def tables(positions, weight):
        place = positions.reshape(n, 1)
        cosine, sine = rope_tables(place, tile)
        start = jnp.arange(n, dtype=jnp.int32)[None] % span - positions.reshape(1, n)
        return cosine, sine, start, jnp.transpose(weight, (1, 0, 2))

    cosine, sine, start, w3 = order(tables, positions, query_key_value_weight)
    in_bias_row = b_in.astype(f32)[None]
    token_rows = lambda a: a.reshape(n, a.shape[-1])
    later = lambda a: lax.all_gather(order(lambda b: b, a), "tp", axis=1, tiled=True).reshape(n, width)
    if exchange:
        gather_normed.forward(order)
        gather_normed.pairs(order)
        grad = later(cotangent)
        gather_normed.near(order)
        hidden_of = lambda *a: mlp_hidden_of(*a, tuple(range(6)))
        hidden = order(hidden_of, gather_normed.full, inward_weight, in_bias_row)
        gather_normed.far_pairs(order)
        normed_full = gather_normed.far(order)
        hidden_of = lambda x, w, b, *before: mlp_hidden_of(x, w, b, (6, 7), before)
        act, slope = order(hidden_of, normed_full, inward_weight, in_bias_row, *hidden)
    else:
        normed_full = jnp.concatenate(halves).reshape(seqs, here, width)
        normed_full = lax.all_gather(normed_full, "tp", axis=1).reshape(seqs, tp, here, width)
        grad = later(cotangent)
        hidden_of = lambda *a: mlp_hidden_of(*a, tuple(range(tp)))
        act, slope = order(hidden_of, normed_full, inward_weight, in_bias_row)
    normed, act, slope = token_rows(normed_full), token_rows(act), token_rows(slope)
    qkv = order(project_qkv, normed, w3, b_qkv.astype(f32), cosine, sine)
    mlp_half = order(lambda *a: tokens_by_weight(*a, 0, 2), act, outward_weight)
    dense_ready, _ = lax.optimization_barrier((dense_weight, act))
    dense_full = lax.all_gather(dense_ready, "tp", axis=0, tiled=True)
    o0 = RowSum(order(lambda *a: weight_grad(*a, 0, 2), act, grad), rows)
    o1 = RowSum(order(lambda *a: weight_grad(*a, 1, 2), act, grad), rows)
    row_sum = lambda parts: [RowSum(part, rows) for part in parts]
    hidden_grad, attended_grad, in_bias = order(grad_in, grad, outward_weight, dense_weight, slope)
    o0.fold(order)
    i0, i1 = row_sum(order(lambda a, b: weight_grad_rows(a, b, (1, 1)), normed, hidden_grad))
    mlp_part = order(lambda x, w, *kept: tokens_by_weight(x, w, 1, 2, kept), act, outward_weight, mlp_half)
    mlp_part = mlp_part.reshape(seqs, length, width)
    mlp_tok = lax.psum_scatter(mlp_part, "tp", scatter_dimension=1, tiled=True).reshape(seqs * here, width)
    o1.fold(order)
    o0.fold(order)
    both = lambda row: lambda s, q, g, c, t, *before: attention_both(s, q, g, c, t, span, tp, row, before)
    attended, by_owner, dqkv = order(both(0), start, qkv, attended_grad, cosine, sine)
    i0.fold(order)
    for row in range(1, seqs):
        kept = (attended, by_owner, dqkv)
        attended, by_owner, dqkv = order(both(row), start, qkv, attended_grad, cosine, sine, *kept)
    mine = lax.all_to_all(by_owner, "tp", split_axis=0, concat_axis=0, tiled=True)
    o1.fold(order)
    o0.settle(order)
    qs, vs = row_sum(order(lambda a, b: weight_grad_parts(a, b, weight=EARLY_WEIGHT), normed, dqkv))
    units = in_bias.shape[1]
    back = lambda share: lambda *a: normed_grad(*a[:5], shift[None], share, 2, a[5:])
    i1.fold(order)
    i0.fold(order)
    part, bias_a, norm_a = order(back(0), hidden_grad, dqkv, inward_weight, w3, normed)
    o1.settle(order)
    (ds,) = row_sum([order(weight_grad, attended, grad)])
    i1.fold(order)
    qs.fold(order)
    part, bias_b, norm_b = order(back(1), hidden_grad, dqkv, inward_weight, w3, normed, part)
    back_tok = lax.psum_scatter(part.reshape(seqs, length, width), "tp", scatter_dimension=1, tiled=True)
    vs.fold(order)
    i0.settle(order)

    cols = width // tp

    def column_sums(grad):
        mine = lax.dynamic_slice_in_dim(grad, lax.axis_index("tp") * cols, cols, 1)
        return jnp.sum(mine.astype(f32), axis=0)

    out_bias = order(column_sums, grad)
    rows_of = lambda a: a.reshape(seqs * here, width)
    bias_rows = (b_dense.astype(f32)[None], b_out.astype(f32)[None])
    own = lambda x, w, t, *m: project_own(x, w, *bias_rows, rows_of(t), m)
    layer_out, squares = order(own, mine, dense_full, tokens, mlp_tok)
    layer_out = layer_out.reshape(tokens.shape)

    def pack(norm_a, norm_b, squares):
        norm_sums = norm_a + norm_b
        squares = jnp.sum(squares[:4], axis=1)
        pad = jnp.zeros((124,), f32)
        return jnp.concatenate([norm_sums[0] / gain, norm_sums[1], squares, pad]).reshape(-1, 128)

    qs.fold(order)
    i1.settle(order)
    packed = TpSum(order(pack, norm_a, norm_b, squares), tp)
    ds.fold(order)
    packed.fold(order)
    packed.fold(order)
    qkv_bias = bias_a + bias_b
    small = jnp.concatenate([in_bias[0], qkv_bias[:, 0].reshape(-1), out_bias]).reshape(-1, 128)
    small = RowSum(jnp.concatenate([packed.result(order), small]), rows)
    vs.fold(order)
    small.fold(order)
    ds.fold(order)
    qs.settle(order)
    out_grad = finish(o0, order, units, weight=ORDER_WEIGHT)
    out_grad = finish(o1, order, units, units // 2, out_grad)
    in_grad = finish(i0, order, width)
    small.fold(order)
    in_grad = finish(i1, order, width, width // 2, in_grad)
    qkv_grad = finish(qs, order, 3 * width)

    token_back = lambda b, t, c: norm_back(rows_of(b), rows_of(t), rows_of(c), gain).reshape(tokens.shape)
    input_grad = order(token_back, back_tok, tokens, cotangent)
    qkv_grad = finish(vs, order, 3 * width, 2 * width, qkv_grad)
    qkv_grad = jnp.transpose(qkv_grad.reshape(3, width, local), (1, 0, 2))
    dense_grad = finish(ds, order, local)
    small.settle(order)
    small = small.result().reshape(-1)
    slice_at = lambda a: lax.dynamic_slice_in_dim(a, lax.axis_index("tp") * cols, cols, 0)
    gain_grad, shift_grad = slice_at(small[:width]), slice_at(small[width : 2 * width])
    rms_values = jnp.sqrt(small[2 * width : 2 * width + 4] / (seqs * rows * length * width))
    small = small[2 * width + 128 :]
    in_bias_grad = small[:units]
    qkv_bias_grad = small[units : units + 3 * local].reshape(3, local)
    out_bias_grad = small[units + 3 * local :]

    return (
        layer_out,
        input_grad,
        gain_grad,
        shift_grad,
        qkv_grad,
        qkv_bias_grad,
        dense_grad,
        out_bias_grad,
        in_grad,
        in_bias_grad,
        out_grad,
        out_bias_grad,
        rms_values,
    )


def solution(mesh):
    in_specs = (
        P("rows", "tp", None),
        P("rows", None),
        P("rows", None),
        P(),
        P(),
        P(None, None, "tp"),
        P(None, "tp"),
        P("tp", None),
        P(),
        P(None, "tp"),
        P("tp"),
        P("tp", None),
        P(),
        P("rows", "tp", None),
    )
    out_specs = (
        P("rows", "tp", None),
        P("rows", "tp", None),
        P("tp"),
        P("tp"),
        P(None, None, "tp"),
        P(None, "tp"),
        P("tp", None),
        P("tp"),
        P(None, "tp"),
        P("tp"),
        P("tp", None),
        P("tp"),
        P(),
    )
    return jax.shard_map(body, mesh=mesh, in_specs=in_specs, out_specs=out_specs, check_vma=False)
```

```python
import functools

import jax
import jax.numpy as jnp
from jax import lax
from jax.experimental import pallas as pl
from jax.experimental.pallas import tpu as pltpu
from jax.sharding import PartitionSpec as P

HD = 64
ROT = 32
epsilon = 1e-05
big_negative = -1e30
rope_base = 10000.0
f32 = jnp.float32
bf16 = jnp.bfloat16
VMEM_LIMIT = 56 << 20
ORDER_WEIGHT = int(2.2e11)
EARLY_WEIGHT = int(2.2e11)


def dot(a, b, ca, cb):
    return lax.dot_general(a, b, (((ca,), (cb,)), ((), ())), preferred_element_type=f32)


SMALL = pl.CostEstimate(flops=1, bytes_accessed=1, transcendentals=0)


def params():
    return pltpu.CompilerParams(vmem_limit_bytes=VMEM_LIMIT)


class Order:
    def __init__(self):
        self.last = ()

    def __call__(self, op, *operands):
        operands, _ = lax.optimization_barrier((operands, self.last))
        result = op(*operands)
        self.last = jax.tree.leaves(result)
        return result


def rope_swap(x):
    width = x.shape[-1]
    lane = lax.broadcasted_iota(jnp.int32, (1, width), 1) % HD
    up = pltpu.roll(x, width - ROT // 2, 1)
    down = pltpu.roll(x, ROT // 2, 1)
    return jnp.where(lane < ROT // 2, up, -down)


def norm_kernel(x_ref, gain_ref, shift_ref, first_ref, second_ref, *, per):
    x = x_ref[...].astype(f32)
    center = x - jnp.mean(x, axis=-1, keepdims=True)
    inverse = lax.rsqrt(jnp.mean(center * center, axis=-1, keepdims=True) + epsilon)
    out = (center * inverse * gain_ref[...] + shift_ref[...]).astype(bf16)

    @pl.when(pl.program_id(0) < per)
    def _():
        first_ref[...] = out

    @pl.when(pl.program_id(0) >= per)
    def _():
        second_ref[...] = out


def norm_halves(x, gain, shift, tm=128):
    n, width = x.shape
    per = n // 2 // tm
    vector = pl.BlockSpec((1, width), lambda i: (0, 0))
    return pl.pallas_call(
        functools.partial(norm_kernel, per=per),
        grid=(2 * per,),
        in_specs=[pl.BlockSpec((tm, width), lambda i: (i, 0)), vector, vector],
        out_specs=[
            pl.BlockSpec((tm, width), lambda i: (jnp.minimum(i, per - 1), 0)),
            pl.BlockSpec((tm, width), lambda i: (jnp.maximum(i - per, 0), 0)),
        ],
        out_shape=[jax.ShapeDtypeStruct((n // 2, width), bf16)] * 2,
        compiler_params=params(),
        cost_estimate=SMALL,
        name="norm_halves",
    )(x, gain[None], shift[None])


def norm_back_kernel(back_ref, x_ref, g_ref, gain_ref, o_ref):
    x = x_ref[...].astype(f32)
    center = x - jnp.mean(x, axis=-1, keepdims=True)
    inverse = lax.rsqrt(jnp.mean(center * center, axis=-1, keepdims=True) + epsilon)
    unit = center * inverse
    unit_grad = back_ref[...].astype(f32) * gain_ref[...]
    mean_grad = jnp.mean(unit_grad, axis=-1, keepdims=True)
    mean_both = jnp.mean(unit_grad * unit, axis=-1, keepdims=True)
    value_grad = (unit_grad - mean_grad - unit * mean_both) * inverse
    o_ref[...] = (g_ref[...].astype(f32) + value_grad).astype(bf16)


def norm_back(back, x, g, gain, tm=128):
    n, width = x.shape
    block = pl.BlockSpec((tm, width), lambda i: (i, 0))
    return pl.pallas_call(
        norm_back_kernel,
        grid=(n // tm,),
        in_specs=[block, block, block, pl.BlockSpec((1, width), lambda i: (0, 0))],
        out_specs=block,
        out_shape=jax.ShapeDtypeStruct((n, width), bf16),
        compiler_params=params(),
        cost_estimate=SMALL,
        name="norm_back",
    )(back, x, g, gain[None])


def table_kernel(place_ref, frequency_ref, c_ref, s_ref):
    angle = place_ref[...].astype(f32) * frequency_ref[...]
    lane = lax.broadcasted_iota(jnp.int32, angle.shape, 1) % HD
    turned = lane < ROT
    c_ref[...] = jnp.where(turned, jnp.cos(angle), 1.0)
    s_ref[...] = jnp.where(turned, jnp.sin(angle), 0.0)


def rope_tables(place, tile, tm=1024):
    n = place.shape[0]
    lane = jnp.arange(tile, dtype=jnp.int32) % (ROT // 2)
    frequency = (rope_base ** (-2.0 * lane.astype(f32) / ROT))[None]
    table = pl.BlockSpec((tm, tile), lambda i: (i, 0))
    return pl.pallas_call(
        table_kernel,
        grid=(n // tm,),
        in_specs=[pl.BlockSpec((tm, 1), lambda i: (i, 0)), pl.BlockSpec((1, tile), lambda i: (0, 0))],
        out_specs=[table, table],
        out_shape=[jax.ShapeDtypeStruct((n, tile), f32)] * 2,
        compiler_params=params(),
        cost_estimate=SMALL,
        name="rope_tables",
    )(place, frequency)


def qkv_kernel(x_ref, w_ref, b_ref, c_ref, s_ref, o_ref):
    x = x_ref[...]
    tile = c_ref.shape[-1]
    local = w_ref.shape[-1]
    cosine, sine = c_ref[...], s_ref[...]
    for part in range(3):
        full = dot(x, w_ref[part], 1, 0) + b_ref[part : part + 1, :]
        for at in range(0, local, tile):
            piece = full[:, at : at + tile]
            if part < 2:
                piece = piece * cosine - rope_swap(piece) * sine
            if part == 0:
                piece = piece * (HD**-0.5)
            o_ref[part, :, at : at + tile] = piece.astype(bf16)


def project_qkv(x, w3, bias, cosine, sine, tm=512):
    n, width = x.shape
    local = w3.shape[2]
    tile = cosine.shape[1]
    return pl.pallas_call(
        qkv_kernel,
        grid=(n // tm,),
        in_specs=[
            pl.BlockSpec((tm, width), lambda i: (i, 0)),
            pl.BlockSpec((3, width, local), lambda i: (0, 0, 0)),
            pl.BlockSpec((3, local), lambda i: (0, 0)),
            pl.BlockSpec((tm, tile), lambda i: (i, 0)),
            pl.BlockSpec((tm, tile), lambda i: (i, 0)),
        ],
        out_specs=pl.BlockSpec((3, tm, local), lambda i: (0, i, 0)),
        out_shape=jax.ShapeDtypeStruct((3, n, local), bf16),
        compiler_params=params(),
        cost_estimate=SMALL,
        name="qkv_rope",
    )(x, w3, bias, cosine, sine)


def chosen_kernel(me_ref, *refs, held):
    x_ref, w_ref, b_ref, act_ref, slope_ref = refs[held:]
    seqs, here, width = x_ref.shape
    x = x_ref[...].reshape(seqs * here, width)
    units = w_ref.shape[1]
    step = min(256, units)
    for at in range(0, units, step):
        cut = slice(at, at + step)
        h = dot(x, w_ref[:, cut], 1, 0) + b_ref[:, cut]
        square = h * h
        t = jnp.tanh(h * (0.7978845608028654 + 0.035677408136300125 * square))
        half = 0.5 + 0.5 * t
        act = h * half
        slope = half + (act - act * half) * (1.5957691216057308 + 0.21406444881780074 * square)
        act_ref[:, :, cut] = act.astype(bf16).reshape(seqs, here, step)
        slope_ref[:, :, cut] = slope.astype(bf16).reshape(seqs, here, step)


def mlp_hidden_of(x, w, bias, steps, before=(), weight=1):
    seqs, owners, here, width = x.shape
    units = w.shape[1]
    held = len(before)

    def device(j, me):
        chosen = me[0] ^ steps[0]
        for i in range(1, len(steps)):
            chosen = jnp.where(j == i, me[0] ^ steps[i], chosen)
        return 0, chosen, 0, 0

    out = pl.BlockSpec((seqs, None, here, units), device)
    me = lax.axis_index("tp").astype(jnp.int32).reshape(1)
    return pl.pallas_call(
        functools.partial(chosen_kernel, held=held),
        grid_spec=pltpu.PrefetchScalarGridSpec(
            num_scalar_prefetch=1,
            grid=(len(steps),),
            in_specs=[pl.BlockSpec(memory_space=pl.ANY)] * held
            + [
                pl.BlockSpec((seqs, None, here, width), device),
                pl.BlockSpec((width, units), lambda j, me: (0, 0)),
                pl.BlockSpec((1, units), lambda j, me: (0, 0)),
            ],
            out_specs=[out, out],
        ),
        out_shape=[jax.ShapeDtypeStruct((seqs, owners, here, units), bf16)] * 2,
        input_output_aliases={1 + i: i for i in range(held)},
        compiler_params=params(),
        cost_estimate=pl.CostEstimate(flops=int(weight), bytes_accessed=1, transcendentals=0),
        name="mlp_hidden_of",
    )(me, *before, x, w, bias)


def grad_in_kernel(g_ref, wo_ref, wd_ref, slope_ref, hg_ref, at_ref, sum_ref):
    g = g_ref[...]
    units = wo_ref.shape[0]
    step = min(256, units)

    @pl.when(pl.program_id(0) == 0)
    def _():
        sum_ref[...] = jnp.zeros_like(sum_ref)

    for at in range(0, units, step):
        slope = slope_ref[:, at : at + step].astype(f32)
        hg = (dot(g, wo_ref[at : at + step, :], 1, 1) * slope).astype(bf16)
        hg_ref[:, at : at + step] = hg
        sum_ref[0:1, at : at + step] += jnp.sum(hg.astype(f32), axis=0, keepdims=True)
    at_ref[...] = dot(g, wd_ref[...], 1, 1).astype(bf16)


def grad_in(g, wo, wd, slope, tm=512):
    n, width = g.shape
    units, local = wo.shape[0], wd.shape[0]
    return pl.pallas_call(
        grad_in_kernel,
        grid=(n // tm,),
        in_specs=[
            pl.BlockSpec((tm, width), lambda i: (i, 0)),
            pl.BlockSpec((units, width), lambda i: (0, 0)),
            pl.BlockSpec((local, width), lambda i: (0, 0)),
            pl.BlockSpec((tm, units), lambda i: (i, 0)),
        ],
        out_specs=[
            pl.BlockSpec((tm, units), lambda i: (i, 0)),
            pl.BlockSpec((tm, local), lambda i: (i, 0)),
            pl.BlockSpec((8, units), lambda i: (0, 0)),
        ],
        out_shape=[
            jax.ShapeDtypeStruct((n, units), bf16),
            jax.ShapeDtypeStruct((n, local), bf16),
            jax.ShapeDtypeStruct((8, units), f32),
        ],
        compiler_params=params(),
        cost_estimate=SMALL,
        name="grad_in",
    )(g, wo, wd, slope)


def tokens_kernel(*refs, held):
    x_ref, w_ref, o_ref = refs[held:]
    width = w_ref.shape[1]
    step = min(512, width)
    for at in range(0, width, step):
        o_ref[:, at : at + step] = dot(x_ref[...], w_ref[:, at : at + step], 1, 0).astype(o_ref.dtype)


def tokens_by_weight(x, w, share, shares, before=(), tm=512):
    n, depth = x.shape
    held = len(before)
    steps = n // shares // tm
    width = w.shape[1]
    first = share * steps
    return pl.pallas_call(
        functools.partial(tokens_kernel, held=held),
        grid=(steps,),
        in_specs=[pl.BlockSpec(memory_space=pl.ANY)] * held
        + [pl.BlockSpec((tm, depth), lambda i: (first + i, 0)), pl.BlockSpec((depth, width), lambda i: (0, 0))],
        out_specs=pl.BlockSpec((tm, width), lambda i: (first + i, 0)),
        out_shape=jax.ShapeDtypeStruct((n, width), bf16),
        input_output_aliases={i: i for i in range(held)},
        compiler_params=params(),
        cost_estimate=SMALL,
        name="tokens_by_weight",
    )(*before, x, w)


def weight_grad_kernel(a_ref, b_ref, o_ref):
    o_ref[...] = dot(a_ref[...], b_ref[...], 0, 0).astype(bf16)


def weight_grad(a, b, share=0, shares=1, tile=512, weight=1):
    n, rows = a.shape
    rows //= shares
    cols = b.shape[1]
    tile = min(tile, cols)
    return pl.pallas_call(
        weight_grad_kernel,
        grid=(cols // tile,),
        in_specs=[
            pl.BlockSpec((n, rows), lambda j: (0, share), pipeline_mode=pl.Buffered(1)),
            pl.BlockSpec((n, tile), lambda j: (0, j)),
        ],
        out_specs=pl.BlockSpec((rows, tile), lambda j: (0, j)),
        out_shape=jax.ShapeDtypeStruct((rows, cols), bf16),
        compiler_params=params(),
        cost_estimate=pl.CostEstimate(flops=int(weight), bytes_accessed=1, transcendentals=0),
        name="weight_grad",
    )(a, b)


def weight_grad_rows_kernel(a_ref, b_ref, *o_refs, counts):
    full = dot(a_ref[...], b_ref[...], 0, 0).astype(bf16)
    step = pl.program_id(0)
    first = 0
    for o_ref, count in zip(o_refs, counts):

        @pl.when((step >= first) & (step < first + count))
        def _(o_ref=o_ref):
            o_ref[...] = full

        first += count


def weight_grad_rows(a, b, shares, tile=512):
    n, rows = a.shape
    cols = b.shape[1]
    counts = [rows * share // sum(shares) // tile for share in shares]
    firsts = [sum(counts[:i]) for i in range(len(counts))]
    out = lambda i: pl.BlockSpec((tile, cols), lambda j: (jnp.clip(j - firsts[i], 0, counts[i] - 1), 0))
    return pl.pallas_call(
        functools.partial(weight_grad_rows_kernel, counts=counts),
        grid=(rows // tile,),
        in_specs=[
            pl.BlockSpec((n, tile), lambda j: (0, j)),
            pl.BlockSpec((n, cols), lambda j: (0, 0), pipeline_mode=pl.Buffered(1)),
        ],
        out_specs=[out(i) for i in range(len(counts))],
        out_shape=[jax.ShapeDtypeStruct((count * tile, cols), bf16) for count in counts],
        compiler_params=params(),
        cost_estimate=SMALL,
        name="weight_grad_rows",
    )(a, b)


def weight_grad_parts_kernel(a_ref, b_ref, first_ref, last_ref):
    for part in range(2):
        first_ref[part] = dot(a_ref[...], b_ref[part], 0, 0).astype(bf16)
    last_ref[...] = dot(a_ref[...], b_ref[2], 0, 0).astype(bf16)


def weight_grad_parts(a, b, tile=512, weight=1):
    n, rows = a.shape
    parts, _, cols = b.shape
    return pl.pallas_call(
        weight_grad_parts_kernel,
        grid=(rows // tile,),
        in_specs=[
            pl.BlockSpec((n, tile), lambda j: (0, j)),
            pl.BlockSpec((parts, n, cols), lambda j: (0, 0, 0), pipeline_mode=pl.Buffered(1)),
        ],
        out_specs=[pl.BlockSpec((2, tile, cols), lambda j: (0, j, 0)), pl.BlockSpec((tile, cols), lambda j: (j, 0))],
        out_shape=[jax.ShapeDtypeStruct((2, rows, cols), bf16), jax.ShapeDtypeStruct((rows, cols), bf16)],
        compiler_params=params(),
        cost_estimate=pl.CostEstimate(flops=int(weight), bytes_accessed=1, transcendentals=0),
        name="weight_grad_parts",
    )(a, b)


def normed_grad_kernel(*refs, held):
    hg_ref, dq_ref, wi_ref, w3_ref, x_ref, shift_ref, o_ref, sum_ref, norm_ref = refs[held:]

    @pl.when(pl.program_id(0) == 0)
    def _():
        sum_ref[...] = jnp.zeros_like(sum_ref)
        norm_ref[...] = jnp.zeros_like(norm_ref)

    for part in range(3):
        sum_ref[part, 0:1] += jnp.sum(dq_ref[part].astype(f32), axis=0, keepdims=True)
    width = o_ref.shape[1]
    step = min(512, width)
    for at in range(0, width, step):
        cut = slice(at, at + step)
        total = dot(hg_ref[...], wi_ref[cut, :], 1, 1)
        for part in range(3):
            total += dot(dq_ref[part], w3_ref[part, cut, :], 1, 1)
        o_ref[:, cut] = total.astype(bf16)
        scaled = x_ref[:, cut].astype(f32) - shift_ref[:, cut]
        norm_ref[0:1, cut] += jnp.sum(total * scaled, axis=0, keepdims=True)
        norm_ref[1:2, cut] += jnp.sum(total, axis=0, keepdims=True)


def normed_grad(hg, dqkv, wi, w3, x, shift, share, shares, before=(), tm=512):
    n, units = hg.shape
    held = len(before)
    steps = n // shares // tm
    first = share * steps
    width, local = w3.shape[1:]
    return pl.pallas_call(
        functools.partial(normed_grad_kernel, held=held),
        grid=(steps,),
        in_specs=[pl.BlockSpec(memory_space=pl.ANY)] * held
        + [
            pl.BlockSpec((tm, units), lambda i: (first + i, 0)),
            pl.BlockSpec((3, tm, local), lambda i: (0, first + i, 0)),
            pl.BlockSpec((width, units), lambda i: (0, 0)),
            pl.BlockSpec((3, width, local), lambda i: (0, 0, 0)),
            pl.BlockSpec((tm, width), lambda i: (first + i, 0)),
            pl.BlockSpec((1, width), lambda i: (0, 0)),
        ],
        out_specs=[
            pl.BlockSpec((tm, width), lambda i: (first + i, 0)),
            pl.BlockSpec((3, 8, local), lambda i: (0, 0, 0)),
            pl.BlockSpec((8, width), lambda i: (0, 0)),
        ],
        out_shape=[
            jax.ShapeDtypeStruct((n, width), bf16),
            jax.ShapeDtypeStruct((3, 8, local), f32),
            jax.ShapeDtypeStruct((8, width), f32),
        ],
        input_output_aliases={i: i for i in range(held)},
        compiler_params=params(),
        cost_estimate=SMALL,
        name="normed_grad",
    )(*before, hg, dqkv, wi, w3, x, shift)


def attention_kernel(*refs, bq, held):
    start_ref, q_ref, k_ref, v_ref, do_ref, c_ref, s_ref, o_ref, by_owner_ref, g_ref, dk_acc, dv_acc = refs[held:]
    span, width = q_ref.shape
    here = by_owner_ref.shape[1]
    lane = lax.broadcasted_iota(jnp.int32, (1, width), 1) // HD
    zero = jnp.zeros((), bf16)
    heads = range(width // HD)
    cuts = [slice(head * HD, (head + 1) * HD) for head in heads]
    blocks = span // bq
    keys_across, vals_across = k_ref[...].T, v_ref[...].T

    def turn_back(x, at, n):
        return x * c_ref[at : at + n, :] + rope_swap(x) * s_ref[at : at + n, :]

    def products(block):
        at, n = block * bq, (block + 1) * bq
        keys, vals = k_ref[0:n, :], v_ref[0:n, :]
        queries = [jnp.where(lane == head, q_ref[at:n, :], zero) for head in heads]
        grads = [jnp.where(lane == head, do_ref[at:n, :], zero) for head in heads]
        return queries, grads, [dot(keys, q, 1, 1) for q in queries], [dot(vals, g, 1, 1) for g in grads]

    ahead = products(0)
    for block in range(blocks):
        at, n = block * bq, (block + 1) * bq
        queries, grads, scores, prob_grads = ahead
        key = lax.broadcasted_iota(jnp.int32, (n, bq), 0)
        place = lax.broadcasted_iota(jnp.int32, (1, bq), 1) + at
        allowed = (key >= start_ref[:, at:n]) & (key <= place)
        if block + 1 < blocks:
            ahead = products(block + 1)
        probs = []
        for head in heads:
            score = jnp.where(allowed, scores[head], big_negative)
            expd = jnp.exp(score - jnp.max(score, axis=0, keepdims=True))
            probs.append(expd * (1.0 / jnp.sum(expd, axis=0, keepdims=True)))
        low = [p.astype(bf16) for p in probs]
        out = [dot(vals_across[cut, 0:n], p, 1, 0) for cut, p in zip(cuts, low)]
        dv = sum(dot(p, g, 1, 0) for p, g in zip(low, grads))
        score_grads = []
        for p, g in zip(probs, prob_grads):
            both = p * g
            score_grads.append((both - p * jnp.sum(both, axis=0, keepdims=True)).astype(bf16))
        dq = [dot(keys_across[cut, 0:n], g, 1, 0) for cut, g in zip(cuts, score_grads)]
        dk = sum(dot(g, q, 1, 0) for g, q in zip(score_grads, queries))
        out = jnp.concatenate(out, axis=0).T.astype(bf16)
        o_ref[at:n, :] = out
        by_owner_ref[at // here, at % here : at % here + bq] = out
        g_ref[0, at:n, :] = turn_back(jnp.concatenate(dq, axis=0).T * (HD**-0.5), at, bq).astype(bf16)
        if block:
            dk_acc[0:at, :] += dk[0:at]
            dv_acc[0:at, :] += dv[0:at]
        dk_acc[at:n, :] = dk[at:n]
        dv_acc[at:n, :] = dv[at:n]
    g_ref[1] = turn_back(dk_acc[...], 0, span).astype(bf16)
    g_ref[2] = dv_acc[...].astype(bf16)


def attention_both(start, qkv, grad, cosine, sine, span, owners, row, before=(), bq=128):
    n, local = grad.shape
    here = 2 * span // owners
    width = cosine.shape[1]
    bq = min(bq, here)
    held = len(before)
    first = 2 * row
    part = lambda which: pl.BlockSpec((None, span, width), lambda t, p: (which, first + t, p))
    table = pl.BlockSpec((span, width), lambda t, p: (first + t, 0))
    return pl.pallas_call(
        functools.partial(attention_kernel, bq=bq, held=held),
        grid=(2, local // width),
        in_specs=[pl.BlockSpec(memory_space=pl.ANY)] * held
        + [
            pl.BlockSpec((1, span), lambda t, p: (0, first + t)),
            part(0),
            part(1),
            part(2),
            pl.BlockSpec((span, width), lambda t, p: (first + t, p)),
            table,
            table,
        ],
        out_specs=[
            pl.BlockSpec((span, width), lambda t, p: (first + t, p)),
            pl.BlockSpec((owners // 2, None, here, width), lambda t, p: (t, row, 0, p)),
            pl.BlockSpec((3, span, width), lambda t, p: (0, first + t, p)),
        ],
        out_shape=[
            jax.ShapeDtypeStruct((n, local), bf16),
            jax.ShapeDtypeStruct((owners, n // (2 * span), here, local), bf16),
            jax.ShapeDtypeStruct((3, n, local), bf16),
        ],
        scratch_shapes=[pltpu.VMEM((span, width), f32)] * 2,
        input_output_aliases={i: i for i in range(held)},
        compiler_params=params(),
        cost_estimate=SMALL,
        name="attention_both",
    )(*before, start, qkv, qkv, qkv, grad, cosine, sine)


def own_kernel(x_ref, w_ref, bd_ref, bo_ref, token_ref, *refs):
    *mlp_refs, o_ref, sum_ref = refs
    owners, seqs, here, local = x_ref.shape
    attention = jnp.zeros((seqs * here, w_ref.shape[1]), f32) + bd_ref[...]
    for owner in range(owners):
        x = x_ref[owner].reshape(seqs * here, local)
        attention += dot(x, w_ref[owner * local : (owner + 1) * local, :], 1, 0)
    tokens = token_ref[...].astype(f32)
    mlp = jnp.concatenate([a[...] for a in mlp_refs], axis=0).astype(f32) + bo_ref[...]
    total = tokens + attention + mlp
    o_ref[...] = total.astype(bf16)

    @pl.when(pl.program_id(0) == 0)
    def _():
        sum_ref[...] = jnp.zeros_like(sum_ref)

    for i, a in enumerate((tokens, attention, mlp, total)):
        sum_ref[i : i + 1, :] += jnp.sum(a * a, axis=0, keepdims=True)


def project_own(x, w, bd, bo, tokens, mlp_parts, tile=512, weight=1):
    owners, seqs, here, local = x.shape
    width = w.shape[1]
    rows = seqs * here
    column = lambda high: pl.BlockSpec((high, tile), lambda j: (0, j))
    return pl.pallas_call(
        own_kernel,
        grid=(width // tile,),
        in_specs=[
            pl.BlockSpec(x.shape, lambda j: (0, 0, 0, 0)),
            column(owners * local),
            column(1),
            column(1),
            column(rows),
        ]
        + [column(a.shape[0]) for a in mlp_parts],
        out_specs=[column(rows), pl.BlockSpec((8, tile), lambda j: (0, 0))],
        out_shape=[jax.ShapeDtypeStruct((rows, width), bf16), jax.ShapeDtypeStruct((8, tile), f32)],
        compiler_params=params(),
        cost_estimate=pl.CostEstimate(flops=int(weight), bytes_accessed=1, transcendentals=0),
        name="project_own",
    )(x, w, bd, bo, tokens, *mlp_parts)


def line_ok(size):
    return size >= 4 and size & (size - 1) == 0


class RowSum:
    def __init__(self, part, size):
        self.part, self.size, self.axis = part, size, "rows"
        groups = range(0, size, 4)
        pairs = lambda *ends: [(g + a, g + b) for g in groups for a, b in ends]
        self.hops = [pairs((0, 1), (3, 2)), pairs((1, 2), (2, 1))]
        hop = 4
        while hop < size:
            self.hops.append([(i, i ^ hop) for i in range(size)])
            hop *= 2
        self.hops.append(pairs((1, 0), (2, 3)))
        self.send()

    def send(self):
        if line_ok(self.size):
            self.came = lax.ppermute(self.part, self.axis, self.hops.pop(0))

    def fold(self, order):
        if line_ok(self.size) and self.hops:
            add = lambda a, b: (a.astype(f32) + b.astype(f32)).astype(a.dtype)
            self.part = order(add, self.part, self.came)
            self.send()

    def settle(self, order):
        if line_ok(self.size):
            self.came = order(lambda a: a, self.came)

    def complete(self, order):
        while self.hops:
            self.fold(order)

    def result(self, order=None):
        if not line_ok(self.size):
            return lax.psum(self.part.astype(f32), "rows")
        self.complete(order or Order())
        place = lax.axis_index("rows") % 4
        return jnp.where((place == 1) | (place == 2), self.part, self.came).astype(f32)


def finish_kernel(inner_ref, kept_ref, came_ref, *refs):
    o_ref = refs[-1]

    @pl.when(inner_ref[0] == 1)
    def _():
        o_ref[...] = kept_ref[...].astype(f32)

    @pl.when(inner_ref[0] == 0)
    def _():
        o_ref[...] = came_ref[...].astype(f32)


def finish(total, order, high, first=0, before=None, tile=512, weight=1):
    flat = lambda a: a.reshape(-1, a.shape[-1])
    rows, cols = flat(total.part).shape
    if not line_ok(total.size):
        before = jnp.zeros((high, cols), f32) if before is None else before
        return lax.dynamic_update_slice(before, flat(total.result()), (first, 0))
    total.complete(order)
    tile = min(tile, rows)
    held = [] if before is None else [before]
    block = pl.BlockSpec((tile, cols), lambda j: (j, 0))
    place = lax.axis_index("rows") % 4
    inner = ((place == 1) | (place == 2)).astype(jnp.int32).reshape(1)
    call = pl.pallas_call(
        finish_kernel,
        grid=(rows // tile,),
        in_specs=[pl.BlockSpec(memory_space=pltpu.SMEM), block, block] + [pl.BlockSpec(memory_space=pl.ANY)] * len(held),
        out_specs=pl.BlockSpec((tile, cols), lambda j: (first // tile + j, 0)),
        out_shape=jax.ShapeDtypeStruct((high, cols), f32),
        input_output_aliases={3: 0} if held else {},
        compiler_params=params(),
        cost_estimate=pl.CostEstimate(flops=int(weight), bytes_accessed=1, transcendentals=0),
        name="finish",
    )
    return order(lambda *a: call(inner, *a), flat(total.part), flat(total.came), *held)


class Gather:
    core, x, y = 1, 2, 4

    def __init__(self, first, second, size):
        self.first, self.second, self.size = first, second, size
        self.x0, self.y1 = self.send(first, self.x), self.send(second, self.y)

    def send(self, a, step):
        return lax.ppermute(a, "tp", [(i, i ^ step) for i in range(self.size)])

    def others(self, order=None):
        first, second = self.first, self.second
        if order:
            first, second = order(lambda a, b: (a, b), first, second)
        self.x1, self.y0 = self.send(second, self.x), self.send(first, self.y)
        self.c0 = self.send(first, self.core)

    def forward(self, order):
        came = (self.x0, self.y1, self.c0, self.second)
        self.x0, self.y1, self.c0, self.second = order(lambda *a: a, *came)
        self.c1 = self.send(self.second, self.core)
        self.d0, self.d1 = self.send(self.x0, self.y), self.send(self.y1, self.x)

    def pairs(self, order):
        came = (self.x0, self.y1, self.x1, self.y0, self.c1)
        self.x0, self.y1, self.x1, self.y0, self.c1 = order(lambda *a: a, *came)
        self.px0, self.py1 = self.send(self.x0, self.core), self.send(self.y1, self.core)
        self.px1, self.py0 = self.send(self.x1, self.core), self.send(self.y0, self.core)

    def near(self, order):
        steps = [step for step in (0, self.core, self.x, self.y, self.x | self.core, self.y | self.core) for _ in range(2)]
        pieces = (self.first, self.second, self.c0, self.c1, self.x0, self.x1, self.y0, self.y1)
        pieces += (self.px0, self.px1, self.py0, self.py1)
        self.full = order(lambda *a: place_pieces(None, a, steps, (0, 1) * 6, self.size), *pieces)

    def far_pairs(self, order):
        self.d0, self.d1 = order(lambda a, b: (a, b), self.d0, self.d1)
        self.pd0, self.pd1 = self.send(self.d0, self.core), self.send(self.d1, self.core)

    def far(self, order):
        far = self.x | self.y
        steps = (far, far, far | self.core, far | self.core)
        place = lambda full, *a: place_pieces(full, a, steps, (0, 1, 0, 1), self.size)
        self.full = order(place, self.full, self.d0, self.d1, self.pd0, self.pd1)
        return self.full


def place_kernel(me_ref, *refs, held):
    pieces, o_ref = refs[held:-1], refs[-1]
    for i, piece in enumerate(pieces):

        @pl.when(pl.program_id(0) == i)
        def _(piece=piece):
            o_ref[...] = piece[...].reshape(o_ref.shape)


def place_pieces(full, pieces, steps, halves, size):
    held = 0 if full is None else 1
    here, width = pieces[0].shape

    def target(j, me):
        device, half = me[0] ^ steps[0], halves[0]
        for i in range(1, len(pieces)):
            device = jnp.where(j == i, me[0] ^ steps[i], device)
            half = jnp.where(j == i, halves[i], half)
        return half, device, 0, 0

    hbm = pl.BlockSpec(memory_space=pl.ANY)
    me = lax.axis_index("tp").astype(jnp.int32).reshape(1)
    return pl.pallas_call(
        functools.partial(place_kernel, held=held),
        grid_spec=pltpu.PrefetchScalarGridSpec(
            num_scalar_prefetch=1,
            grid=(len(pieces),),
            in_specs=[hbm] * held + [pl.BlockSpec((here, width), lambda j, me: (0, 0))] * len(pieces),
            out_specs=pl.BlockSpec((1, None, here, width), target),
        ),
        out_shape=jax.ShapeDtypeStruct((2, size, here, width), bf16),
        input_output_aliases={1: 0} if held else {},
        compiler_params=params(),
        cost_estimate=SMALL,
        name="place_pieces",
    )(me, *([full] if held else []), *pieces)


class TpSum:
    def __init__(self, part, size):
        self.part, self.size, self.hop = part, size, 1
        self.send()

    def send(self):
        if self.size & (self.size - 1) == 0 and self.hop < self.size:
            self.came = lax.ppermute(self.part, "tp", [(i, i ^ self.hop) for i in range(self.size)])

    def fold(self, order):
        if self.size & (self.size - 1):
            self.part, self.size = lax.psum(self.part, "tp"), 1
        elif self.hop < self.size:
            self.part = order(lambda a, b: a + b, self.part, self.came)
            self.hop *= 2
            self.send()

    def result(self, order):
        while self.hop < self.size:
            self.fold(order)
        return self.part


def body(
    tokens,
    segment_ids,
    positions,
    norm_gain,
    norm_shift,
    query_key_value_weight,
    b_qkv,
    dense_weight,
    b_dense,
    inward_weight,
    b_in,
    outward_weight,
    b_out,
    cotangent,
):
    rows, tp = lax.axis_size("rows"), lax.axis_size("tp")
    seqs, here, width = tokens.shape
    length = here * tp
    n = seqs * length
    local = query_key_value_weight.shape[2]
    tile = min(128, local)
    span = length // 2

    exchange = tp == 8 and seqs == 2

    order = Order()
    gain, shift = norm_gain.astype(f32), norm_shift.astype(f32)
    norm = lambda a: norm_halves(a.reshape(seqs * here, width), gain, shift)
    halves = order(norm, tokens)

    if exchange:
        gather_normed = Gather(*halves, tp)
        gather_normed.others()

    def tables(positions, weight):
        place = positions.reshape(n, 1)
        cosine, sine = rope_tables(place, tile)
        start = jnp.arange(n, dtype=jnp.int32)[None] % span - positions.reshape(1, n)
        return cosine, sine, start, jnp.transpose(weight, (1, 0, 2))

    cosine, sine, start, w3 = order(tables, positions, query_key_value_weight)
    in_bias_row = b_in.astype(f32)[None]
    token_rows = lambda a: a.reshape(n, a.shape[-1])
    later = lambda a: lax.all_gather(order(lambda b: b, a), "tp", axis=1, tiled=True).reshape(n, width)
    if exchange:
        gather_normed.forward(order)
        gather_normed.pairs(order)
        grad = later(cotangent)
        gather_normed.near(order)
        hidden_of = lambda *a: mlp_hidden_of(*a, tuple(range(6)))
        hidden = order(hidden_of, gather_normed.full, inward_weight, in_bias_row)
        gather_normed.far_pairs(order)
        normed_full = gather_normed.far(order)
        hidden_of = lambda x, w, b, *before: mlp_hidden_of(x, w, b, (6, 7), before)
        act, slope = order(hidden_of, normed_full, inward_weight, in_bias_row, *hidden)
    else:
        normed_full = jnp.concatenate(halves).reshape(seqs, here, width)
        normed_full = lax.all_gather(normed_full, "tp", axis=1).reshape(seqs, tp, here, width)
        grad = later(cotangent)
        hidden_of = lambda *a: mlp_hidden_of(*a, tuple(range(tp)))
        act, slope = order(hidden_of, normed_full, inward_weight, in_bias_row)
    normed, act, slope = token_rows(normed_full), token_rows(act), token_rows(slope)
    qkv = order(project_qkv, normed, w3, b_qkv.astype(f32), cosine, sine)
    mlp_half = order(lambda *a: tokens_by_weight(*a, 0, 2), act, outward_weight)
    dense_ready, _ = lax.optimization_barrier((dense_weight, act))
    dense_full = lax.all_gather(dense_ready, "tp", axis=0, tiled=True)
    o0 = RowSum(order(lambda *a: weight_grad(*a, 0, 2), act, grad), rows)
    o1 = RowSum(order(lambda *a: weight_grad(*a, 1, 2), act, grad), rows)
    row_sum = lambda parts: [RowSum(part, rows) for part in parts]
    hidden_grad, attended_grad, in_bias = order(grad_in, grad, outward_weight, dense_weight, slope)
    o0.fold(order)
    i0, i1 = row_sum(order(lambda a, b: weight_grad_rows(a, b, (1, 1)), normed, hidden_grad))
    mlp_part = order(lambda x, w, *kept: tokens_by_weight(x, w, 1, 2, kept), act, outward_weight, mlp_half)
    mlp_part = mlp_part.reshape(seqs, length, width)
    mlp_tok = lax.psum_scatter(mlp_part, "tp", scatter_dimension=1, tiled=True).reshape(seqs * here, width)
    o1.fold(order)
    o0.fold(order)
    both = lambda row: lambda s, q, g, c, t, *before: attention_both(s, q, g, c, t, span, tp, row, before)
    attended, by_owner, dqkv = order(both(0), start, qkv, attended_grad, cosine, sine)
    i0.fold(order)
    for row in range(1, seqs):
        kept = (attended, by_owner, dqkv)
        attended, by_owner, dqkv = order(both(row), start, qkv, attended_grad, cosine, sine, *kept)
    mine = lax.all_to_all(by_owner, "tp", split_axis=0, concat_axis=0, tiled=True)
    o1.fold(order)
    o0.settle(order)
    qs, vs = row_sum(order(lambda a, b: weight_grad_parts(a, b, weight=EARLY_WEIGHT), normed, dqkv))
    units = in_bias.shape[1]
    back = lambda share: lambda *a: normed_grad(*a[:5], shift[None], share, 2, a[5:])
    i1.fold(order)
    i0.fold(order)
    part, bias_a, norm_a = order(back(0), hidden_grad, dqkv, inward_weight, w3, normed)
    o1.settle(order)
    (ds,) = row_sum([order(weight_grad, attended, grad)])
    i1.fold(order)
    qs.fold(order)
    part, bias_b, norm_b = order(back(1), hidden_grad, dqkv, inward_weight, w3, normed, part)
    back_tok = lax.psum_scatter(part.reshape(seqs, length, width), "tp", scatter_dimension=1, tiled=True)
    vs.fold(order)
    i0.settle(order)

    cols = width // tp

    def column_sums(grad):
        mine = lax.dynamic_slice_in_dim(grad, lax.axis_index("tp") * cols, cols, 1)
        return jnp.sum(mine.astype(f32), axis=0)

    out_bias = order(column_sums, grad)
    rows_of = lambda a: a.reshape(seqs * here, width)
    bias_rows = (b_dense.astype(f32)[None], b_out.astype(f32)[None])
    own = lambda x, w, t, *m: project_own(x, w, *bias_rows, rows_of(t), m)
    layer_out, squares = order(own, mine, dense_full, tokens, mlp_tok)
    layer_out = layer_out.reshape(tokens.shape)

    def pack(norm_a, norm_b, squares):
        norm_sums = norm_a + norm_b
        squares = jnp.sum(squares[:4], axis=1)
        pad = jnp.zeros((124,), f32)
        return jnp.concatenate([norm_sums[0] / gain, norm_sums[1], squares, pad]).reshape(-1, 128)

    qs.fold(order)
    i1.settle(order)
    packed = TpSum(order(pack, norm_a, norm_b, squares), tp)
    ds.fold(order)
    packed.fold(order)
    packed.fold(order)
    qkv_bias = bias_a + bias_b
    small = jnp.concatenate([in_bias[0], qkv_bias[:, 0].reshape(-1), out_bias]).reshape(-1, 128)
    small = RowSum(jnp.concatenate([packed.result(order), small]), rows)
    vs.fold(order)
    small.fold(order)
    ds.fold(order)
    qs.settle(order)
    out_grad = finish(o0, order, units, weight=ORDER_WEIGHT)
    out_grad = finish(o1, order, units, units // 2, out_grad)
    in_grad = finish(i0, order, width)
    small.fold(order)
    in_grad = finish(i1, order, width, width // 2, in_grad)
    qkv_grad = finish(qs, order, 3 * width)

    qkv_grad = finish(vs, order, 3 * width, 2 * width, qkv_grad)
    qkv_grad = jnp.transpose(qkv_grad.reshape(3, width, local), (1, 0, 2))
    dense_grad = finish(ds, order, local)
    token_back = lambda b, t, c: norm_back(rows_of(b), rows_of(t), rows_of(c), gain).reshape(tokens.shape)
    input_grad = order(token_back, back_tok, tokens, cotangent)
    small.settle(order)
    small = small.result().reshape(-1)
    slice_at = lambda a: lax.dynamic_slice_in_dim(a, lax.axis_index("tp") * cols, cols, 0)
    gain_grad, shift_grad = slice_at(small[:width]), slice_at(small[width : 2 * width])
    rms_values = jnp.sqrt(small[2 * width : 2 * width + 4] / (seqs * rows * length * width))
    small = small[2 * width + 128 :]
    in_bias_grad = small[:units]
    qkv_bias_grad = small[units : units + 3 * local].reshape(3, local)
    out_bias_grad = small[units + 3 * local :]

    return (
        layer_out,
        input_grad,
        gain_grad,
        shift_grad,
        qkv_grad,
        qkv_bias_grad,
        dense_grad,
        out_bias_grad,
        in_grad,
        in_bias_grad,
        out_grad,
        out_bias_grad,
        rms_values,
    )


def solution(mesh):
    in_specs = (
        P("rows", "tp", None),
        P("rows", None),
        P("rows", None),
        P(),
        P(),
        P(None, None, "tp"),
        P(None, "tp"),
        P("tp", None),
        P(),
        P(None, "tp"),
        P("tp"),
        P("tp", None),
        P(),
        P("rows", "tp", None),
    )
    out_specs = (
        P("rows", "tp", None),
        P("rows", "tp", None),
        P("tp"),
        P("tp"),
        P(None, None, "tp"),
        P(None, "tp"),
        P("tp", None),
        P("tp"),
        P(None, "tp"),
        P("tp"),
        P("tp", None),
        P("tp"),
        P(),
    )
    return jax.shard_map(body, mesh=mesh, in_specs=in_specs, out_specs=out_specs, check_vma=False)
```
